32 devices in a mesh: wide: 8 (over z, x), narrow: 4 (over y, core).
Axes of the slice: x: 2, y: 2, z: 4, core: 2. Of those that a mesh axis runs over, the one named last changes fastest.
Arguments:
- tokens: bfloat16 [24576, 768], P('wide'), may hold values from -6 to 6
- qkv_weight: bfloat16 [3, 768, 768], P(None, None, 'narrow'), may hold values from -0.21875 to 0.21875
- out_weight: bfloat16 [768, 768], P('narrow'), may hold values from -0.875 to 0.875
- norm_bias: float32 [6, 768], replicated, as said below
- up_weight: bfloat16 [2, 768, 3072], P(None, None, 'narrow'), may hold values from -0.21875 to 0.21875
- down_weight: bfloat16 [3072, 768], P('narrow'), may hold values from -0.15625 to 0.15625
- window_lengths: int32 [48], P('wide'), may hold values from 64 to 512, as said below
- cot_out: bfloat16 [24576, 768], P('wide'), may hold values from -6 to 6
Outputs:
- block_out: bfloat16 [24576, 768], P('wide')
- input_grad: float32 [24576, 768], P('wide')
- qkv_grad: float32 [3, 768, 768], P(None, 'wide', 'narrow')
- out_grad: float32 [768, 768], P('narrow', 'wide')
- up_grad: float32 [2, 768, 3072], P(None, 'wide', 'narrow')
- down_grad: float32 [3072, 768], P('narrow', 'wide')
- norm_bias_grad: float32 [6, 768], P(None, 'wide')
The draws below stay inside these ranges and needn't reach their ends.
Inputs may be any that keep to these rules, and one draw needn't show every extreme that they name: `window_lengths`: keys at or past a window's length are padding; some window holds exactly 512 and some exactly 64. `norm_bias`: rows 0 and 3 lie between 0.5 and 2.
All inputs are finite; a program needn't handle non-finite values.
Results may differ from the reference program's by a relative error of at most 0.025.
Values may be sent and summed in bfloat16 or wider, within the bound.
A program may use at most 192 MiB of HBM per device.

```python
import math
import jax
import jax.numpy as jnp
from jax import lax

D = 768
HEADS = 12
HEAD_DIM = 64
FF = 3072
WIN_LEN = 512
WINDOWS = 48
TOKENS = 24576
N_NARROW = 4


def draw_window_lengths(key, part):
    first, second, third = jax.random.split(key, 3)
    lengths = jax.random.randint(first, (WINDOWS,), WIN_LEN // 8, WIN_LEN + 1)
    full_at = jax.random.randint(second, (), 0, WINDOWS)
    short_at = (full_at + 1 + jax.random.randint(third, (), 0, WINDOWS - 1)) % WINDOWS
    lengths = lengths.at[full_at].set(WIN_LEN).at[short_at].set(WIN_LEN // 8)
    return lengths.astype(jnp.int32)


def draw_norm_bias(key, part):
    first, second = jax.random.split(key)
    gains = jnp.exp(jax.random.uniform(first, (2, D), jnp.float32, -0.69, 0.69))
    shifts = 0.3 * jax.random.normal(second, (4, D), jnp.float32)
    return jnp.stack([gains[0], shifts[0], shifts[1], gains[1], shifts[2], shifts[3]]).astype(jnp.float32)


def strengthened(values, key, source, target, blocks, factor):
    owner, partner = [(jnp.arange(values.shape[dim]) // (values.shape[dim] // blocks)).reshape([-1 if axis == dim else 1 for axis in range(values.ndim)]) for dim in (source, target)]
    chosen = jax.random.permutation(key, blocks)[partner]
    strong = (owner == chosen) | (owner == (partner + blocks // 2) % blocks)
    return jnp.where(strong, factor * values, values)


def level_of(key, shape, cuts, low, high):
    def one(dim, blocks):
        heights = jax.random.uniform(jax.random.fold_in(jax.random.fold_in(key, 6), dim), (blocks,), jnp.float32, low / len(cuts), high / len(cuts))
        return jnp.repeat(jnp.exp(heights), shape[dim] // blocks).reshape((-1,) + (1,) * (len(shape) - dim - 1))

    factor_of = one(*cuts[0])
    for cut in cuts[1:]:
        factor_of = factor_of * one(*cut)
    return factor_of


def normal_values(key, shape, width, limit, pieces=(), kind=jnp.bfloat16):
    array = width * jax.random.normal(key, shape, jnp.float32)
    if pieces:
        array = array * level_of(key, shape, pieces, -0.22, 0.18)
    return jnp.clip(array, -limit, limit).astype(kind)


def heavy_noise(rng, shape, deviation, most, cuts, heavy, kind=jnp.bfloat16):
    values = deviation * jax.random.normal(rng, shape, jnp.float32)
    if cuts:
        values = values * level_of(rng, shape, cuts, -0.22, 0.18)
    return jnp.clip(strengthened(values, jax.random.fold_in(rng, 3), *heavy), -most, most).astype(kind)


def setup_inputs(seed: int = 0) -> dict:
    key_list = jax.random.split(jax.random.key(seed), 9)
    tokens = heavy_noise(key_list[0], (TOKENS, D), 1.0, 6.0, ((0, 8),), (0, 1, 8, 2.0))
    qkv_weight = normal_values(key_list[1], (3, D, D), D ** -0.5, 0.21875, ((2, 4),))
    out_weight = normal_values(key_list[2], (D, D), (D // 16) ** -0.5, 0.875, ((0, 4),))
    norm_bias = draw_norm_bias(jax.random.fold_in(key_list[8], 71), 0)
    up_weight = normal_values(key_list[4], (2, D, FF), D ** -0.5, 0.21875, ((2, 4),))
    down_weight = normal_values(key_list[5], (FF, D), (FF // 2) ** -0.5, 0.15625, ((0, 4),))
    window_lengths = draw_window_lengths(jax.random.fold_in(key_list[8], 71), 0)
    cot_out = heavy_noise(key_list[7], (TOKENS, D), 1.0, 6.0, ((0, 8),), (0, 1, 8, 2.0))
    return {"tokens": tokens, "qkv_weight": qkv_weight, "out_weight": out_weight, "norm_bias": norm_bias, "up_weight": up_weight, "down_weight": down_weight, "window_lengths": window_lengths, "cot_out": cot_out}


@jax.custom_vjp
def low(v):
    return lax.optimization_barrier(v.astype(jnp.bfloat16)).astype(jnp.float32)

@jax.custom_vjp
def low_back(v):
    return v

def low_keep(v):
    return (low(v), None)

def low_pass(kept, grad):
    return (grad,)

def back_keep(v):
    return (v, None)

def back_low(kept, grad):
    return (low(grad),)
low.defvjp(low_keep, low_pass)
low_back.defvjp(back_keep, back_low)

def layer_norm(value, gain, shift):
    center = value - lax.optimization_barrier(jnp.mean(value, axis=-1, keepdims=True))
    spread = lax.optimization_barrier(jnp.mean(center * center, axis=-1, keepdims=True))
    return center * lax.rsqrt(spread + 1e-05) * gain + shift

def attend(window, length):
    raw_scores = low_back(jnp.einsum('hqc,hkc->hqk', window[0], window[1], precision=lax.Precision.HIGHEST))
    position = jnp.arange(WIN_LEN)
    distance = jnp.abs(position[:, None] - position[None, :]).astype(jnp.float32)
    slopes = 2.0 ** (-8.0 * (jnp.arange(HEADS) + 1).astype(jnp.float32) / HEADS)
    logits = raw_scores * (1.0 / math.sqrt(HEAD_DIM)) - slopes[:, None, None] * distance[None]
    logits = jnp.where(position[None, None, :] < length, logits, -1e+30)
    weights_soft = low(jax.nn.softmax(logits, axis=-1))
    return jnp.einsum('hqk,hkc->hqc', weights_soft, window[2], precision=lax.Precision.HIGHEST)

def forward(source, qkv_w, out_w, norm_b, up_w, down_w, lengths):
    high = lax.Precision.HIGHEST
    count = source.shape[0]
    windows = count // WIN_LEN
    group_width = D // N_NARROW
    group_heads = HEADS // N_NARROW
    group_ff = FF // N_NARROW
    source_groups = low_back(jnp.broadcast_to(source[None], (N_NARROW, count, D)))
    projected = jnp.einsum('gtd,kdgf->kgtf', source_groups, qkv_w.reshape(3, D, N_NARROW, group_width), precision=high)
    projected = low_back(low(projected))
    blocks = projected.reshape(3, N_NARROW, windows, WIN_LEN, group_heads, HEAD_DIM)
    blocks = blocks.transpose(2, 0, 1, 4, 3, 5).reshape(windows, 3, HEADS, WIN_LEN, HEAD_DIM)
    attend_saved = jax.checkpoint(lambda item: attend(item[0], item[1]))
    attended = lax.map(attend_saved, (blocks, lengths))
    attended = attended.reshape(windows, N_NARROW, group_heads, WIN_LEN, HEAD_DIM)
    attended = low_back(low(attended.transpose(1, 0, 3, 2, 4).reshape(N_NARROW, count, group_width)))
    parts = jnp.einsum('gtf,gfe->gte', attended, out_w.reshape(N_NARROW, group_width, D), precision=high)
    attn_branch = low_back(lax.optimization_barrier(jnp.sum(low(parts), axis=0)))
    hidden = layer_norm(attn_branch + norm_b[2] + source, norm_b[0], norm_b[1])
    hidden_low = low(hidden)
    hidden_groups = low_back(jnp.broadcast_to(hidden_low[None], (N_NARROW, count, D)))
    gate_up = jnp.einsum('gtd,kdgf->kgtf', hidden_groups, up_w.reshape(2, D, N_NARROW, group_ff), precision=high)
    gate_up = low_back(gate_up)
    activation = low(jax.nn.gelu(gate_up[0], approximate=False) * gate_up[1])
    parts_ffn = jnp.einsum('gtf,gfe->gte', activation, down_w.reshape(N_NARROW, group_ff, D), precision=high)
    ffn_branch = low_back(lax.optimization_barrier(jnp.sum(low(parts_ffn), axis=0)))
    return layer_norm(ffn_branch + norm_b[5] + hidden, norm_b[3], norm_b[4])

def reference(tokens, qkv_weight, out_weight, norm_bias, up_weight, down_weight, window_lengths, cot_out):

    def run(source, qkv_w, out_w, norm_b, up_w, down_w):
        return forward(source, qkv_w, out_w, norm_b, up_w, down_w, window_lengths)
    result, pullback = jax.vjp(run, tokens.astype(jnp.float32), qkv_weight.astype(jnp.float32), out_weight.astype(jnp.float32), norm_bias.astype(jnp.float32), up_weight.astype(jnp.float32), down_weight.astype(jnp.float32))
    grads = pullback(cot_out.astype(jnp.float32))
    return (result.astype(jnp.bfloat16), grads[0], grads[1], grads[2], grads[4], grads[5], grads[3])
```

```python
import functools
import math

import jax
import jax.numpy as jnp
from jax import lax
from jax.experimental import pallas as pl
from jax.experimental.pallas import tpu as pltpu
from jax.sharding import Mesh, PartitionSpec as P

HEADS = 12
HEAD_DIM = 64
EPS = 1e-05
F32 = jnp.float32
BF16 = jnp.bfloat16
SCALE = 1.0 / math.sqrt(HEAD_DIM)
NEG = -1e30
VMEM_LIMIT = 56 * 1024 * 1024


def dot(a, b):
    return lax.dot_general(a, b, (((1,), (0,)), ((), ())), preferred_element_type=F32)


def dot_nt(a, b):
    return lax.dot_general(a, b, (((1,), (1,)), ((), ())), preferred_element_type=F32)


def dot_tn(a, b):
    return lax.dot_general(a, b, (((0,), (0,)), ((), ())), preferred_element_type=F32)


def whole(shape):
    return pl.BlockSpec(shape, lambda i, *_: (0,) * len(shape))


def head_lanes(width):
    lane = lax.broadcasted_iota(jnp.int32, (1, width), 1)
    return [(lane >= h * HEAD_DIM) & (lane < (h + 1) * HEAD_DIM) for h in range(width // HEAD_DIM)]


def fill_distance(ref):
    n = ref.shape[0]
    row = lax.broadcasted_iota(jnp.int32, (n, n), 0)
    col = lax.broadcasted_iota(jnp.int32, (n, n), 1)
    ref[...] = jnp.abs(row - col).astype(F32)


def params():
    return pltpu.CompilerParams(vmem_limit_bytes=VMEM_LIMIT, dimension_semantics=("arbitrary",))


def attn_fwd_kernel(last, info, slopes, x_ref, wqkv, wout, *rest):
    if last:
        prev, proj, att_ref, lse_ref, part, dist = rest
    else:
        proj, att_ref, lse_ref, part, dist = rest
    step = pl.program_id(0)
    win = x_ref.shape[0]
    width = wqkv.shape[2]
    heads = width // HEAD_DIM

    @pl.when(step == 0)
    def _():
        fill_distance(dist)

    x = x_ref[...]
    q = dot(x, wqkv[0]).astype(BF16)
    k = dot(x, wqkv[1]).astype(BF16)
    v = dot(x, wqkv[2]).astype(BF16)
    proj[0], proj[1], proj[2] = q, k, v
    limit = info[1 + info[0] * pl.num_programs(0) + step]
    lanes = head_lanes(width)
    key_on = lax.broadcasted_iota(jnp.int32, (1, win), 1) < limit
    rows = win // 2
    stat_lane = lax.broadcasted_iota(jnp.int32, (1, 128), 1)
    for b in range(win // rows):
        at = slice(b * rows, (b + 1) * rows)
        qb = q[at] * jnp.asarray(SCALE, BF16)
        att = jnp.zeros((rows, width), F32)
        stat = jnp.zeros((rows, 128), F32)
        for h in range(heads):
            qh = jnp.where(lanes[h], qb, jnp.zeros_like(qb))
            s = dot_nt(qh, k) - slopes[h] * dist[at]
            s = jnp.where(key_on, s, NEG)
            top = jnp.max(s, axis=1, keepdims=True)
            p = jnp.exp(s - top)
            total = jnp.sum(p, axis=1, keepdims=True)
            o = dot(p.astype(BF16), v) * (1.0 / total)
            att = jnp.where(lanes[h], o, att)
            stat = jnp.where(stat_lane == h, top + jnp.log(total), stat)
        attb = att.astype(BF16)
        att_ref[at] = attb
        lse_ref[0, :, at] = stat.T[0:8]
        out = dot(attb, wout[...])
        if last:
            out = out + prev[at].astype(F32)
        part[at] = out.astype(BF16)


def attn_fwd(info, slopes, tokens, wqkv, wout, prev):
    _, d, width = wqkv.shape
    nwin = (info.shape[0] - 1) // 2
    win = tokens.shape[0] // (2 * nwin)
    half = nwin * win
    last = prev is not None
    heads = width // HEAD_DIM
    row = lambda w: pl.BlockSpec((win, w), lambda i, *_: (i, 0))
    specs = [
        pl.BlockSpec((win, d), lambda i, info, sl: (info[0] * nwin + i, 0)),
        whole(wqkv.shape),
        whole(wout.shape),
    ]
    args = [tokens, wqkv, wout]
    if last:
        specs.append(row(d))
        args.append(prev)
    return pl.pallas_call(
        functools.partial(attn_fwd_kernel, last),
        grid_spec=pltpu.PrefetchScalarGridSpec(
            num_scalar_prefetch=2,
            grid=(nwin,),
            in_specs=specs,
            out_specs=[
                pl.BlockSpec((3, win, width), lambda i, *_: (0, i, 0)),
                row(width),
                pl.BlockSpec((1, 8, win), lambda i, *_: (i, 0, 0)),
                row(d),
            ],
            scratch_shapes=[pltpu.VMEM((win, win), F32)],
        ),
        out_shape=[
            jax.ShapeDtypeStruct((3, half, width), BF16),
            jax.ShapeDtypeStruct((half, width), BF16),
            jax.ShapeDtypeStruct((nwin, 8, win), F32),
            jax.ShapeDtypeStruct((half, d), BF16),
        ],
        compiler_params=params(),
        cost_estimate=pl.CostEstimate(
            flops=2 * half * d * width * 4 + 4 * nwin * heads * win * win * 256,
            bytes_accessed=2 * (half * d * 2 + half * width * 4 + d * width * 4),
            transcendentals=nwin * heads * win * win,
        ),
        name="attn_fwd_last" if last else "attn_fwd_first",
    )(info, slopes, *args)


def standardize(value):
    center = value - jnp.mean(value, axis=1, keepdims=True)
    recip = lax.rsqrt(jnp.mean(center * center, axis=1, keepdims=True) + EPS)
    return center * recip, recip


def norm_grad(grad, normed, recip, gain):
    e = grad * gain
    inner = jnp.mean(e * normed, axis=1, keepdims=True)
    return recip * (e - jnp.mean(e, axis=1, keepdims=True) - normed * inner)


def rows_of_sums(values):
    width = values[0].shape[1]
    sums = [jnp.sum(v, axis=0, keepdims=True) for v in values]
    return jnp.concatenate(sums + [jnp.zeros((8 - len(sums), width), F32)], axis=0)


def feed(hb, up, down, a_ref, b_ref, act_ref):
    hidden = down.shape[0]
    step = 256
    total = None
    for at in range(0, hidden, step):
        cols = slice(at, at + step)
        gate = dot(hb, up[0, :, cols])
        lift = dot(hb, up[1, :, cols])
        cdf = 0.5 * (1.0 + lax.erf(gate * (1.0 / math.sqrt(2.0))))
        pdf = jnp.exp(-0.5 * gate * gate) * (1.0 / math.sqrt(2.0 * math.pi))
        gelu = gate * cdf
        act = (gelu * lift).astype(BF16)
        a_ref[:, cols] = (lift * (cdf + gate * pdf)).astype(BF16)
        b_ref[:, cols] = gelu.astype(BF16)
        act_ref[:, cols] = act
        term = dot(act, down[cols, :])
        total = term if total is None else total + term
    return total


def ffn_first_kernel(pa, pb, x_ref, nb, up, down, normed_ref, recip_ref, h_ref, a_ref, b_ref, act_ref, part):
    first = pa[...].astype(F32) + pb[...].astype(F32) + nb[2:3] + x_ref[...].astype(F32)
    normed, recip = standardize(first)
    normed_ref[...] = normed
    recip_ref[...] = jnp.broadcast_to(recip, recip_ref.shape)
    hb = (normed * nb[0:1] + nb[1:2]).astype(BF16)
    h_ref[...] = hb
    part[...] = feed(hb, up, down, a_ref, b_ref, act_ref).astype(BF16)


def ffn_second_kernel(hb, prev, up, down, a_ref, b_ref, act_ref, part):
    total = feed(hb[...], up, down, a_ref, b_ref, act_ref)
    part[...] = (total + prev[...].astype(F32)).astype(BF16)


def ffn_first(half_block, pa, pb, tokens, nb, up, down, tile=256):
    half, d = pa.shape
    hidden = down.shape[0]
    n = half // tile
    row = lambda w: pl.BlockSpec((tile, w), lambda i, *_: (i, 0))

    def kernel(info, *refs):
        ffn_first_kernel(*refs)

    return pl.pallas_call(
        kernel,
        grid_spec=pltpu.PrefetchScalarGridSpec(
            num_scalar_prefetch=1,
            grid=(n,),
            in_specs=[
                row(d),
                row(d),
                pl.BlockSpec((tile, d), lambda i, info: (info[0] * n + i, 0)),
                whole(nb.shape),
                whole(up.shape),
                whole(down.shape),
            ],
            out_specs=[row(d), row(128), row(d), row(hidden), row(hidden), row(hidden), row(d)],
        ),
        out_shape=[
            jax.ShapeDtypeStruct((half, d), F32),
            jax.ShapeDtypeStruct((half, 128), F32),
            jax.ShapeDtypeStruct((half, d), BF16),
            jax.ShapeDtypeStruct((half, hidden), BF16),
            jax.ShapeDtypeStruct((half, hidden), BF16),
            jax.ShapeDtypeStruct((half, hidden), BF16),
            jax.ShapeDtypeStruct((half, d), BF16),
        ],
        compiler_params=params(),
        cost_estimate=pl.CostEstimate(
            flops=6 * half * d * hidden, bytes_accessed=half * d * 14 + half * hidden * 6 + 6 * d * hidden,
            transcendentals=half * hidden * 2,
        ),
        name="ffn_first",
    )(half_block, pa, pb, tokens, nb, up, down)


def ffn_second(hb, prev, up, down, tile=256):
    half, d = hb.shape
    hidden = down.shape[0]
    row = lambda w: pl.BlockSpec((tile, w), lambda i: (i, 0))
    return pl.pallas_call(
        ffn_second_kernel,
        grid=(half // tile,),
        in_specs=[row(d), row(d), whole(up.shape), whole(down.shape)],
        out_specs=[row(hidden), row(hidden), row(hidden), row(d)],
        out_shape=[jax.ShapeDtypeStruct((half, hidden), BF16)] * 3 + [jax.ShapeDtypeStruct((half, d), BF16)],
        compiler_params=params(),
        cost_estimate=pl.CostEstimate(
            flops=6 * half * d * hidden, bytes_accessed=half * d * 6 + half * hidden * 6 + 6 * d * hidden,
            transcendentals=half * hidden * 2,
        ),
        name="ffn_second",
    )(hb, prev, up, down)


def ffn_bwd_kernel(info, pa, pb, normed_ref, cot, nb, up0, up1, down0, down1, a0, a1, b0, b1,
                   out_ref, d2_ref, d2b_ref, dgu0, dgu1, dh_ref, sums_ref):
    hidden = down0.shape[0]
    h = normed_ref[...] * nb[0:1] + nb[1:2]
    second = pa[...].astype(F32) + pb[...].astype(F32) + nb[5:6] + h
    normed, recip = standardize(second)
    gain = nb[3:4]
    out_ref[...] = (normed * gain + nb[4:5]).astype(BF16)
    c = cot[...].astype(F32)
    d2 = norm_grad(c, normed, recip, gain)
    d2_ref[...] = d2
    d2b = d2.astype(BF16)
    d2b_ref[...] = d2b
    sums = rows_of_sums([c * normed, c, d2])

    @pl.when(pl.program_id(0) == 0)
    def _():
        sums_ref[...] = sums

    @pl.when(pl.program_id(0) > 0)
    def _():
        sums_ref[...] += sums

    total = None
    step = 256
    for up, down, a_ref, b_ref, dgu in ((up0, down0, a0, b0, dgu0), (up1, down1, a1, b1, dgu1)):
        for at in range(0, hidden, step):
            cols = slice(at, at + step)
            dact = dot_nt(d2b, down[cols, :])
            dg = (dact * a_ref[:, cols].astype(F32)).astype(BF16)
            du = (dact * b_ref[:, cols].astype(F32)).astype(BF16)
            dgu[:, cols] = dg
            dgu[:, slice(hidden + at, hidden + at + step)] = du
            term = dot_nt(dg, up[0, :, cols]) + dot_nt(du, up[1, :, cols])
            total = term if total is None else total + term
    dh_ref[...] = total.astype(BF16)


def ffn_bwd(info, pa, pb, normed, cot, nb, up0, up1, down0, down1, a0, a1, b0, b1, tile=256):
    half, d = pa.shape
    hidden = down0.shape[0]
    n = half // tile
    row = lambda w: pl.BlockSpec((tile, w), lambda i, *_: (i, 0))
    return pl.pallas_call(
        ffn_bwd_kernel,
        grid_spec=pltpu.PrefetchScalarGridSpec(
            num_scalar_prefetch=1,
            grid=(n,),
            in_specs=[
                row(d), row(d), row(d),
                pl.BlockSpec((tile, d), lambda i, info: (info[0] * n + i, 0)),
                whole(nb.shape),
                whole(up0.shape), whole(up1.shape), whole(down0.shape), whole(down1.shape),
                row(hidden), row(hidden), row(hidden), row(hidden),
            ],
            out_specs=[row(d), row(d), row(d), row(2 * hidden), row(2 * hidden), row(d), whole((8, d))],
        ),
        out_shape=[
            jax.ShapeDtypeStruct((half, d), BF16),
            jax.ShapeDtypeStruct((half, d), F32),
            jax.ShapeDtypeStruct((half, d), BF16),
            jax.ShapeDtypeStruct((half, 2 * hidden), BF16),
            jax.ShapeDtypeStruct((half, 2 * hidden), BF16),
            jax.ShapeDtypeStruct((half, d), BF16),
            jax.ShapeDtypeStruct((8, d), F32),
        ],
        compiler_params=params(),
        cost_estimate=pl.CostEstimate(
            flops=12 * half * d * hidden, bytes_accessed=half * d * 20 + half * hidden * 16 + 12 * d * hidden,
            transcendentals=half,
        ),
        name="ffn_bwd",
    )(info, pa, pb, normed, cot, nb, up0, up1, down0, down1, a0, a1, b0, b1)


def attn_bwd_kernel(info, slopes, d2_ref, ha, hb, normed_ref, recip_ref, nb, wqkv0, wqkv1, wout0, wout1,
                    proj0, proj1, att0, att1, lse0, lse1,
                    d1_ref, d1b_ref, dproj0, dproj1, part, sums_ref, dist):
    step = pl.program_id(0)
    win = d2_ref.shape[0]
    width = wout0.shape[0]
    heads = width // HEAD_DIM

    @pl.when(step == 0)
    def _():
        fill_distance(dist)

    normed = normed_ref[...]
    dh = d2_ref[...] + (ha[...].astype(F32) + hb[...].astype(F32))
    d1 = norm_grad(dh, normed, recip_ref[:, 0:1], nb[0:1])
    d1_ref[...] = d1
    d1b = d1.astype(BF16)
    d1b_ref[...] = d1b
    sums = rows_of_sums([dh * normed, dh, d1])

    @pl.when(step == 0)
    def _():
        sums_ref[...] = sums

    @pl.when(step > 0)
    def _():
        sums_ref[...] += sums

    limit = info[1 + info[0] * pl.num_programs(0) + step]
    lanes = head_lanes(width)
    key_on = lax.broadcasted_iota(jnp.int32, (win, 1), 0) < limit
    stat_lane = lax.broadcasted_iota(jnp.int32, (1, 128), 1)
    total = None
    for g, (wqkv, wout, proj, att_ref, lse, dproj) in enumerate(
        ((wqkv0, wout0, proj0, att0, lse0, dproj0), (wqkv1, wout1, proj1, att1, lse1, dproj1))
    ):
        q, k, v = proj[0], proj[1], proj[2]
        datt = dot_nt(d1b, wout[...]).astype(BF16)
        product = datt.astype(F32) * att_ref[...].astype(F32)
        stat = jnp.zeros((win, 128), F32)
        for h in range(heads):
            inner = jnp.sum(jnp.where(lanes[h], product, 0.0), axis=1, keepdims=True)
            stat = jnp.where(stat_lane == h, inner, stat)
        inner_rows = stat.T[0:8]
        qs = q * jnp.asarray(SCALE, BF16)
        dq = jnp.zeros((win, width), F32)
        dk = jnp.zeros((win, width), F32)
        dv = jnp.zeros((win, width), F32)
        for h in range(heads):
            qh = jnp.where(lanes[h], qs, jnp.zeros_like(qs))
            oh = jnp.where(lanes[h], datt, jnp.zeros_like(datt))
            s = dot_nt(k, qh) - slopes[g * heads + h] * dist[...]
            s = jnp.where(key_on, s, NEG)
            p = jnp.exp(s - lse[0, h:h + 1, :])
            dp = dot_nt(v, oh)
            ds = (p * (dp - inner_rows[h:h + 1, :])).astype(BF16)
            dv = jnp.where(lanes[h], dot(p.astype(BF16), datt), dv)
            dk = jnp.where(lanes[h], dot(ds, q), dk)
            dq = jnp.where(lanes[h], dot_tn(ds, k), dq)
        dqb = (dq * SCALE).astype(BF16)
        dkb = (dk * SCALE).astype(BF16)
        dvb = dv.astype(BF16)
        dproj[0], dproj[1], dproj[2] = dqb, dkb, dvb
        term = dot_nt(dqb, wqkv[0]) + dot_nt(dkb, wqkv[1]) + dot_nt(dvb, wqkv[2])
        total = term if total is None else total + term
    part[...] = total.astype(BF16)


def attn_bwd(info, slopes, d2, ha, hb, normed, recip, nb, wqkv0, wqkv1, wout0, wout1,
             proj0, proj1, att0, att1, lse0, lse1):
    half, d = d2.shape
    width = wout0.shape[0]
    nwin, _, win = lse0.shape
    heads = 2 * width // HEAD_DIM
    row = lambda w: pl.BlockSpec((win, w), lambda i, *_: (i, 0))
    deep = pl.BlockSpec((3, win, width), lambda i, *_: (0, i, 0))
    stat = pl.BlockSpec((1, 8, win), lambda i, *_: (i, 0, 0))
    return pl.pallas_call(
        attn_bwd_kernel,
        grid_spec=pltpu.PrefetchScalarGridSpec(
            num_scalar_prefetch=2,
            grid=(nwin,),
            in_specs=[
                row(d), row(d), row(d), row(d), row(128), whole(nb.shape),
                whole(wqkv0.shape), whole(wqkv1.shape), whole(wout0.shape), whole(wout1.shape),
                deep, deep, row(width), row(width), stat, stat,
            ],
            out_specs=[row(d), row(d), deep, deep, row(d), whole((8, d))],
            scratch_shapes=[pltpu.VMEM((win, win), F32)],
        ),
        out_shape=[
            jax.ShapeDtypeStruct((half, d), F32),
            jax.ShapeDtypeStruct((half, d), BF16),
            jax.ShapeDtypeStruct((3, half, width), BF16),
            jax.ShapeDtypeStruct((3, half, width), BF16),
            jax.ShapeDtypeStruct((half, d), BF16),
            jax.ShapeDtypeStruct((8, d), F32),
        ],
        compiler_params=params(),
        cost_estimate=pl.CostEstimate(
            flops=2 * half * d * width * 8 + 10 * nwin * heads * win * win * 256,
            bytes_accessed=half * d * 20 + half * width * 32 + d * width * 16,
            transcendentals=nwin * heads * win * win,
        ),
        name="attn_bwd",
    )(info, slopes, d2, ha, hb, normed, recip, nb, wqkv0, wqkv1, wout0, wout1,
      proj0, proj1, att0, att1, lse0, lse1)


def place_kernel(order, mine, near, far, out):
    step = pl.program_id(0)

    @pl.when(step < 2)
    def _():
        out[...] = mine[...].astype(out.dtype)

    @pl.when(step == 2)
    def _():
        out[...] = near[...].astype(out.dtype)

    @pl.when(step == 3)
    def _():
        out[...] = far[...].astype(out.dtype)


def place(order, mine, near, far, dtype):
    quarter, d = near.shape
    return pl.pallas_call(
        place_kernel,
        grid_spec=pltpu.PrefetchScalarGridSpec(
            num_scalar_prefetch=1,
            grid=(4,),
            in_specs=[
                pl.BlockSpec((quarter, d), lambda i, o: (jnp.minimum(i, 1), 0)),
                whole((quarter, d)),
                whole((quarter, d)),
            ],
            out_specs=pl.BlockSpec((quarter, d), lambda i, o: (o[i], 0)),
        ),
        out_shape=jax.ShapeDtypeStruct((4 * quarter, d), dtype),
        compiler_params=params(),
        cost_estimate=pl.CostEstimate(flops=0, bytes_accessed=24 * quarter * d, transcendentals=0),
        name="place",
    )(order, mine, near, far)


SWAP = [(0, 1), (1, 0)]
WIDE = ("wo", "x")


def swap(value, axis):
    return lax.ppermute(value, axis, SWAP)


def shards(tokens, wqkv, wout, nb, up, down, lengths, cot):
    x_at, y_at, c_at = (lax.axis_index(name) for name in ("x", "y", "core"))
    group_heads = wqkv.shape[2] // HEAD_DIM
    own = 2 * y_at + c_at
    heads = jnp.concatenate([own * group_heads + jnp.arange(group_heads), (own ^ 2) * group_heads + jnp.arange(group_heads)])
    slopes = 2.0 ** (-8.0 * (heads + 1).astype(F32) / HEADS)
    info = jnp.concatenate([y_at[None].astype(jnp.int32), lengths])

    wqkv1 = swap(wqkv, "y")
    wout1 = swap(wout, "y")
    half_up = swap(lax.dynamic_index_in_dim(up, x_at, 0, keepdims=False), "y")
    other_up = swap(half_up, "x")
    up1 = jnp.stack([jnp.where(x_at == 0, half_up, other_up), jnp.where(x_at == 0, other_up, half_up)])
    rows = down.shape[0] // 2
    half_down = swap(lax.dynamic_slice_in_dim(down, x_at * rows, rows, 0), "y")
    other_down = swap(half_down, "x")
    down1 = jnp.concatenate(
        [jnp.where(x_at == 0, half_down, other_down), jnp.where(x_at == 0, other_down, half_down)], axis=0
    )

    proj0, att0, lse0, part0 = attn_fwd(info, slopes[:group_heads], tokens, wqkv, wout, None)
    proj1, att1, lse1, part = attn_fwd(info, slopes[group_heads:], tokens, wqkv1, wout1, part0)
    part_other = swap(part, "core")
    normed, recip, hb, a0, b0, act0, fpart0 = ffn_first(info, part, part_other, tokens, nb, up, down)
    a1, b1, act1, fpart = ffn_second(hb, fpart0, up1, down1)
    fpart_other = swap(fpart, "core")
    out, d2, d2b, dgu0, dgu1, dh, sums2 = ffn_bwd(
        info, fpart, fpart_other, normed, cot, nb, up, up1, down, down1, a0, a1, b0, b1
    )
    dh_other = swap(dh, "core")

    def grad(a, b):
        return lax.dot_general(a, b, (((0,), (0,)), ((), ())), preferred_element_type=F32)

    down_peer = swap(grad(d2b, act1).astype(BF16), "y")
    up_peer = swap(grad(hb, dgu1).astype(BF16), "y")
    down_all = (grad(d2b, act0) + down_peer.astype(F32)).astype(BF16)
    up_all = (grad(hb, dgu0) + up_peer.astype(F32)).astype(BF16)
    scatter = functools.partial(lax.psum_scatter, axis_name=WIDE, scatter_dimension=0, tiled=True)
    down_share = scatter(down_all).astype(F32).T
    up_share = scatter(up_all).astype(F32)
    hidden = down.shape[0]
    up_share = jnp.stack([up_share[:, :hidden], up_share[:, hidden:]])

    d1, d1b, dproj0, dproj1, ipart, sums1 = attn_bwd(
        info, slopes, d2, dh, dh_other, normed, recip, nb, wqkv, wqkv1, wout, wout1,
        proj0, proj1, att0, att1, lse0, lse1,
    )
    half = d1.shape[0]
    mine = lax.dynamic_slice_in_dim(tokens, y_at * half, half, 0)

    def attn_grads(dproj, att):
        pieces = [grad(mine, dproj[i]) for i in range(3)] + [grad(d1b, att)]
        return jnp.concatenate(pieces, axis=1)

    attn_peer = swap(attn_grads(dproj1, att1).astype(BF16), "y")
    attn_all = (attn_grads(dproj0, att0) + attn_peer.astype(F32)).astype(BF16)
    attn_share = scatter(attn_all).astype(F32)
    width = wqkv.shape[2]
    qkv_share = jnp.stack([attn_share[:, i * width:(i + 1) * width] for i in range(3)])
    out_share = attn_share[:, 3 * width:].T

    small = jnp.concatenate([sums1[:3], sums2[:3]], axis=0)
    small_share = lax.psum_scatter(lax.psum(small, "y"), WIDE, scatter_dimension=1, tiled=True)

    quarter = half // 2
    order = jnp.stack([2 * y_at, 2 * y_at + 1, 2 * (1 - y_at) + c_at, 2 * (1 - y_at) + 1 - c_at]).astype(jnp.int32)

    def share(value, dtype):
        near = swap(lax.dynamic_slice_in_dim(value, c_at * quarter, quarter, 0), "y")
        far = swap(near, "core")
        return place(order, value, near, far, dtype)

    block_out = share(out, BF16)
    ipart_other = swap(ipart, "core")
    total = (d1 + (ipart.astype(F32) + ipart_other.astype(F32))).astype(BF16)
    input_grad = share(total, F32)
    return (block_out, input_grad, qkv_share, out_share, up_share, down_share, small_share)


def solution(mesh):
    wide = mesh.shape["wide"]
    grid = Mesh(mesh.devices.reshape(wide // 2, 2, 2, 2), ("wo", "x", "y", "core"))
    narrow = ("y", "core")
    placed = (
        P(WIDE, None),
        P(None, None, narrow),
        P(narrow, None),
        P(),
        P(None, None, narrow),
        P(narrow, None),
        P(WIDE),
        P(WIDE, None),
    )
    return jax.shard_map(
        shards,
        mesh=grid,
        in_specs=placed,
        out_specs=(
            P(WIDE, None),
            P(WIDE, None),
            P(None, WIDE, narrow),
            P(narrow, WIDE),
            P(None, WIDE, narrow),
            P(narrow, WIDE),
            P(None, WIDE),
        ),
        check_vma=False,
    )
```

```python
import functools
import math

import jax
import jax.numpy as jnp
from jax import lax
from jax.experimental import pallas as pl
from jax.experimental.pallas import tpu as pltpu
from jax.sharding import Mesh, PartitionSpec as P

HEADS = 12
HEAD_DIM = 64
EPS = 1e-05
F32 = jnp.float32
BF16 = jnp.bfloat16
SCALE = 1.0 / math.sqrt(HEAD_DIM)
NEG = -1e30
VMEM_LIMIT = 56 * 1024 * 1024


def dot(a, b):
    return lax.dot_general(a, b, (((1,), (0,)), ((), ())), preferred_element_type=F32)


def dot_nt(a, b):
    return lax.dot_general(a, b, (((1,), (1,)), ((), ())), preferred_element_type=F32)


def dot_tn(a, b):
    return lax.dot_general(a, b, (((0,), (0,)), ((), ())), preferred_element_type=F32)


def whole(shape):
    return pl.BlockSpec(shape, lambda i, *_: (0,) * len(shape))


def head_lanes(width):
    lane = lax.broadcasted_iota(jnp.int32, (1, width), 1)
    return [(lane >= h * HEAD_DIM) & (lane < (h + 1) * HEAD_DIM) for h in range(width // HEAD_DIM)]


def fill_distance(ref):
    n = ref.shape[0]
    row = lax.broadcasted_iota(jnp.int32, (n, n), 0)
    col = lax.broadcasted_iota(jnp.int32, (n, n), 1)
    ref[...] = jnp.abs(row - col).astype(F32)


def params():
    return pltpu.CompilerParams(vmem_limit_bytes=VMEM_LIMIT, dimension_semantics=("arbitrary",))


def attn_fwd_kernel(last, info, slopes, x_ref, wqkv, wout, *rest):
    if last:
        prev, proj, att_ref, lse_ref, part, dist = rest
    else:
        proj, att_ref, lse_ref, part, dist = rest
    step = pl.program_id(0)
    win = x_ref.shape[0]
    width = wqkv.shape[2]
    heads = width // HEAD_DIM

    @pl.when(step == 0)
    def _():
        fill_distance(dist)

    x = x_ref[...]
    q = dot(x, wqkv[0]).astype(BF16)
    k = dot(x, wqkv[1]).astype(BF16)
    v = dot(x, wqkv[2]).astype(BF16)
    proj[0], proj[1], proj[2] = q, k, v
    limit = info[1 + info[0] * pl.num_programs(0) + step]
    lanes = head_lanes(width)
    key_on = lax.broadcasted_iota(jnp.int32, (1, win), 1) < limit
    rows = win // 2
    stat_lane = lax.broadcasted_iota(jnp.int32, (1, 128), 1)
    for b in range(win // rows):
        at = slice(b * rows, (b + 1) * rows)
        qb = q[at] * jnp.asarray(SCALE, BF16)
        att = jnp.zeros((rows, width), F32)
        stat = jnp.zeros((rows, 128), F32)
        for h in range(heads):
            qh = jnp.where(lanes[h], qb, jnp.zeros_like(qb))
            s = dot_nt(qh, k) - slopes[h] * dist[at]
            s = jnp.where(key_on, s, NEG)
            top = jnp.max(s, axis=1, keepdims=True)
            p = jnp.exp(s - top)
            total = jnp.sum(p, axis=1, keepdims=True)
            o = dot(p.astype(BF16), v) * (1.0 / total)
            att = jnp.where(lanes[h], o, att)
            stat = jnp.where(stat_lane == h, top + jnp.log(total), stat)
        attb = att.astype(BF16)
        att_ref[at] = attb
        lse_ref[0, :, at] = stat.T[0:8]
        out = dot(attb, wout[...])
        if last:
            out = out + prev[at].astype(F32)
        part[at] = out.astype(BF16)


def attn_fwd(info, slopes, tokens, wqkv, wout, prev):
    _, d, width = wqkv.shape
    nwin = (info.shape[0] - 1) // 2
    win = tokens.shape[0] // (2 * nwin)
    half = nwin * win
    last = prev is not None
    heads = width // HEAD_DIM
    row = lambda w: pl.BlockSpec((win, w), lambda i, *_: (i, 0))
    specs = [
        pl.BlockSpec((win, d), lambda i, info, sl: (info[0] * nwin + i, 0)),
        whole(wqkv.shape),
        whole(wout.shape),
    ]
    args = [tokens, wqkv, wout]
    if last:
        specs.append(row(d))
        args.append(prev)
    return pl.pallas_call(
        functools.partial(attn_fwd_kernel, last),
        grid_spec=pltpu.PrefetchScalarGridSpec(
            num_scalar_prefetch=2,
            grid=(nwin,),
            in_specs=specs,
            out_specs=[
                pl.BlockSpec((3, win, width), lambda i, *_: (0, i, 0)),
                row(width),
                pl.BlockSpec((1, 8, win), lambda i, *_: (i, 0, 0)),
                row(d),
            ],
            scratch_shapes=[pltpu.VMEM((win, win), F32)],
        ),
        out_shape=[
            jax.ShapeDtypeStruct((3, half, width), BF16),
            jax.ShapeDtypeStruct((half, width), BF16),
            jax.ShapeDtypeStruct((nwin, 8, win), F32),
            jax.ShapeDtypeStruct((half, d), BF16),
        ],
        compiler_params=params(),
        cost_estimate=pl.CostEstimate(
            flops=2 * half * d * width * 4 + 4 * nwin * heads * win * win * 256,
            bytes_accessed=2 * (half * d * 2 + half * width * 4 + d * width * 4),
            transcendentals=nwin * heads * win * win,
        ),
        name="attn_fwd_last" if last else "attn_fwd_first",
    )(info, slopes, *args)


def standardize(value):
    center = value - jnp.mean(value, axis=1, keepdims=True)
    recip = lax.rsqrt(jnp.mean(center * center, axis=1, keepdims=True) + EPS)
    return center * recip, recip


def norm_grad(grad, normed, recip, gain):
    e = grad * gain
    inner = jnp.mean(e * normed, axis=1, keepdims=True)
    return recip * (e - jnp.mean(e, axis=1, keepdims=True) - normed * inner)


def rows_of_sums(values):
    width = values[0].shape[1]
    sums = [jnp.sum(v, axis=0, keepdims=True) for v in values]
    return jnp.concatenate(sums + [jnp.zeros((8 - len(sums), width), F32)], axis=0)


def feed(hb, up, down, a_ref, b_ref, act_ref):
    hidden = down.shape[0]
    step = 256
    for at in range(0, hidden, step):
        cols = slice(at, at + step)
        gate = dot(hb, up[0, :, cols])
        lift = dot(hb, up[1, :, cols])
        cdf = 0.5 * (1.0 + lax.erf(gate * (1.0 / math.sqrt(2.0))))
        pdf = jnp.exp(-0.5 * gate * gate) * (1.0 / math.sqrt(2.0 * math.pi))
        gelu = gate * cdf
        act = (gelu * lift).astype(BF16)
        a_ref[:, cols] = (lift * (cdf + gate * pdf)).astype(BF16)
        b_ref[:, cols] = gelu.astype(BF16)
        act_ref[:, cols] = act
    return dot(act_ref[...], down[...])


def ffn_first_kernel(pa, pb, x_ref, nb, up, down, normed_ref, recip_ref, h_ref, a_ref, b_ref, act_ref, part):
    first = pa[...].astype(F32) + pb[...].astype(F32) + nb[2:3] + x_ref[...].astype(F32)
    normed, recip = standardize(first)
    normed_ref[...] = normed
    recip_ref[...] = jnp.broadcast_to(recip, recip_ref.shape)
    hb = (normed * nb[0:1] + nb[1:2]).astype(BF16)
    h_ref[...] = hb
    part[...] = feed(hb, up, down, a_ref, b_ref, act_ref).astype(BF16)


def ffn_second_kernel(hb, prev, up, down, a_ref, b_ref, act_ref, part):
    total = feed(hb[...], up, down, a_ref, b_ref, act_ref)
    part[...] = (total + prev[...].astype(F32)).astype(BF16)


def ffn_first(half_block, pa, pb, tokens, nb, up, down, tile=256):
    half, d = pa.shape
    hidden = down.shape[0]
    n = half // tile
    row = lambda w: pl.BlockSpec((tile, w), lambda i, *_: (i, 0))

    def kernel(info, *refs):
        ffn_first_kernel(*refs)

    return pl.pallas_call(
        kernel,
        grid_spec=pltpu.PrefetchScalarGridSpec(
            num_scalar_prefetch=1,
            grid=(n,),
            in_specs=[
                row(d),
                row(d),
                pl.BlockSpec((tile, d), lambda i, info: (info[0] * n + i, 0)),
                whole(nb.shape),
                whole(up.shape),
                whole(down.shape),
            ],
            out_specs=[row(d), row(128), row(d), row(hidden), row(hidden), row(hidden), row(d)],
        ),
        out_shape=[
            jax.ShapeDtypeStruct((half, d), F32),
            jax.ShapeDtypeStruct((half, 128), F32),
            jax.ShapeDtypeStruct((half, d), BF16),
            jax.ShapeDtypeStruct((half, hidden), BF16),
            jax.ShapeDtypeStruct((half, hidden), BF16),
            jax.ShapeDtypeStruct((half, hidden), BF16),
            jax.ShapeDtypeStruct((half, d), BF16),
        ],
        compiler_params=params(),
        cost_estimate=pl.CostEstimate(
            flops=6 * half * d * hidden, bytes_accessed=half * d * 14 + half * hidden * 6 + 6 * d * hidden,
            transcendentals=half * hidden * 2,
        ),
        name="ffn_first",
    )(half_block, pa, pb, tokens, nb, up, down)


def ffn_second(hb, prev, up, down, tile=256):
    half, d = hb.shape
    hidden = down.shape[0]
    row = lambda w: pl.BlockSpec((tile, w), lambda i: (i, 0))
    return pl.pallas_call(
        ffn_second_kernel,
        grid=(half // tile,),
        in_specs=[row(d), row(d), whole(up.shape), whole(down.shape)],
        out_specs=[row(hidden), row(hidden), row(hidden), row(d)],
        out_shape=[jax.ShapeDtypeStruct((half, hidden), BF16)] * 3 + [jax.ShapeDtypeStruct((half, d), BF16)],
        compiler_params=params(),
        cost_estimate=pl.CostEstimate(
            flops=6 * half * d * hidden, bytes_accessed=half * d * 6 + half * hidden * 6 + 6 * d * hidden,
            transcendentals=half * hidden * 2,
        ),
        name="ffn_second",
    )(hb, prev, up, down)


def ffn_bwd_kernel(info, pa, pb, normed_ref, cot, nb, up0, up1, down0, down1, a_all, b_all,
                   out_ref, d2_ref, d2b_ref, dgu0, dgu1, dh_ref, sums_ref):
    hidden = down0.shape[0]
    h = normed_ref[...] * nb[0:1] + nb[1:2]
    second = pa[...].astype(F32) + pb[...].astype(F32) + nb[5:6] + h
    normed, recip = standardize(second)
    gain = nb[3:4]
    out_ref[...] = (normed * gain + nb[4:5]).astype(BF16)
    c = cot[...].astype(F32)
    d2 = norm_grad(c, normed, recip, gain)
    d2_ref[...] = d2
    d2b = d2.astype(BF16)
    d2b_ref[...] = d2b
    sums = rows_of_sums([c * normed, c, d2])

    @pl.when(pl.program_id(0) == 0)
    def _():
        sums_ref[...] = sums

    @pl.when(pl.program_id(0) > 0)
    def _():
        sums_ref[...] += sums

    total = None
    step = 256
    for g, (up, down, dgu) in enumerate(((up0, down0, dgu0), (up1, down1, dgu1))):
        for at in range(0, hidden, step):
            cols = slice(at, at + step)
            dact = dot_nt(d2b, down[cols, :])
            dgu[:, cols] = (dact * a_all[g, :, cols].astype(F32)).astype(BF16)
            dgu[:, slice(hidden + at, hidden + at + step)] = (dact * b_all[g, :, cols].astype(F32)).astype(BF16)
        for k in range(2):
            term = dot_nt(dgu[:, k * hidden:(k + 1) * hidden], up[k])
            total = term if total is None else total + term
    dh_ref[...] = total.astype(BF16)


def ffn_bwd(info, pa, pb, normed, cot, nb, up0, up1, down0, down1, a_all, b_all, tile=256):
    half, d = pa.shape
    hidden = down0.shape[0]
    n = half // tile
    row = lambda w: pl.BlockSpec((tile, w), lambda i, *_: (i, 0))
    return pl.pallas_call(
        ffn_bwd_kernel,
        grid_spec=pltpu.PrefetchScalarGridSpec(
            num_scalar_prefetch=1,
            grid=(n,),
            in_specs=[
                row(d), row(d), row(d),
                pl.BlockSpec((tile, d), lambda i, info: (info[0] * n + i, 0)),
                whole(nb.shape),
                whole(up0.shape), whole(up1.shape), whole(down0.shape), whole(down1.shape),
                pl.BlockSpec((2, tile, hidden), lambda i, *_: (0, i, 0)),
                pl.BlockSpec((2, tile, hidden), lambda i, *_: (0, i, 0)),
            ],
            out_specs=[row(d), row(d), row(d), row(2 * hidden), row(2 * hidden), row(d), whole((8, d))],
        ),
        out_shape=[
            jax.ShapeDtypeStruct((half, d), BF16),
            jax.ShapeDtypeStruct((half, d), F32),
            jax.ShapeDtypeStruct((half, d), BF16),
            jax.ShapeDtypeStruct((half, 2 * hidden), BF16),
            jax.ShapeDtypeStruct((half, 2 * hidden), BF16),
            jax.ShapeDtypeStruct((half, d), BF16),
            jax.ShapeDtypeStruct((8, d), F32),
        ],
        compiler_params=params(),
        cost_estimate=pl.CostEstimate(
            flops=12 * half * d * hidden, bytes_accessed=half * d * 20 + half * hidden * 16 + 12 * d * hidden,
            transcendentals=half,
        ),
        name="ffn_bwd",
    )(info, pa, pb, normed, cot, nb, up0, up1, down0, down1, a_all, b_all)


def attn_bwd_kernel(info, slopes, x_ref, d2_ref, ha, hb, normed_ref, recip_ref, nb, wqkv0, wqkv1, wout0, wout1,
                    proj_all, att_all, lse_all,
                    d1_ref, part, grad0, grad1, sums_ref, dist, sum0, sum1):
    step = pl.program_id(0)
    win = d2_ref.shape[0]
    width = wout0.shape[0]
    heads = width // HEAD_DIM

    @pl.when(step == 0)
    def _():
        fill_distance(dist)

    normed = normed_ref[...]
    dh = d2_ref[...] + (ha[...].astype(F32) + hb[...].astype(F32))
    d1 = norm_grad(dh, normed, recip_ref[:, 0:1], nb[0:1])
    d1_ref[...] = d1
    d1b = d1.astype(BF16)
    x = x_ref[...]
    sums = rows_of_sums([dh * normed, dh, d1])

    @pl.when(step == 0)
    def _():
        sums_ref[...] = sums

    @pl.when(step > 0)
    def _():
        sums_ref[...] += sums

    limit = info[1 + info[0] * pl.num_programs(0) + step]
    lanes = head_lanes(width)
    key_on = lax.broadcasted_iota(jnp.int32, (win, 1), 0) < limit
    stat_lane = lax.broadcasted_iota(jnp.int32, (1, 128), 1)
    total = None
    for g, (wqkv, wout, acc) in enumerate(((wqkv0, wout0, sum0), (wqkv1, wout1, sum1))):
        q, k, v = proj_all[g, 0], proj_all[g, 1], proj_all[g, 2]
        datt = dot_nt(d1b, wout[...]).astype(BF16)
        product = datt.astype(F32) * att_all[g].astype(F32)
        stat = jnp.zeros((win, 128), F32)
        for h in range(heads):
            inner = jnp.sum(jnp.where(lanes[h], product, 0.0), axis=1, keepdims=True)
            stat = jnp.where(stat_lane == h, inner, stat)
        inner_rows = stat.T[0:8]
        qs = q * jnp.asarray(SCALE, BF16)
        dq = jnp.zeros((win, width), F32)
        dk = jnp.zeros((win, width), F32)
        dv = jnp.zeros((win, width), F32)
        for h in range(heads):
            qh = jnp.where(lanes[h], qs, jnp.zeros_like(qs))
            oh = jnp.where(lanes[h], datt, jnp.zeros_like(datt))
            s = dot_nt(k, qh) - slopes[g * heads + h] * dist[...]
            s = jnp.where(key_on, s, NEG)
            p = jnp.exp(s - lse_all[g, 0, h:h + 1, :])
            dp = dot_nt(v, oh)
            ds = (p * (dp - inner_rows[h:h + 1, :])).astype(BF16)
            dv = jnp.where(lanes[h], dot(p.astype(BF16), datt), dv)
            dk = jnp.where(lanes[h], dot(ds, q), dk)
            dq = jnp.where(lanes[h], dot_tn(ds, k), dq)
        dqb = (dq * SCALE).astype(BF16)
        dkb = (dk * SCALE).astype(BF16)
        dvb = dv.astype(BF16)
        terms = [dot_tn(x, dqb), dot_tn(x, dkb), dot_tn(x, dvb), dot_tn(d1b, att_all[g])]

        @pl.when(step == 0)
        def _():
            for i in range(4):
                acc[i] = terms[i]

        @pl.when(step > 0)
        def _():
            for i in range(4):
                acc[i] += terms[i]

        term = dot_nt(dqb, wqkv[0]) + dot_nt(dkb, wqkv[1]) + dot_nt(dvb, wqkv[2])
        total = term if total is None else total + term
    part[...] = total.astype(BF16)

    @pl.when(step == pl.num_programs(0) - 1)
    def _():
        for acc, grad in ((sum0, grad0), (sum1, grad1)):
            for i in range(4):
                grad[:, i * width:(i + 1) * width] = acc[i].astype(BF16)


def attn_bwd(info, slopes, tokens, d2, ha, hb, normed, recip, nb, wqkv0, wqkv1, wout0, wout1,
             proj, att, lse):
    half, d = d2.shape
    width = wout0.shape[0]
    _, nwin, _, win = lse.shape
    heads = 2 * width // HEAD_DIM
    row = lambda w: pl.BlockSpec((win, w), lambda i, *_: (i, 0))
    return pl.pallas_call(
        attn_bwd_kernel,
        grid_spec=pltpu.PrefetchScalarGridSpec(
            num_scalar_prefetch=2,
            grid=(nwin,),
            in_specs=[
                pl.BlockSpec((win, d), lambda i, info, sl: (info[0] * nwin + i, 0)),
                row(d), row(d), row(d), row(d), row(128), whole(nb.shape),
                whole(wqkv0.shape), whole(wqkv1.shape), whole(wout0.shape), whole(wout1.shape),
                pl.BlockSpec((2, 3, win, width), lambda i, *_: (0, 0, i, 0)),
                pl.BlockSpec((2, win, width), lambda i, *_: (0, i, 0)),
                pl.BlockSpec((2, 1, 8, win), lambda i, *_: (0, i, 0, 0)),
            ],
            out_specs=[row(d), row(d), whole((d, 4 * width)), whole((d, 4 * width)), whole((8, d))],
            scratch_shapes=[pltpu.VMEM((win, win), F32), pltpu.VMEM((4, d, width), F32), pltpu.VMEM((4, d, width), F32)],
        ),
        out_shape=[
            jax.ShapeDtypeStruct((half, d), F32),
            jax.ShapeDtypeStruct((half, d), BF16),
            jax.ShapeDtypeStruct((d, 4 * width), BF16),
            jax.ShapeDtypeStruct((d, 4 * width), BF16),
            jax.ShapeDtypeStruct((8, d), F32),
        ],
        compiler_params=params(),
        cost_estimate=pl.CostEstimate(
            flops=2 * half * d * width * 16 + 10 * nwin * heads * win * win * 256,
            bytes_accessed=half * d * 20 + half * width * 32 + d * width * 16,
            transcendentals=nwin * heads * win * win,
        ),
        name="attn_bwd",
    )(info, slopes, tokens, d2, ha, hb, normed, recip, nb, wqkv0, wqkv1, wout0, wout1,
      proj, att, lse)


def place_kernel(order, mine, near, far, out):
    step = pl.program_id(0)

    @pl.when(step < 2)
    def _():
        out[...] = mine[...].astype(out.dtype)

    @pl.when(step == 2)
    def _():
        out[...] = near[...].astype(out.dtype)

    @pl.when(step == 3)
    def _():
        out[...] = far[...].astype(out.dtype)


def place(order, mine, near, far, dtype):
    quarter, d = near.shape
    return pl.pallas_call(
        place_kernel,
        grid_spec=pltpu.PrefetchScalarGridSpec(
            num_scalar_prefetch=1,
            grid=(4,),
            in_specs=[
                pl.BlockSpec((quarter, d), lambda i, o: (jnp.minimum(i, 1), 0)),
                whole((quarter, d)),
                whole((quarter, d)),
            ],
            out_specs=pl.BlockSpec((quarter, d), lambda i, o: (o[i], 0)),
        ),
        out_shape=jax.ShapeDtypeStruct((4 * quarter, d), dtype),
        compiler_params=params(),
        cost_estimate=pl.CostEstimate(flops=0, bytes_accessed=24 * quarter * d, transcendentals=0),
        name="place",
    )(order, mine, near, far)


MESH_ID = pl.DeviceIdType.MESH
TILE = 256


def remote(src, dst, send, recv, axis, peer):
    return pltpu.make_async_remote_copy(src, dst, send, recv, device_id={axis: peer}, device_id_type=MESH_ID)


def forward_kernel(info, slopes, nb, tokens, wqkv, wout, up, down,
                   proj_out, att_out, lse_out, normed_out, recip_out, h_out, a_out, b_out, act_out, fown_out, frecv_out,
                   wqkv1_out, wout1_out, up1_out, down1_out,
                   xbuf, wqv, wov, upv, downv, projb, attb, lseb, pown, precv, normedb, recipb, hbuf, ab, bb, actb,
                   facc, fown, frecv, dist,
                   load_sem, ysend, yrecv, xsend, xrecv, psend, prem, fsend, frem, out_sem, pout_sem, tout_sem, fout_sem):
    x_at, y_at, c_at = (lax.axis_index(n) for n in ("x", "y", "core"))
    nwin, _, win = lse_out.shape[1:]
    half, d = xbuf.shape
    width = wout.shape[0]
    hidden = down.shape[0]
    heads = width // HEAD_DIM
    tiles = half // TILE

    barrier = pltpu.get_barrier_semaphore()
    for axis, at in (("x", x_at), ("y", y_at), ("core", c_at)):
        pl.semaphore_signal(barrier, inc=1, device_id={axis: 1 - at}, device_id_type=MESH_ID)
    pl.semaphore_wait(barrier, 3)

    hd, hw, hf = d // 2, width // 2, hidden // 2

    def pieces(at):
        rows = pl.ds(at * hd, hd)
        return (
            (wqkv.at[0:2, rows], wqv.at[1, 0:2, rows]),
            (wqkv.at[2:3, rows], wqv.at[1, 2:3, rows]),
            (wout.at[pl.ds(at * hw, hw)], wov.at[1, pl.ds(at * hw, hw)]),
            (up.at[at, 0:hd], upv.at[1, at, 0:hd]),
            (up.at[at, hd:d], upv.at[1, at, hd:d]),
            (down.at[pl.ds(at * hf, hf)], downv.at[1, pl.ds(at * hf, hf)]),
        )

    mine = pieces(x_at)
    theirs = pieces(1 - x_at)

    def over_y(i):
        return remote(mine[i][0], mine[i][1], ysend.at[i], yrecv.at[i], "y", 1 - y_at)

    def over_x(i):
        return remote(mine[i][1], mine[i][1], xsend.at[i], xrecv.at[i], "x", 1 - x_at)

    def arriving_x(i):
        return remote(theirs[i][1], theirs[i][1], xsend.at[i], xrecv.at[i], "x", 1 - x_at)

    def pass_on(i):
        over_y(i).wait_recv()
        over_x(i).start()

    loads = [
        pltpu.make_async_copy(tokens.at[pl.ds(y_at * half, half)], xbuf, load_sem.at[0]),
        pltpu.make_async_copy(wqkv, wqv.at[0], load_sem.at[1]),
        pltpu.make_async_copy(wout, wov.at[0], load_sem.at[2]),
        pltpu.make_async_copy(up, upv.at[0], load_sem.at[3]),
        pltpu.make_async_copy(down, downv.at[0], load_sem.at[4]),
    ]
    for i in range(6):
        over_y(i).start()
    for load in loads:
        load.start()
    fill_distance(dist)
    lanes = head_lanes(width)
    stat_lane = lax.broadcasted_iota(jnp.int32, (1, 128), 1)
    key_at = lax.broadcasted_iota(jnp.int32, (1, win), 1)
    for load in loads[:3]:
        load.wait()

    def part_copy(w):
        rows = pl.ds(w * win, win)
        return remote(pown.at[rows], precv.at[rows], psend.at[w], prem.at[w], "core", 1 - c_at)

    def proj_copy(t):
        g, rows = t // nwin, pl.ds((t % nwin) * win, win)
        return (
            pltpu.make_async_copy(projb.at[g, :, rows], proj_out.at[g, :, rows], pout_sem.at[0, t]),
            pltpu.make_async_copy(attb.at[g, rows], att_out.at[g, rows], pout_sem.at[1, t]),
        )

    def attention(t, carry):
        g, w = t // nwin, t % nwin
        start = w * win
        x = xbuf[pl.ds(start, win)]
        q = dot(x, wqv[g, 0]).astype(BF16)
        k = dot(x, wqv[g, 1]).astype(BF16)
        v = dot(x, wqv[g, 2]).astype(BF16)
        projb[g, 0, pl.ds(start, win)] = q
        projb[g, 1, pl.ds(start, win)] = k
        projb[g, 2, pl.ds(start, win)] = v
        key_on = key_at < info[y_at * nwin + w]
        rows = win // 2
        for b in range(2):
            at = slice(b * rows, (b + 1) * rows)
            qb = q[at] * jnp.asarray(SCALE, BF16)
            att = jnp.zeros((rows, width), F32)
            stat = jnp.zeros((rows, 128), F32)
            for h in range(heads):
                qh = jnp.where(lanes[h], qb, jnp.zeros_like(qb))
                s = dot_nt(qh, k) - slopes[g * heads + h] * dist[at]
                s = jnp.where(key_on, s, NEG)
                top = jnp.max(s, axis=1, keepdims=True)
                p = jnp.exp(s - top)
                total = jnp.sum(p, axis=1, keepdims=True)
                o = dot(p.astype(BF16), v) * (1.0 / total)
                att = jnp.where(lanes[h], o, att)
                stat = jnp.where(stat_lane == h, top + jnp.log(total), stat)
            attb[g, pl.ds(start + b * rows, rows)] = att.astype(BF16)
            lseb[g, w, :, at] = stat.T[0:8]
        for copy in proj_copy(t):
            copy.start()

        @pl.when(t >= nwin)
        def _():
            out = dot(attb[0, pl.ds(start, win)], wov[0]) + dot(attb[1, pl.ds(start, win)], wov[1])
            pown[pl.ds(start, win)] = out.astype(BF16)
            part_copy(w).start()

        @pl.when(t == nwin - 2)
        def _():
            pass_on(0)

        @pl.when(t == nwin - 1)
        def _():
            pass_on(1)
            pass_on(2)
            for i in range(3):
                arriving_x(i).wait_recv()

        @pl.when(t == 2 * nwin - 2)
        def _():
            pass_on(3)

        return carry

    lax.fori_loop(0, 2 * nwin, attention, 0)
    lse_copy = pltpu.make_async_copy(lseb, lse_out, out_sem.at[0])
    lse_copy.start()
    loads[3].wait()
    loads[4].wait()
    step = 256

    def hidden_units(g, start, hb):
        for at in range(0, hidden, step):
            cols = slice(at, at + step)
            gate = dot(hb, upv[g, 0, :, cols])
            lift = dot(hb, upv[g, 1, :, cols])
            cdf = 0.5 * (1.0 + lax.erf(gate * (1.0 / math.sqrt(2.0))))
            pdf = jnp.exp(-0.5 * gate * gate) * (1.0 / math.sqrt(2.0 * math.pi))
            gelu = gate * cdf
            rows = pl.ds(start, TILE)
            ab[g, rows, cols] = (lift * (cdf + gate * pdf)).astype(BF16)
            bb[g, rows, cols] = gelu.astype(BF16)
            actb[g, rows, cols] = (gelu * lift).astype(BF16)

    def tile_copies(t):
        g, rows = t // tiles, pl.ds((t % tiles) * TILE, TILE)
        return [
            pltpu.make_async_copy(b.at[g, rows], o.at[g, rows], tout_sem.at[i, t])
            for i, (b, o) in enumerate(((ab, a_out), (bb, b_out), (actb, act_out)))
        ]

    def norm_copies(i):
        rows = pl.ds(i * TILE, TILE)
        return [
            pltpu.make_async_copy(b.at[rows], o.at[rows], fout_sem.at[n, i])
            for n, (b, o) in enumerate(((normedb, normed_out), (recipb, recip_out), (hbuf, h_out)))
        ]

    def first(i, carry):
        start = i * TILE

        @pl.when(i % (win // TILE) == 0)
        def _():
            part_copy(i // (win // TILE)).wait_recv()

        rows = pl.ds(start, TILE)
        value = (pown[rows].astype(F32) + precv[rows].astype(F32)) + nb[2:3] + xbuf[rows].astype(F32)
        normed, recip = standardize(value)
        normedb[rows] = normed
        recipb[rows] = jnp.broadcast_to(recip, (TILE, 128))
        hb = (normed * nb[0:1] + nb[1:2]).astype(BF16)
        hbuf[rows] = hb
        hidden_units(0, start, hb)
        facc[rows] = dot(actb[0, rows], downv[0])
        for copy in tile_copies(i) + norm_copies(i):
            copy.start()

        @pl.when(i == 1)
        def _():
            pass_on(4)

        @pl.when(i == tiles - 1)
        def _():
            pass_on(5)

        return carry

    lax.fori_loop(0, tiles, first, 0)
    arriving_x(3).wait_recv()
    arriving_x(4).wait_recv()

    def second(i, carry):
        start = i * TILE
        hidden_units(1, start, hbuf[pl.ds(start, TILE)])
        for copy in tile_copies(tiles + i):
            copy.start()
        return carry

    lax.fori_loop(0, tiles, second, 0)
    arriving_x(5).wait_recv()

    def final_copy(i):
        rows = pl.ds(i * TILE, TILE)
        return (
            remote(fown.at[rows], frecv.at[rows], fsend.at[i], frem.at[i], "core", 1 - c_at),
            pltpu.make_async_copy(fown.at[rows], fown_out.at[rows], fout_sem.at[3, i]),
        )

    def third(i, carry):
        rows = pl.ds(i * TILE, TILE)
        fown[rows] = (facc[rows] + dot(actb[1, rows], downv[1])).astype(BF16)
        for copy in final_copy(i):
            copy.start()
        return carry

    weights_out = [
        pltpu.make_async_copy(wqv.at[1], wqkv1_out, out_sem.at[1]),
        pltpu.make_async_copy(wov.at[1], wout1_out, out_sem.at[2]),
        pltpu.make_async_copy(upv.at[1], up1_out, out_sem.at[3]),
        pltpu.make_async_copy(downv.at[1], down1_out, out_sem.at[4]),
    ]
    for copy in weights_out:
        copy.start()
    lax.fori_loop(0, tiles, third, 0)

    def finish(i, carry):
        sent, kept = final_copy(i)
        sent.wait_recv()
        back = pltpu.make_async_copy(frecv.at[pl.ds(i * TILE, TILE)], frecv_out.at[pl.ds(i * TILE, TILE)], fout_sem.at[4, i])
        back.start()
        sent.wait_send()
        kept.wait()
        for copy in norm_copies(i):
            copy.wait()
        return carry

    lax.fori_loop(0, tiles, finish, 0)

    def drain(i, carry):
        pltpu.make_async_copy(
            frecv.at[pl.ds(i * TILE, TILE)], frecv_out.at[pl.ds(i * TILE, TILE)], fout_sem.at[4, i]
        ).wait()
        return carry

    lax.fori_loop(0, tiles, drain, 0)

    def drain_tiles(t, carry):
        for copy in tile_copies(t):
            copy.wait()
        return carry

    lax.fori_loop(0, 2 * tiles, drain_tiles, 0)

    def drain_proj(t, carry):
        for copy in proj_copy(t):
            copy.wait()
        return carry

    lax.fori_loop(0, 2 * nwin, drain_proj, 0)

    def drain_part(w, carry):
        part_copy(w).wait_send()
        return carry

    lax.fori_loop(0, nwin, drain_part, 0)
    lse_copy.wait()
    for copy in weights_out:
        copy.wait()
    for i in range(6):
        over_y(i).wait_send()
        over_x(i).wait_send()


def forward(lengths, slopes, nb, tokens, wqkv, wout, up, down):
    d = tokens.shape[1]
    nwin = lengths.shape[0] // 2
    half = tokens.shape[0] // 2
    win = half // nwin
    width, hidden = wout.shape[0], down.shape[0]
    tiles = half // TILE
    heads = width // HEAD_DIM
    smem = pl.BlockSpec(memory_space=pltpu.SMEM)
    vmem = pl.BlockSpec(memory_space=pltpu.VMEM)
    hbm = pl.BlockSpec(memory_space=pl.ANY)
    acts = [((2, half, hidden), BF16)] * 3
    outs = [
        ((2, 3, half, width), BF16), ((2, half, width), BF16), ((2, nwin, 8, win), F32),
        ((half, d), F32), ((half, 128), F32), ((half, d), BF16), *acts,
        ((half, d), BF16), ((half, d), BF16),
        (wqkv.shape, BF16), (wout.shape, BF16), (up.shape, BF16), (down.shape, BF16),
    ]
    bufs = [
        ((half, d), BF16), ((2,) + wqkv.shape, BF16), ((2,) + wout.shape, BF16), ((2,) + up.shape, BF16),
        ((2,) + down.shape, BF16), ((2, 3, half, width), BF16), ((2, half, width), BF16), ((2, nwin, 8, win), F32),
        ((half, d), BF16), ((half, d), BF16), ((half, d), F32), ((half, 128), F32), ((half, d), BF16), *acts,
        ((half, d), F32), ((half, d), BF16), ((half, d), BF16), ((win, win), F32),
    ]
    sems = [(5,), (6,), (6,), (6,), (6,), (nwin,), (nwin,), (tiles,), (tiles,), (5,), (2, 2 * nwin), (3, 2 * tiles), (5, tiles)]
    return pl.pallas_call(
        forward_kernel,
        in_specs=[smem, smem, vmem] + [hbm] * 5,
        out_specs=[hbm] * len(outs),
        out_shape=[jax.ShapeDtypeStruct(*o) for o in outs],
        scratch_shapes=[pltpu.VMEM(*b) for b in bufs] + [pltpu.SemaphoreType.DMA(n) for n in sems],
        compiler_params=pltpu.CompilerParams(vmem_limit_bytes=62 * 1024 * 1024, collective_id=0, has_side_effects=True),
        cost_estimate=pl.CostEstimate(
            flops=2 * half * d * width * 16 + 12 * half * d * hidden + 8 * nwin * heads * win * win * 256,
            bytes_accessed=half * d * 30 + half * hidden * 12, transcendentals=half * hidden * 4,
        ),
        name="forward",
    )(lengths, slopes, nb, tokens, wqkv, wout, up, down)


SWAP = [(0, 1), (1, 0)]
WIDE = ("wo", "x")


def swap(value, axis):
    return lax.ppermute(value, axis, SWAP)


def after(value, *others):
    return lax.optimization_barrier((value, *others))[0]


def shards(tokens, wqkv, wout, nb, up, down, lengths, cot):
    x_at, y_at, c_at = (lax.axis_index(name) for name in ("x", "y", "core"))
    d = tokens.shape[1]
    group_heads = wqkv.shape[2] // HEAD_DIM
    own = 2 * y_at + c_at
    heads = jnp.concatenate([own * group_heads + jnp.arange(group_heads), (own ^ 2) * group_heads + jnp.arange(group_heads)])
    slopes = 2.0 ** (-8.0 * (heads + 1).astype(F32) / HEADS)
    info = jnp.concatenate([y_at[None].astype(jnp.int32), lengths])

    (proj, att, lse, normed, recip, hb, a_all, b_all, act, fpart, fpart_other,
     wqkv1, wout1, up1, down1) = forward(lengths, slopes, nb, tokens, wqkv, wout, up, down)
    act0, act1 = act[0], act[1]
    out, d2, d2b, dgu0, dgu1, dh, sums2 = ffn_bwd(
        info, fpart, fpart_other, normed, cot, nb, up, up1, down, down1, a_all, b_all
    )
    dh_other = swap(dh, "core")

    def grad(a, b):
        return lax.dot_general(a, b, (((0,), (0,)), ((), ())), preferred_element_type=F32).astype(BF16)

    wo = lax.axis_size("wo")

    def part_of(value, at):
        split = value.reshape(wo, 2, -1, value.shape[1])
        return lax.dynamic_index_in_dim(split, at, 1, keepdims=False).reshape(-1, value.shape[1])

    def add(a, b):
        return a.astype(F32) + b.astype(F32)

    down_peer = grad(d2b, act1)
    down_peer_in = swap(down_peer, "y")
    up_peer = grad(hb, dgu1)
    up_own = grad(hb, dgu0)
    up_in = swap(jnp.concatenate([part_of(up_own, 1 - x_at), part_of(up_peer, 1 - x_at)], axis=0), "x")
    down_own = grad(d2b, act0)

    quarter = out.shape[0] // 2
    order = jnp.stack([2 * y_at, 2 * y_at + 1, 2 * (1 - y_at) + c_at, 2 * (1 - y_at) + 1 - c_at]).astype(jnp.int32)

    def mine(value):
        return lax.dynamic_slice_in_dim(value, c_at * quarter, quarter, 0)

    d2 = after(d2, down_own)
    d1, ipart, agrad0, agrad1, sums1 = attn_bwd(
        info, slopes, tokens, d2, dh, dh_other, normed, recip, nb, wqkv, wqkv1, wout, wout1,
        proj, att, lse,
    )
    ipart_other = swap(ipart, "core")
    near_out = swap(mine(out), "y")

    attn_in = swap(jnp.concatenate([part_of(agrad0, 1 - x_at), part_of(agrad1, 1 - x_at)], axis=0), "x")

    total = (d1 + add(ipart, ipart_other)).astype(BF16)
    near_in = swap(mine(total), "y")

    down_all = add(down_own, down_peer_in).astype(BF16)
    down_in = swap(part_of(down_all, 1 - x_at), "x")
    down_half = add(part_of(down_all, x_at), down_in).astype(BF16)
    n = d // 2
    up_peer_half = add(part_of(up_peer, x_at), up_in[n:]).astype(BF16)
    up_half = add(add(part_of(up_own, x_at), up_in[:n]), swap(up_peer_half, "y")).astype(BF16)
    attn_peer_half = add(part_of(agrad1, x_at), attn_in[n:]).astype(BF16)
    attn_half = add(add(part_of(agrad0, x_at), attn_in[:n]), swap(attn_peer_half, "y")).astype(BF16)

    scatter = functools.partial(lax.psum_scatter, axis_name="wo", scatter_dimension=0, tiled=True)
    ffn_share = scatter(jnp.concatenate([down_half, up_half], axis=1)).astype(F32)
    hidden = down.shape[0]
    down_share = ffn_share[:, :hidden].T
    up_share = jnp.stack([ffn_share[:, hidden:2 * hidden], ffn_share[:, 2 * hidden:]])
    attn_share = scatter(attn_half).astype(F32)
    width = wqkv.shape[2]
    qkv_share = jnp.stack([attn_share[:, i * width:(i + 1) * width] for i in range(3)])
    out_share = attn_share[:, 3 * width:].T

    small = jnp.concatenate([sums1[:3], sums2[:3]], axis=0)
    small_share = lax.psum_scatter(lax.psum(small, "y"), WIDE, scatter_dimension=1, tiled=True)

    block_out = place(order, out, near_out, swap(near_out, "core"), BF16)
    input_grad = place(order, total, near_in, swap(near_in, "core"), F32)
    return (block_out, input_grad, qkv_share, out_share, up_share, down_share, small_share)


def solution(mesh):
    wide = mesh.shape["wide"]
    grid = Mesh(mesh.devices.reshape(wide // 2, 2, 2, 2), ("wo", "x", "y", "core"))
    narrow = ("y", "core")
    placed = (
        P(WIDE, None),
        P(None, None, narrow),
        P(narrow, None),
        P(),
        P(None, None, narrow),
        P(narrow, None),
        P(WIDE),
        P(WIDE, None),
    )
    return jax.shard_map(
        shards,
        mesh=grid,
        in_specs=placed,
        out_specs=(
            P(WIDE, None),
            P(WIDE, None),
            P(None, WIDE, narrow),
            P(narrow, WIDE),
            P(None, WIDE, narrow),
            P(narrow, WIDE),
            P(None, WIDE),
        ),
        check_vma=False,
    )
```

```python
import functools
import math

import jax
import jax.numpy as jnp
from jax import lax
from jax.experimental import pallas as pl
from jax.experimental.pallas import tpu as pltpu
from jax.sharding import Mesh, PartitionSpec as P

HEADS = 12
HEAD_DIM = 64
EPS = 1e-05
F32 = jnp.float32
BF16 = jnp.bfloat16
SCALE = 1.0 / math.sqrt(HEAD_DIM)
NEG = -1e30
VMEM_LIMIT = 56 * 1024 * 1024


def dot(a, b):
    return lax.dot_general(a, b, (((1,), (0,)), ((), ())), preferred_element_type=F32)


def dot_nt(a, b):
    return lax.dot_general(a, b, (((1,), (1,)), ((), ())), preferred_element_type=F32)


def dot_tn(a, b):
    return lax.dot_general(a, b, (((0,), (0,)), ((), ())), preferred_element_type=F32)


def whole(shape):
    return pl.BlockSpec(shape, lambda i, *_: (0,) * len(shape))


def head_lanes(width):
    lane = lax.broadcasted_iota(jnp.int32, (1, width), 1)
    return [(lane >= h * HEAD_DIM) & (lane < (h + 1) * HEAD_DIM) for h in range(width // HEAD_DIM)]


def fill_distance(ref):
    n = ref.shape[0]
    row = lax.broadcasted_iota(jnp.int32, (n, n), 0)
    col = lax.broadcasted_iota(jnp.int32, (n, n), 1)
    ref[...] = jnp.abs(row - col).astype(F32)


def params():
    return pltpu.CompilerParams(vmem_limit_bytes=VMEM_LIMIT, dimension_semantics=("arbitrary",))


def standardize(value):
    center = value - jnp.mean(value, axis=1, keepdims=True)
    recip = lax.rsqrt(jnp.mean(center * center, axis=1, keepdims=True) + EPS)
    return center * recip, recip


def norm_grad(grad, normed, recip, gain):
    e = grad * gain
    inner = jnp.mean(e * normed, axis=1, keepdims=True)
    return recip * (e - jnp.mean(e, axis=1, keepdims=True) - normed * inner)


def rows_of_sums(values):
    width = values[0].shape[1]
    sums = [jnp.sum(v, axis=0, keepdims=True) for v in values]
    return jnp.concatenate(sums + [jnp.zeros((8 - len(sums), width), F32)], axis=0)


def ffn_bwd_kernel(info, pa, pb, normed_ref, cot, nb, up0, up1, down0, down1, a_all, b_all,
                   out_ref, d2_ref, d2t_ref, dgu, dh_ref, sums_ref):
    hidden = down0.shape[0]
    h = normed_ref[...] * nb[0:1] + nb[1:2]
    second = pa[...].astype(F32) + pb[...].astype(F32) + nb[5:6] + h
    normed, recip = standardize(second)
    gain = nb[3:4]
    out_ref[...] = (normed * gain + nb[4:5]).astype(BF16)
    c = cot[...].astype(F32)
    d2 = norm_grad(c, normed, recip, gain)
    d2_ref[...] = d2
    d2b = d2.astype(BF16)
    d2t_ref[...] = d2b.T
    sums = rows_of_sums([c * normed, c, d2])

    @pl.when(pl.program_id(0) == 0)
    def _():
        sums_ref[...] = sums

    @pl.when(pl.program_id(0) > 0)
    def _():
        sums_ref[...] += sums

    total = None
    step = 256
    for g, (up, down) in enumerate(((up0, down0), (up1, down1))):
        for at in range(0, hidden, step):
            cols = slice(at, at + step)
            dact = dot_nt(d2b, down[cols, :])
            dgu[g, :, cols] = (dact * a_all[g, :, cols].astype(F32)).astype(BF16)
            dgu[g, :, slice(hidden + at, hidden + at + step)] = (dact * b_all[g, :, cols].astype(F32)).astype(BF16)
        for k in range(2):
            term = dot_nt(dgu[g, :, k * hidden:(k + 1) * hidden], up[k])
            total = term if total is None else total + term
    dh_ref[...] = total.astype(BF16)


def ffn_bwd(info, pa, pb, normed, cot, nb, up0, up1, down0, down1, a_all, b_all, tile=256):
    half, d = pa.shape
    hidden = down0.shape[0]
    n = half // tile
    row = lambda w: pl.BlockSpec((tile, w), lambda i, *_: (i, 0))
    return pl.pallas_call(
        ffn_bwd_kernel,
        grid_spec=pltpu.PrefetchScalarGridSpec(
            num_scalar_prefetch=1,
            grid=(n,),
            in_specs=[
                row(d), row(d), row(d),
                pl.BlockSpec((tile, d), lambda i, info: (info[0] * n + i, 0)),
                whole(nb.shape),
                whole(up0.shape), whole(up1.shape), whole(down0.shape), whole(down1.shape),
                pl.BlockSpec((2, tile, hidden), lambda i, *_: (0, i, 0)),
                pl.BlockSpec((2, tile, hidden), lambda i, *_: (0, i, 0)),
            ],
            out_specs=[
                pl.BlockSpec((tile, d), lambda i, info: (info[0] * n + i, 0)), row(d),
                pl.BlockSpec((d, tile), lambda i, *_: (0, i)),
                pl.BlockSpec((2, tile, 2 * hidden), lambda i, *_: (0, i, 0)), row(d), whole((8, d)),
            ],
        ),
        out_shape=[
            jax.ShapeDtypeStruct((2 * half, d), BF16),
            jax.ShapeDtypeStruct((half, d), F32),
            jax.ShapeDtypeStruct((d, half), BF16),
            jax.ShapeDtypeStruct((2, half, 2 * hidden), BF16),
            jax.ShapeDtypeStruct((half, d), BF16),
            jax.ShapeDtypeStruct((8, d), F32),
        ],
        compiler_params=params(),
        cost_estimate=pl.CostEstimate(
            flops=12 * half * d * hidden, bytes_accessed=half * d * 20 + half * hidden * 16 + 12 * d * hidden,
            transcendentals=half,
        ),
        name="ffn_bwd",
    )(info, pa, pb, normed, cot, nb, up0, up1, down0, down1, a_all, b_all)


def attn_bwd_kernel(info, slopes, x_ref, d2_ref, ha, hb, normed_ref, recip_ref, nb, wqkv0, wqkv1, wout0, wout1,
                    proj_all, att_all, lse_all,
                    d1_ref, part, grad0, grad1, sums_ref, dist, sum0, sum1):
    step = pl.program_id(0)
    win = d2_ref.shape[0]
    width = wout0.shape[0]
    heads = width // HEAD_DIM

    @pl.when(step == 0)
    def _():
        fill_distance(dist)

    normed = normed_ref[...]
    dh = d2_ref[...] + (ha[...].astype(F32) + hb[...].astype(F32))
    d1 = norm_grad(dh, normed, recip_ref[:, 0:1], nb[0:1])
    d1_ref[...] = d1
    d1b = d1.astype(BF16)
    x = x_ref[...]
    sums = rows_of_sums([dh * normed, dh, d1])

    @pl.when(step == 0)
    def _():
        sums_ref[...] = sums

    @pl.when(step > 0)
    def _():
        sums_ref[...] += sums

    limit = info[1 + info[0] * pl.num_programs(0) + step]
    lanes = head_lanes(width)
    key_on = lax.broadcasted_iota(jnp.int32, (win, 1), 0) < limit
    stat_lane = lax.broadcasted_iota(jnp.int32, (1, 128), 1)
    total = None
    for g, (wqkv, wout, acc) in enumerate(((wqkv0, wout0, sum0), (wqkv1, wout1, sum1))):
        q, k, v = proj_all[g, 0], proj_all[g, 1], proj_all[g, 2]
        datt = dot_nt(d1b, wout[...]).astype(BF16)
        product = datt.astype(F32) * att_all[g].astype(F32)
        stat = jnp.zeros((win, 128), F32)
        for h in range(heads):
            inner = jnp.sum(jnp.where(lanes[h], product, 0.0), axis=1, keepdims=True)
            stat = jnp.where(stat_lane == h, inner, stat)
        inner_rows = stat.T[0:8]
        qs = q * jnp.asarray(SCALE, BF16)
        dq = jnp.zeros((win, width), F32)
        dk = jnp.zeros((win, width), F32)
        dv = jnp.zeros((win, width), F32)
        for h in range(heads):
            qh = jnp.where(lanes[h], qs, jnp.zeros_like(qs))
            oh = jnp.where(lanes[h], datt, jnp.zeros_like(datt))
            s = dot_nt(k, qh) - slopes[g * heads + h] * dist[...]
            s = jnp.where(key_on, s, NEG)
            p = jnp.exp(s - lse_all[g, 0, h:h + 1, :])
            dp = dot_nt(v, oh)
            ds = (p * (dp - inner_rows[h:h + 1, :])).astype(BF16)
            dv = jnp.where(lanes[h], dot(p.astype(BF16), datt), dv)
            dk = jnp.where(lanes[h], dot(ds, q), dk)
            dq = jnp.where(lanes[h], dot_tn(ds, k), dq)
        dqb = (dq * SCALE).astype(BF16)
        dkb = (dk * SCALE).astype(BF16)
        dvb = dv.astype(BF16)
        terms = [dot_tn(x, dqb), dot_tn(x, dkb), dot_tn(x, dvb), dot_tn(d1b, att_all[g])]

        @pl.when(step == 0)
        def _():
            for i in range(4):
                acc[i] = terms[i]

        @pl.when(step > 0)
        def _():
            for i in range(4):
                acc[i] += terms[i]

        term = dot_nt(dqb, wqkv[0]) + dot_nt(dkb, wqkv[1]) + dot_nt(dvb, wqkv[2])
        total = term if total is None else total + term
    part[...] = total.astype(BF16)

    @pl.when(step == pl.num_programs(0) - 1)
    def _():
        for acc, grad in ((sum0, grad0), (sum1, grad1)):
            for i in range(4):
                grad[:, i * width:(i + 1) * width] = acc[i].astype(BF16)


def attn_bwd(info, slopes, tokens, d2, ha, hb, normed, recip, nb, wqkv0, wqkv1, wout0, wout1,
             proj, att, lse):
    half, d = d2.shape
    width = wout0.shape[0]
    _, nwin, _, win = lse.shape
    heads = 2 * width // HEAD_DIM
    row = lambda w: pl.BlockSpec((win, w), lambda i, *_: (i, 0))
    return pl.pallas_call(
        attn_bwd_kernel,
        grid_spec=pltpu.PrefetchScalarGridSpec(
            num_scalar_prefetch=2,
            grid=(nwin,),
            in_specs=[
                pl.BlockSpec((win, d), lambda i, info, sl: (info[0] * nwin + i, 0)),
                row(d), row(d), row(d), row(d), row(128), whole(nb.shape),
                whole(wqkv0.shape), whole(wqkv1.shape), whole(wout0.shape), whole(wout1.shape),
                pl.BlockSpec((2, 3, win, width), lambda i, *_: (0, 0, i, 0)),
                pl.BlockSpec((2, win, width), lambda i, *_: (0, i, 0)),
                pl.BlockSpec((2, 1, 8, win), lambda i, *_: (0, i, 0, 0)),
            ],
            out_specs=[row(d), row(d), whole((d, 4 * width)), whole((d, 4 * width)), whole((8, d))],
            scratch_shapes=[pltpu.VMEM((win, win), F32), pltpu.VMEM((4, d, width), F32), pltpu.VMEM((4, d, width), F32)],
        ),
        out_shape=[
            jax.ShapeDtypeStruct((half, d), F32),
            jax.ShapeDtypeStruct((half, d), BF16),
            jax.ShapeDtypeStruct((d, 4 * width), BF16),
            jax.ShapeDtypeStruct((d, 4 * width), BF16),
            jax.ShapeDtypeStruct((8, d), F32),
        ],
        compiler_params=params(),
        cost_estimate=pl.CostEstimate(
            flops=2 * half * d * width * 16 + 10 * nwin * heads * win * win * 256,
            bytes_accessed=half * d * 20 + half * width * 32 + d * width * 16,
            transcendentals=nwin * heads * win * win,
        ),
        name="attn_bwd",
    )(info, slopes, tokens, d2, ha, hb, normed, recip, nb, wqkv0, wqkv1, wout0, wout1,
      proj, att, lse)


def place_kernel(order, mine, near, far, out):
    step = pl.program_id(0)

    @pl.when(step < 2)
    def _():
        out[...] = mine[...].astype(out.dtype)

    @pl.when(step == 2)
    def _():
        out[...] = near[...].astype(out.dtype)

    @pl.when(step == 3)
    def _():
        out[...] = far[...].astype(out.dtype)


def place(order, mine, near, far, dtype):
    quarter, d = near.shape
    return pl.pallas_call(
        place_kernel,
        grid_spec=pltpu.PrefetchScalarGridSpec(
            num_scalar_prefetch=1,
            grid=(4,),
            in_specs=[
                pl.BlockSpec((quarter, d), lambda i, o: (jnp.minimum(i, 1), 0)),
                whole((quarter, d)),
                whole((quarter, d)),
            ],
            out_specs=pl.BlockSpec((quarter, d), lambda i, o: (o[i], 0)),
        ),
        out_shape=jax.ShapeDtypeStruct((4 * quarter, d), dtype),
        compiler_params=params(),
        cost_estimate=pl.CostEstimate(flops=0, bytes_accessed=24 * quarter * d, transcendentals=0),
        name="place",
    )(order, mine, near, far)


MESH_ID = pl.DeviceIdType.MESH
TILE = 256


def remote(src, dst, send, recv, axis, peer):
    return pltpu.make_async_remote_copy(src, dst, send, recv, device_id={axis: peer}, device_id_type=MESH_ID)


def forward_kernel(info, slopes, nb, tokens, wqkv, wout, up, down,
                   proj_out, att_out, lse_out, normed_out, recip_out, ht_out, a_out, b_out, act_out, fown_out, frecv_out,
                   wqkv1_out, wout1_out, up1_out, down1_out,
                   xbuf, wqv, wov, upv, downv, projb, attb, lseb, pown, precv, normedb, recipb, hbuf, htb, ab, bb, actb,
                   facc, fown, frecv, dist,
                   load_sem, ysend, yrecv, xsend, xrecv, psend, prem, fsend, frem, out_sem, pout_sem, tout_sem, fout_sem):
    x_at, y_at, c_at = (lax.axis_index(n) for n in ("x", "y", "core"))
    nwin, _, win = lse_out.shape[1:]
    half, d = xbuf.shape
    width = wout.shape[0]
    hidden = down.shape[0]
    heads = width // HEAD_DIM
    tiles = half // TILE

    barrier = pltpu.get_barrier_semaphore()
    for axis, at in (("x", x_at), ("y", y_at), ("core", c_at)):
        pl.semaphore_signal(barrier, inc=1, device_id={axis: 1 - at}, device_id_type=MESH_ID)
    pl.semaphore_wait(barrier, 3)

    hd, hw, hf = d // 2, width // 2, hidden // 2

    def pieces(at):
        rows = pl.ds(at * hd, hd)
        return (
            (wqkv.at[0:2, rows], wqv.at[1, 0:2, rows]),
            (wqkv.at[2:3, rows], wqv.at[1, 2:3, rows]),
            (wout.at[pl.ds(at * hw, hw)], wov.at[1, pl.ds(at * hw, hw)]),
            (up.at[at, 0:hd], upv.at[1, at, 0:hd]),
            (up.at[at, hd:d], upv.at[1, at, hd:d]),
            (down.at[pl.ds(at * hf, hf)], downv.at[1, pl.ds(at * hf, hf)]),
        )

    mine = pieces(x_at)
    theirs = pieces(1 - x_at)

    def over_y(i):
        return remote(mine[i][0], mine[i][1], ysend.at[i], yrecv.at[i], "y", 1 - y_at)

    def over_x(i):
        return remote(mine[i][1], mine[i][1], xsend.at[i], xrecv.at[i], "x", 1 - x_at)

    def arriving_x(i):
        return remote(theirs[i][1], theirs[i][1], xsend.at[i], xrecv.at[i], "x", 1 - x_at)

    def pass_on(i):
        over_y(i).wait_recv()
        over_x(i).start()

    loads = [
        pltpu.make_async_copy(tokens.at[pl.ds(y_at * half, half)], xbuf, load_sem.at[0]),
        pltpu.make_async_copy(wqkv, wqv.at[0], load_sem.at[1]),
        pltpu.make_async_copy(wout, wov.at[0], load_sem.at[2]),
        pltpu.make_async_copy(up, upv.at[0], load_sem.at[3]),
        pltpu.make_async_copy(down, downv.at[0], load_sem.at[4]),
    ]
    for i in range(6):
        over_y(i).start()
    for load in loads:
        load.start()
    fill_distance(dist)
    lanes = head_lanes(width)
    stat_lane = lax.broadcasted_iota(jnp.int32, (1, 128), 1)
    key_at = lax.broadcasted_iota(jnp.int32, (1, win), 1)
    for load in loads[:3]:
        load.wait()

    def part_copy(w):
        rows = pl.ds(w * win, win)
        return remote(pown.at[rows], precv.at[rows], psend.at[w], prem.at[w], "core", 1 - c_at)

    def proj_copy(t):
        g, rows = t // nwin, pl.ds((t % nwin) * win, win)
        return (
            pltpu.make_async_copy(projb.at[g, :, rows], proj_out.at[g, :, rows], pout_sem.at[0, t]),
            pltpu.make_async_copy(attb.at[g, rows], att_out.at[g, rows], pout_sem.at[1, t]),
        )

    def attention(t, carry):
        g, w = t // nwin, t % nwin
        start = w * win
        x = xbuf[pl.ds(start, win)]
        q = dot(x, wqv[g, 0]).astype(BF16)
        k = dot(x, wqv[g, 1]).astype(BF16)
        v = dot(x, wqv[g, 2]).astype(BF16)
        projb[g, 0, pl.ds(start, win)] = q
        projb[g, 1, pl.ds(start, win)] = k
        projb[g, 2, pl.ds(start, win)] = v
        key_on = key_at < info[y_at * nwin + w]
        rows = win // 2
        for b in range(2):
            at = slice(b * rows, (b + 1) * rows)
            qb = q[at] * jnp.asarray(SCALE, BF16)
            att = jnp.zeros((rows, width), F32)
            stat = jnp.zeros((rows, 128), F32)
            for h in range(heads):
                qh = jnp.where(lanes[h], qb, jnp.zeros_like(qb))
                s = dot_nt(qh, k) - slopes[g * heads + h] * dist[at]
                s = jnp.where(key_on, s, NEG)
                top = jnp.max(s, axis=1, keepdims=True)
                p = jnp.exp(s - top)
                total = jnp.sum(p, axis=1, keepdims=True)
                o = dot(p.astype(BF16), v) * (1.0 / total)
                att = jnp.where(lanes[h], o, att)
                stat = jnp.where(stat_lane == h, top + jnp.log(total), stat)
            attb[g, pl.ds(start + b * rows, rows)] = att.astype(BF16)
            lseb[g, w, :, at] = stat.T[0:8]
        for copy in proj_copy(t):
            copy.start()

        @pl.when(t >= nwin)
        def _():
            out = dot(attb[0, pl.ds(start, win)], wov[0]) + dot(attb[1, pl.ds(start, win)], wov[1])
            pown[pl.ds(start, win)] = out.astype(BF16)
            part_copy(w).start()

        @pl.when(t == nwin - 2)
        def _():
            pass_on(0)

        @pl.when(t == nwin - 1)
        def _():
            pass_on(1)
            pass_on(2)
            for i in range(3):
                arriving_x(i).wait_recv()

        @pl.when(t == 2 * nwin - 2)
        def _():
            pass_on(3)

        return carry

    lax.fori_loop(0, 2 * nwin, attention, 0)
    lse_copy = pltpu.make_async_copy(lseb, lse_out, out_sem.at[0])
    lse_copy.start()
    loads[3].wait()
    loads[4].wait()
    step = 256

    def hidden_units(g, start, hb):
        for at in range(0, hidden, step):
            cols = slice(at, at + step)
            gate = dot(hb, upv[g, 0, :, cols])
            lift = dot(hb, upv[g, 1, :, cols])
            cdf = 0.5 * (1.0 + lax.erf(gate * (1.0 / math.sqrt(2.0))))
            pdf = jnp.exp(-0.5 * gate * gate) * (1.0 / math.sqrt(2.0 * math.pi))
            gelu = gate * cdf
            rows = pl.ds(start, TILE)
            ab[g, rows, cols] = (lift * (cdf + gate * pdf)).astype(BF16)
            bb[g, rows, cols] = gelu.astype(BF16)
            actb[g, rows, cols] = (gelu * lift).astype(BF16)

    def tile_copies(t):
        g, rows = t // tiles, pl.ds((t % tiles) * TILE, TILE)
        return [
            pltpu.make_async_copy(b.at[g, rows], o.at[g, rows], tout_sem.at[i, t])
            for i, (b, o) in enumerate(((ab, a_out), (bb, b_out), (actb, act_out)))
        ]

    def norm_copies(i):
        rows = pl.ds(pl.multiple_of(i * TILE, TILE), TILE)
        return [
            pltpu.make_async_copy(b.at[rows], o.at[rows], fout_sem.at[n, i])
            for n, (b, o) in enumerate(((normedb, normed_out), (recipb, recip_out)))
        ] + [pltpu.make_async_copy(htb.at[:, rows], ht_out.at[:, rows], fout_sem.at[2, i])]

    def first(i, carry):
        start = i * TILE

        @pl.when(i % (win // TILE) == 0)
        def _():
            part_copy(i // (win // TILE)).wait_recv()

        rows = pl.ds(start, TILE)
        value = (pown[rows].astype(F32) + precv[rows].astype(F32)) + nb[2:3] + xbuf[rows].astype(F32)
        normed, recip = standardize(value)
        normedb[rows] = normed
        recipb[rows] = jnp.broadcast_to(recip, (TILE, 128))
        hb = (normed * nb[0:1] + nb[1:2]).astype(BF16)
        hbuf[rows] = hb
        htb[:, pl.ds(pl.multiple_of(start, TILE), TILE)] = hb.T
        hidden_units(0, start, hb)
        facc[rows] = dot(actb[0, rows], downv[0])
        for copy in tile_copies(i) + norm_copies(i):
            copy.start()

        @pl.when(i == 1)
        def _():
            pass_on(4)

        @pl.when(i == tiles - 1)
        def _():
            pass_on(5)

        return carry

    lax.fori_loop(0, tiles, first, 0)
    arriving_x(3).wait_recv()
    arriving_x(4).wait_recv()

    def second(i, carry):
        start = i * TILE
        hidden_units(1, start, hbuf[pl.ds(start, TILE)])
        for copy in tile_copies(tiles + i):
            copy.start()
        return carry

    lax.fori_loop(0, tiles, second, 0)
    arriving_x(5).wait_recv()

    def final_copy(i):
        rows = pl.ds(i * TILE, TILE)
        return (
            remote(fown.at[rows], frecv.at[rows], fsend.at[i], frem.at[i], "core", 1 - c_at),
            pltpu.make_async_copy(fown.at[rows], fown_out.at[rows], fout_sem.at[3, i]),
        )

    def third(i, carry):
        rows = pl.ds(i * TILE, TILE)
        fown[rows] = (facc[rows] + dot(actb[1, rows], downv[1])).astype(BF16)
        for copy in final_copy(i):
            copy.start()
        return carry

    weights_out = [
        pltpu.make_async_copy(wqv.at[1], wqkv1_out, out_sem.at[1]),
        pltpu.make_async_copy(wov.at[1], wout1_out, out_sem.at[2]),
        pltpu.make_async_copy(upv.at[1], up1_out, out_sem.at[3]),
        pltpu.make_async_copy(downv.at[1], down1_out, out_sem.at[4]),
    ]
    for copy in weights_out:
        copy.start()
    lax.fori_loop(0, tiles, third, 0)

    def finish(i, carry):
        sent, kept = final_copy(i)
        sent.wait_recv()
        back = pltpu.make_async_copy(frecv.at[pl.ds(i * TILE, TILE)], frecv_out.at[pl.ds(i * TILE, TILE)], fout_sem.at[4, i])
        back.start()
        sent.wait_send()
        kept.wait()
        for copy in norm_copies(i):
            copy.wait()
        return carry

    lax.fori_loop(0, tiles, finish, 0)

    def drain(i, carry):
        pltpu.make_async_copy(
            frecv.at[pl.ds(i * TILE, TILE)], frecv_out.at[pl.ds(i * TILE, TILE)], fout_sem.at[4, i]
        ).wait()
        return carry

    lax.fori_loop(0, tiles, drain, 0)

    def drain_tiles(t, carry):
        for copy in tile_copies(t):
            copy.wait()
        return carry

    lax.fori_loop(0, 2 * tiles, drain_tiles, 0)

    def drain_proj(t, carry):
        for copy in proj_copy(t):
            copy.wait()
        return carry

    lax.fori_loop(0, 2 * nwin, drain_proj, 0)

    def drain_part(w, carry):
        part_copy(w).wait_send()
        return carry

    lax.fori_loop(0, nwin, drain_part, 0)
    lse_copy.wait()
    for copy in weights_out:
        copy.wait()
    for i in range(6):
        over_y(i).wait_send()
        over_x(i).wait_send()


def forward(lengths, slopes, nb, tokens, wqkv, wout, up, down):
    d = tokens.shape[1]
    nwin = lengths.shape[0] // 2
    half = tokens.shape[0] // 2
    win = half // nwin
    width, hidden = wout.shape[0], down.shape[0]
    tiles = half // TILE
    heads = width // HEAD_DIM
    smem = pl.BlockSpec(memory_space=pltpu.SMEM)
    vmem = pl.BlockSpec(memory_space=pltpu.VMEM)
    hbm = pl.BlockSpec(memory_space=pl.ANY)
    acts = [((2, half, hidden), BF16)] * 3
    outs = [
        ((2, 3, half, width), BF16), ((2, half, width), BF16), ((2, nwin, 8, win), F32),
        ((half, d), F32), ((half, 128), F32), ((d, half), BF16), *acts,
        ((half, d), BF16), ((half, d), BF16),
        (wqkv.shape, BF16), (wout.shape, BF16), (up.shape, BF16), (down.shape, BF16),
    ]
    bufs = [
        ((half, d), BF16), ((2,) + wqkv.shape, BF16), ((2,) + wout.shape, BF16), ((2,) + up.shape, BF16),
        ((2,) + down.shape, BF16), ((2, 3, half, width), BF16), ((2, half, width), BF16), ((2, nwin, 8, win), F32),
        ((half, d), BF16), ((half, d), BF16), ((half, d), F32), ((half, 128), F32), ((half, d), BF16), ((d, half), BF16), *acts,
        ((half, d), F32), ((half, d), BF16), ((half, d), BF16), ((win, win), F32),
    ]
    sems = [(5,), (6,), (6,), (6,), (6,), (nwin,), (nwin,), (tiles,), (tiles,), (5,), (2, 2 * nwin), (3, 2 * tiles), (5, tiles)]
    return pl.pallas_call(
        forward_kernel,
        in_specs=[smem, smem, vmem] + [hbm] * 5,
        out_specs=[hbm] * len(outs),
        out_shape=[jax.ShapeDtypeStruct(*o) for o in outs],
        scratch_shapes=[pltpu.VMEM(*b) for b in bufs] + [pltpu.SemaphoreType.DMA(n) for n in sems],
        compiler_params=pltpu.CompilerParams(vmem_limit_bytes=62 * 1024 * 1024, collective_id=0, has_side_effects=True),
        cost_estimate=pl.CostEstimate(
            flops=2 * half * d * width * 16 + 12 * half * d * hidden + 8 * nwin * heads * win * win * 256,
            bytes_accessed=half * d * 30 + half * hidden * 12, transcendentals=half * hidden * 4,
        ),
        name="forward",
    )(lengths, slopes, nb, tokens, wqkv, wout, up, down)


BLOCK = 256
FLIGHT = 4


def backward_kernel(lengths, slopes, nb, sums2, tokens, d2_in, dh_in, normed_in, recip_in, wqkv, wqkv1, wout, wout1,
                    proj_in, att_in, lse_in, dgu_in, act_in, ht_in, d2t_in, half_in,
                    share, total_sums, block_out, input_grad,
                    gbuf, r1, r2, zr, dhr, dhw, normw, d2w, recw, xw, projw, attw, lsev, wqv, wov, ipown, iprecv, totb,
                    sumb, sumr, sumz, sum1,
                    g1s, g1r, g2s, g2r, zs, zrs, pre_sem, win_sem, w_sem, dh_s, dh_r, ip_s, ip_r,
                    tot_sem, iy_s, iy_r, ic_s, ic_r, bo_s, bo_r, sm_s, sm_r, smz_s, smz_r, ring_sem, t_sem):
    at = {n: lax.axis_index(n) for n in ("wo", "x", "y", "core")}
    wo_at, x_at, y_at, c_at = at["wo"], at["x"], at["y"], at["core"]
    n_wo = gbuf.shape[3]
    blocks = gbuf.shape[0]
    own_rows = gbuf.shape[4]
    half, d = normed_in.shape
    _, nwin, _, win = lse_in.shape
    width = wout.shape[0]
    hidden = act_in.shape[2]
    heads = width // HEAD_DIM
    ffn_blocks = 3 * hidden // BLOCK

    barrier = pltpu.get_barrier_semaphore()
    for axis in ("x", "y", "core"):
        pl.semaphore_signal(barrier, inc=1, device_id={axis: 1 - at[axis]}, device_id_type=MESH_ID)
    for k in range(n_wo - 1):
        pl.semaphore_signal(barrier, inc=1, device_id={"wo": (wo_at + k + 1) % n_wo}, device_id_type=MESH_ID)
    pl.semaphore_wait(barrier, n_wo + 2)

    def copy_one(b, is_y):
        send = 1 if is_y else 1 - x_at
        axis = "y" if is_y else "x"
        return remote(gbuf.at[b, send], r1.at[b], g1s.at[b], g1r.at[b], axis, 1 - at[axis])

    def copy_two(b, is_y):
        keep = 0 if is_y else x_at
        send = 1 - x_at if is_y else 1
        axis = "x" if is_y else "y"
        return remote(gbuf.at[b, keep, send], r2.at[b], g2s.at[b], g2r.at[b], axis, 1 - at[axis])

    def copy_z(b, is_y, k):
        keep = 0 if is_y else x_at
        keep2 = x_at if is_y else 0
        to = (wo_at + k + 1) % n_wo
        return remote(gbuf.at[b, keep, keep2, to], zr.at[b, k], zs.at[b, k], zrs.at[b, k], "wo", to)

    def by_kind(b, f):
        @pl.when(b % 4 == 1)
        def _():
            f(True)

        @pl.when(b % 4 != 1)
        def _():
            f(False)

    def stage_one(b):
        copy_one(b, False).wait_recv()

        def go(is_y):
            keep = 0 if is_y else x_at
            gbuf[b, keep] = (gbuf[b, keep].astype(F32) + r1[b].astype(F32)).astype(BF16)
            copy_two(b, is_y).start()

        by_kind(b, go)

        @pl.when((b + FLIGHT < blocks) & ((b + FLIGHT < ffn_blocks) | (b >= 2 * nwin)))
        def _():
            by_kind(b + FLIGHT, lambda is_y: copy_one(b + FLIGHT, is_y).start())

    def stage_two(b):
        copy_two(b, False).wait_recv()

        def go(is_y):
            keep = 0 if is_y else x_at
            keep2 = x_at if is_y else 0
            gbuf[b, keep, keep2] = (gbuf[b, keep, keep2].astype(F32) + r2[b].astype(F32)).astype(BF16)
            for k in range(n_wo - 1):
                copy_z(b, is_y, k).start()

        by_kind(b, go)

    def stage_three(b):
        for k in range(n_wo - 1):
            copy_z(b, False, k).wait_recv()

        def go(is_y):
            keep = 0 if is_y else x_at
            keep2 = x_at if is_y else 0
            total = gbuf[b, keep, keep2, wo_at].astype(F32)
            for k in range(n_wo - 1):
                total = total + zr[b, k].astype(F32)
            share[b] = total

        by_kind(b, go)

    def advance(j):
        @pl.when(j < blocks)
        def _():
            stage_one(j)

        @pl.when((j >= 1) & (j < blocks + 1))
        def _():
            stage_two(j - 1)

        @pl.when((j >= 2) & (j < blocks + 2))
        def _():
            stage_three(j - 2)

    def put(b, g, value):
        for j in range(2 * n_wo):
            rows = value[j * own_rows:(j + 1) * own_rows].astype(BF16)
            px, w = j % 2, j // 2

            @pl.when(b % 4 == 1)
            def _():
                gbuf[b, g, px, w] = rows

            @pl.when(b % 4 != 1)
            def _():
                gbuf[b, px, g, w] = rows

    def pre_loads(w):
        rows = pl.ds(w * win, win)
        return [
            pltpu.make_async_copy(src, dst, pre_sem.at[i])
            for i, (src, dst) in enumerate((
                (normed_in.at[rows], normw), (d2_in.at[rows], d2w), (recip_in.at[rows], recw), (dh_in.at[rows], dhw),
                (tokens.at[pl.ds(y_at * half + w * win, win)], xw),
            ))
        ]

    def win_loads(w):
        rows, slot = pl.ds(w * win, win), w % 2
        return [
            pltpu.make_async_copy(proj_in.at[:, :, rows], projw.at[slot], win_sem.at[0, slot]),
            pltpu.make_async_copy(att_in.at[:, rows], attw.at[slot], win_sem.at[1, slot]),
        ]

    dh_copy = remote(dh_in, dhr, dh_s.at[0], dh_r.at[0], "core", 1 - c_at)
    quarter = half // 2
    near = pl.ds(y_at * half + c_at * quarter, quarter)
    near_in = pl.ds((1 - y_at) * half + c_at * quarter, quarter)
    out_y = remote(block_out.at[near], block_out.at[near], bo_s.at[0], bo_r.at[0], "y", 1 - y_at)
    out_c = remote(block_out.at[near_in], block_out.at[near_in], bo_s.at[1], bo_r.at[1], "core", 1 - c_at)

    loads = [
        pltpu.make_async_copy(src, dst, w_sem.at[i])
        for i, (src, dst) in enumerate((
            (wqkv, wqv.at[0]), (wqkv1, wqv.at[1]), (wout, wov.at[0]), (wout1, wov.at[1]), (lse_in, lsev),
        ))
    ]

    def ffn_grads(ring, lhs_d, lhs_h):
        lhs = [pltpu.make_async_copy(d2t_in, lhs_d, t_sem.at[0]), pltpu.make_async_copy(ht_in, lhs_h, t_sem.at[1])]
        down_blocks = hidden // BLOCK
        up_blocks = 2 * hidden // BLOCK

        def fetch(src, b, g):
            return pltpu.make_async_copy(src.at[g, :, pl.ds(pl.multiple_of(b * BLOCK, BLOCK), BLOCK)],
                                         ring.at[b % 2, g], ring_sem.at[b % 2, g])

        def run(src, left, count, first):
            for g in range(2):
                fetch(src, 0, g).start()

            def one(b, carry):
                @pl.when(b + 1 < count)
                def _():
                    for g in range(2):
                        fetch(src, b + 1, g).start()

                for g in range(2):
                    fetch(src, b, g).wait()
                    put(b + first, g, dot(left[...], ring[b % 2, g]))

                @pl.when(b + first < FLIGHT)
                def _():
                    by_kind(b + first, lambda is_y: copy_one(b + first, is_y).start())

                return carry

            lax.fori_loop(0, count, one, 0)

        lhs[0].start()
        dh_copy.start()
        out_y.start()
        lhs[1].start()
        for copy in loads + pre_loads(0) + win_loads(0):
            copy.start()
        lhs[0].wait()
        run(act_in, lhs_d, down_blocks, 0)
        lhs[1].wait()
        run(dgu_in, lhs_h, up_blocks, down_blocks)

    pl.run_scoped(ffn_grads, pltpu.VMEM((2, 2, half, BLOCK), BF16), pltpu.VMEM((d, half), BF16), pltpu.VMEM((d, half), BF16))

    for load in loads:
        load.wait()
    dh_copy.wait_recv()
    lanes = head_lanes(width)
    stat_lane = lax.broadcasted_iota(jnp.int32, (1, 128), 1)

    def part_copy(w):
        return remote(ipown.at[w], iprecv.at[w], ip_s.at[w], ip_r.at[w], "core", 1 - c_at)

    side = win // 2

    def own_copy(w):
        return pltpu.make_async_copy(totb.at[w], input_grad.at[pl.ds(y_at * half + w * win, win)], tot_sem.at[w])

    def in_y(w):
        return remote(totb.at[w, pl.ds(c_at * side, side)], input_grad.at[pl.ds(y_at * half + w * win + c_at * side, side)],
                      iy_s.at[w], iy_r.at[w], "y", 1 - y_at)

    def in_c(w):
        rows = pl.ds((1 - y_at) * half + w * win + c_at * side, side)
        return remote(input_grad.at[rows], input_grad.at[rows], ic_s.at[w], ic_r.at[w], "core", 1 - c_at)

    def attention(acc, xt, d1t, d1b, d1w, iptot, dist, stage):
        fill_distance(dist)
        acc[...] = jnp.zeros_like(acc)
        sum1[...] = jnp.zeros_like(sum1)

        def send_total(w):
            part_copy(w).wait_recv()
            value = d1w[w % 2] + (ipown[w].astype(F32) + iprecv[w].astype(F32))
            totb[w] = value.astype(BF16)
            own_copy(w).start()
            in_y(w).start()

        def step(t, carry):
            w, g = t // 2, t % 2
            slot = w % 2

            @pl.when(g == 0)
            def _():
                for copy in pre_loads(w) + win_loads(w):
                    copy.wait()
                normed = normw[...]
                dh = d2w[...] + (dhw[...].astype(F32) + dhr[pl.ds(w * win, win)].astype(F32))
                d1 = norm_grad(dh, normed, recw[:, 0:1], nb[0:1])
                d1w[slot] = d1
                low = d1.astype(BF16)
                d1b[...] = low
                d1t[...] = low.T
                xt[...] = xw[...].T
                sum1[...] += rows_of_sums([dh * normed, dh, d1])

                @pl.when(w + 1 < nwin)
                def _():
                    for copy in pre_loads(w + 1) + win_loads(w + 1):
                        copy.start()

            q, k, v = projw[slot, g, 0], projw[slot, g, 1], projw[slot, g, 2]
            att = attw[slot, g]
            datt = dot_nt(d1b[...], wov[g]).astype(BF16)
            product = datt.astype(F32) * att.astype(F32)
            stat = jnp.zeros((win, 128), F32)
            for h in range(heads):
                inner = jnp.sum(jnp.where(lanes[h], product, 0.0), axis=1, keepdims=True)
                stat = jnp.where(stat_lane == h, inner, stat)
            inner_rows = stat.T[0:8]
            qs = q * jnp.asarray(SCALE, BF16)
            dq = jnp.zeros((win, width), F32)
            dks, dvs = [], []
            half_keys = win // 2
            limit = lengths[y_at * nwin + w]
            for kb in range(2):
                keys = slice(kb * half_keys, (kb + 1) * half_keys)
                kk, vk = k[keys], v[keys]
                key_on = lax.broadcasted_iota(jnp.int32, (half_keys, 1), 0) + kb * half_keys < limit
                dk = jnp.zeros((half_keys, width), F32)
                dv = jnp.zeros((half_keys, width), F32)
                for h in range(heads):
                    qh = jnp.where(lanes[h], qs, jnp.zeros_like(qs))
                    oh = jnp.where(lanes[h], datt, jnp.zeros_like(datt))
                    s = dot_nt(kk, qh) - slopes[g * heads + h] * dist[keys]
                    s = jnp.where(key_on, s, NEG)
                    p = jnp.exp(s - lsev[g, w, h:h + 1, :])
                    dp = dot_nt(vk, oh)
                    ds = (p * (dp - inner_rows[h:h + 1, :])).astype(BF16)
                    dv = jnp.where(lanes[h], dot(p.astype(BF16), datt), dv)
                    dk = jnp.where(lanes[h], dot(ds, q), dk)
                    dq = dq + jnp.where(lanes[h], dot_tn(ds, kk), 0.0)
                dks.append((dk * SCALE).astype(BF16))
                dvs.append(dv.astype(BF16))
            dqb = (dq * SCALE).astype(BF16)
            dkb = jnp.concatenate(dks, axis=0)
            dvb = jnp.concatenate(dvs, axis=0)
            acc[g, 0] += dot(xt[...], dqb)
            acc[g, 1] += dot(xt[...], dkb)
            acc[g, 2] += dot(xt[...], dvb)
            acc[g, 3] += dot(d1t[...], att)
            term = dot_nt(dqb, wqv[g, 0]) + dot_nt(dkb, wqv[g, 1]) + dot_nt(dvb, wqv[g, 2])

            @pl.when(g == 0)
            def _():
                iptot[...] = term

            @pl.when(g == 1)
            def _():
                ipown[w] = (iptot[...] + term).astype(BF16)
                part_copy(w).start()

            @pl.when((g == 0) & (w > 0))
            def _():
                send_total(w - 1)

            advance(t)

            @pl.when(t == 3)
            def _():
                out_y.wait_recv()
                out_c.start()

            return carry

        lax.fori_loop(0, 2 * nwin, step, 0)

        first = blocks - 4 * width // BLOCK
        for g in range(2):
            for i in range(4):
                stage[:, i * width:(i + 1) * width] = acc[g, i].astype(BF16)
            for i in range(4 * width // BLOCK):
                put(first + i, g, stage[:, i * BLOCK:(i + 1) * BLOCK])
        for i in range(first, min(2 * nwin + FLIGHT, blocks)):
            copy_one(i, i % 4 == 1).start()
        send_total(nwin - 1)

    pl.run_scoped(
        attention,
        pltpu.VMEM((2, 4, d, width), F32), pltpu.VMEM((d, win), BF16), pltpu.VMEM((d, win), BF16), pltpu.VMEM((win, d), BF16),
        pltpu.VMEM((2, win, d), F32), pltpu.VMEM((win, d), F32), pltpu.VMEM((win, win), F32), pltpu.VMEM((d, 4 * width), BF16),
    )

    sumb[0] = jnp.concatenate([sum1[0:3], sums2[0:3], jnp.zeros((2, d), F32)], axis=0)

    def sum_copy(i, axis):
        return remote(sumb.at[i], sumr.at[i], sm_s.at[i], sm_r.at[i], axis, 1 - at[axis])

    def sum_z(k):
        to = (wo_at + k + 1) % n_wo
        return remote(sumb.at[2], sumz.at[k], smz_s.at[k], smz_r.at[k], "wo", to)

    sum_copy(0, "y").start()

    def tail(i, carry):
        j = 2 * nwin + i
        advance(j)

        @pl.when(i < nwin)
        def _():
            in_y(i).wait_recv()
            in_c(i).start()

        @pl.when(i == 0)
        def _():
            sum_copy(0, "y").wait_recv()
            sumb[1] = sumb[0] + sumr[0]
            sum_copy(1, "x").start()

        @pl.when(i == 1)
        def _():
            sum_copy(1, "x").wait_recv()
            sumb[2] = sumb[1] + sumr[1]
            for k in range(n_wo - 1):
                sum_z(k).start()

        return carry

    lax.fori_loop(0, blocks + 2 - 2 * nwin, tail, 0)
    total = sumb[2]
    for k in range(n_wo - 1):
        sum_z(k).wait_recv()
        total = total + sumz[k]
    total_sums[...] = total

    out_c.wait_recv()
    out_y.wait_send()
    out_c.wait_send()
    dh_copy.wait_send()
    for i, axis in ((0, "y"), (1, "x")):
        sum_copy(i, axis).wait_send()
    for k in range(n_wo - 1):
        sum_z(k).wait_send()

    def drain_window(w, carry):
        part_copy(w).wait_send()
        own_copy(w).wait()
        in_y(w).wait_send()
        in_c(w).wait_send()
        in_c(w).wait_recv()
        return carry

    lax.fori_loop(0, nwin, drain_window, 0)

    def drain_block(b, carry):
        copy_one(b, False).wait_send()
        copy_two(b, False).wait_send()
        for k in range(n_wo - 1):
            copy_z(b, False, k).wait_send()
        return carry

    lax.fori_loop(0, blocks, drain_block, 0)


def backward(n_wo, lengths, slopes, nb, sums2, tokens, d2, dh, normed, recip, wqkv, wqkv1, wout, wout1,
             proj, att, lse, dgu, act, ht, d2t, half_out):
    half, d = normed.shape
    _, nwin, _, win = lse.shape
    width, hidden = wout.shape[0], act.shape[2]
    rows = d // (2 * n_wo)
    blocks = (3 * hidden + 4 * width) // BLOCK
    heads = width // HEAD_DIM
    smem = pl.BlockSpec(memory_space=pltpu.SMEM)
    vmem = pl.BlockSpec(memory_space=pltpu.VMEM)
    hbm = pl.BlockSpec(memory_space=pl.ANY)
    outs = [((blocks, rows, BLOCK), F32), ((8, d), F32), (tokens.shape, BF16), (tokens.shape, BF16)]
    bufs = [
        ((blocks, 2, 2, n_wo, rows, BLOCK), BF16), ((blocks, 2, n_wo, rows, BLOCK), BF16), ((blocks, n_wo, rows, BLOCK), BF16),
        ((blocks, n_wo - 1, rows, BLOCK), BF16), ((half, d), BF16), ((win, d), BF16), ((win, d), F32), ((win, d), F32),
        ((win, 128), F32), ((win, d), BF16), ((2, 2, 3, win, width), BF16), ((2, 2, win, width), BF16), (lse.shape, F32),
        ((2,) + wqkv.shape, BF16), ((2,) + wout.shape, BF16), ((nwin, win, d), BF16), ((nwin, win, d), BF16),
        ((nwin, win, d), BF16), ((3, 8, d), F32), ((2, 8, d), F32), ((n_wo - 1, 8, d), F32), ((8, d), F32),
    ]
    sems = [(blocks,)] * 4 + [(blocks, n_wo - 1)] * 2 + [(5,), (2, 2), (5,), (1,), (1,)] + [(nwin,)] * 7
    sems += [(2,), (2,), (2,), (2,), (n_wo - 1,), (n_wo - 1,), (2, 2), (2,)]
    return pl.pallas_call(
        backward_kernel,
        in_specs=[smem, smem, vmem, vmem] + [hbm] * 17,
        out_specs=[vmem, vmem, hbm, hbm],
        input_output_aliases={20: 2},
        out_shape=[jax.ShapeDtypeStruct(*o) for o in outs],
        scratch_shapes=[pltpu.VMEM(*b) for b in bufs] + [pltpu.SemaphoreType.DMA(n) for n in sems],
        compiler_params=pltpu.CompilerParams(vmem_limit_bytes=63 * 1024 * 1024, collective_id=1, has_side_effects=True),
        cost_estimate=pl.CostEstimate(
            flops=2 * half * d * width * 16 + 12 * half * d * hidden + 20 * nwin * heads * win * win * 256,
            bytes_accessed=half * d * 60 + half * hidden * 12, transcendentals=2 * nwin * heads * win * win,
        ),
        name="backward",
    )(lengths, slopes, nb, sums2, tokens, d2, dh, normed, recip, wqkv, wqkv1, wout, wout1,
      proj, att, lse, dgu, act, ht, d2t, half_out)


SWAP = [(0, 1), (1, 0)]
WIDE = ("wo", "x")


def swap(value, axis):
    return lax.ppermute(value, axis, SWAP)


def after(value, *others):
    return lax.optimization_barrier((value, *others))[0]


def weight_shares(columns, hidden, width):
    down_share = columns[:, :hidden].T
    up_share = jnp.stack([columns[:, hidden:2 * hidden], columns[:, 2 * hidden:3 * hidden]])
    start = 3 * hidden
    qkv_share = jnp.stack([columns[:, start + i * width:start + (i + 1) * width] for i in range(3)])
    out_share = columns[:, start + 3 * width:].T
    return qkv_share, out_share, up_share, down_share


def shards(tokens, wqkv, wout, nb, up, down, lengths, cot):
    x_at, y_at, c_at = (lax.axis_index(name) for name in ("x", "y", "core"))
    d = tokens.shape[1]
    group_heads = wqkv.shape[2] // HEAD_DIM
    own = 2 * y_at + c_at
    heads = jnp.concatenate([own * group_heads + jnp.arange(group_heads), (own ^ 2) * group_heads + jnp.arange(group_heads)])
    slopes = 2.0 ** (-8.0 * (heads + 1).astype(F32) / HEADS)
    info = jnp.concatenate([y_at[None].astype(jnp.int32), lengths])

    (proj, att, lse, normed, recip, ht, a_all, b_all, act, fpart, fpart_other,
     wqkv1, wout1, up1, down1) = forward(lengths, slopes, nb, tokens, wqkv, wout, up, down)
    out, d2, d2t, dgu, dh, sums2 = ffn_bwd(
        info, fpart, fpart_other, normed, cot, nb, up, up1, down, down1, a_all, b_all
    )
    wo = lax.axis_size("wo")
    width, hidden = wqkv.shape[2], down.shape[0]
    if (d // (2 * wo)) % 16 == 0:
        share, sums, block_out, input_low = backward(
            wo, lengths, slopes, nb, sums2, tokens, d2, dh, normed, recip, wqkv, wqkv1, wout, wout1,
            proj, att, lse, dgu, act, ht, d2t, out,
        )
        columns = jnp.concatenate(list(share), axis=1)
        small_share = lax.dynamic_slice_in_dim(sums[:6], (lax.axis_index("wo") * 2 + x_at) * (d // (2 * wo)), d // (2 * wo), 1)
        return (block_out, input_low.astype(F32), *weight_shares(columns, hidden, width), small_share)

    out = lax.dynamic_slice_in_dim(out, y_at * (out.shape[0] // 2), out.shape[0] // 2, 0)
    dh_other = swap(dh, "core")

    def grad(a, b):
        return lax.dot_general(a, b, (((1,), (0,)), ((), ())), preferred_element_type=F32).astype(BF16)

    def part_of(value, at):
        split = value.reshape(wo, 2, -1, value.shape[1])
        return lax.dynamic_index_in_dim(split, at, 1, keepdims=False).reshape(-1, value.shape[1])

    def add(a, b):
        return a.astype(F32) + b.astype(F32)

    down_peer = grad(d2t, act[1])
    down_peer_in = swap(down_peer, "y")
    up_peer = grad(ht, dgu[1])
    up_own = grad(ht, dgu[0])
    up_in = swap(jnp.concatenate([part_of(up_own, 1 - x_at), part_of(up_peer, 1 - x_at)], axis=0), "x")
    down_own = grad(d2t, act[0])

    quarter = out.shape[0] // 2
    order = jnp.stack([2 * y_at, 2 * y_at + 1, 2 * (1 - y_at) + c_at, 2 * (1 - y_at) + 1 - c_at]).astype(jnp.int32)

    def mine(value):
        return lax.dynamic_slice_in_dim(value, c_at * quarter, quarter, 0)

    d2 = after(d2, down_own)
    d1, ipart, agrad0, agrad1, sums1 = attn_bwd(
        info, slopes, tokens, d2, dh, dh_other, normed, recip, nb, wqkv, wqkv1, wout, wout1,
        proj, att, lse,
    )
    ipart_other = swap(ipart, "core")
    near_out = swap(mine(out), "y")

    attn_in = swap(jnp.concatenate([part_of(agrad0, 1 - x_at), part_of(agrad1, 1 - x_at)], axis=0), "x")

    total = (d1 + add(ipart, ipart_other)).astype(BF16)
    near_in = swap(mine(total), "y")

    down_all = add(down_own, down_peer_in).astype(BF16)
    down_in = swap(part_of(down_all, 1 - x_at), "x")
    down_half = add(part_of(down_all, x_at), down_in).astype(BF16)
    n = d // 2
    up_peer_half = add(part_of(up_peer, x_at), up_in[n:]).astype(BF16)
    up_half = add(add(part_of(up_own, x_at), up_in[:n]), swap(up_peer_half, "y")).astype(BF16)
    attn_peer_half = add(part_of(agrad1, x_at), attn_in[n:]).astype(BF16)
    attn_half = add(add(part_of(agrad0, x_at), attn_in[:n]), swap(attn_peer_half, "y")).astype(BF16)

    scatter = functools.partial(lax.psum_scatter, axis_name="wo", scatter_dimension=0, tiled=True)
    columns = jnp.concatenate([scatter(jnp.concatenate([down_half, up_half], axis=1)), scatter(attn_half)], axis=1).astype(F32)
    small = jnp.concatenate([sums1[:3], sums2[:3]], axis=0)
    small_share = lax.psum_scatter(lax.psum(small, "y"), WIDE, scatter_dimension=1, tiled=True)

    block_out = place(order, out, near_out, swap(near_out, "core"), BF16)
    input_grad = place(order, total, near_in, swap(near_in, "core"), F32)
    return (block_out, input_grad, *weight_shares(columns, hidden, width), small_share)


def solution(mesh):
    wide = mesh.shape["wide"]
    grid = Mesh(mesh.devices.reshape(wide // 2, 2, 2, 2), ("wo", "x", "y", "core"))
    narrow = ("y", "core")
    placed = (
        P(WIDE, None),
        P(None, None, narrow),
        P(narrow, None),
        P(),
        P(None, None, narrow),
        P(narrow, None),
        P(WIDE),
        P(WIDE, None),
    )
    return jax.shard_map(
        shards,
        mesh=grid,
        in_specs=placed,
        out_specs=(
            P(WIDE, None),
            P(WIDE, None),
            P(None, WIDE, narrow),
            P(narrow, WIDE),
            P(None, WIDE, narrow),
            P(narrow, WIDE),
            P(None, WIDE),
        ),
        check_vma=False,
    )
```

```python
import functools
import math

import jax
import jax.numpy as jnp
from jax import lax
from jax.experimental import pallas as pl
from jax.experimental.pallas import tpu as pltpu
from jax.sharding import Mesh, PartitionSpec as P

HEADS = 12
HEAD_DIM = 64
EPS = 1e-05
F32 = jnp.float32
BF16 = jnp.bfloat16
SCALE = 1.0 / math.sqrt(HEAD_DIM)
NEG = -1e30
MESH_ID = pl.DeviceIdType.MESH
VMEM_LIMIT = 56 * 1024 * 1024


def dot(a, b):
    return lax.dot_general(a, b, (((1,), (0,)), ((), ())), preferred_element_type=F32)


def dot_nt(a, b):
    return lax.dot_general(a, b, (((1,), (1,)), ((), ())), preferred_element_type=F32)


def dot_tn(a, b):
    return lax.dot_general(a, b, (((0,), (0,)), ((), ())), preferred_element_type=F32)


def whole(shape):
    return pl.BlockSpec(shape, lambda i, *_: (0,) * len(shape))


def head_lanes(width):
    lane = lax.broadcasted_iota(jnp.int32, (1, width), 1)
    return [(lane >= h * HEAD_DIM) & (lane < (h + 1) * HEAD_DIM) for h in range(width // HEAD_DIM)]


def fill_distance(ref):
    n = ref.shape[0]
    row = lax.broadcasted_iota(jnp.int32, (n, n), 0)
    col = lax.broadcasted_iota(jnp.int32, (n, n), 1)
    ref[...] = jnp.abs(row - col).astype(F32)


def params():
    return pltpu.CompilerParams(vmem_limit_bytes=VMEM_LIMIT, dimension_semantics=("arbitrary",))


def remote(src, dst, send, recv, axis, peer):
    return pltpu.make_async_remote_copy(src, dst, send, recv, device_id={axis: peer}, device_id_type=MESH_ID)


def standardize(value):
    center = value - jnp.mean(value, axis=1, keepdims=True)
    recip = lax.rsqrt(jnp.mean(center * center, axis=1, keepdims=True) + EPS)
    return center * recip, recip


def norm_grad(grad, normed, recip, gain):
    e = grad * gain
    inner = jnp.mean(e * normed, axis=1, keepdims=True)
    return recip * (e - jnp.mean(e, axis=1, keepdims=True) - normed * inner)


def rows_of_sums(values):
    width = values[0].shape[1]
    sums = [jnp.sum(v, axis=0, keepdims=True) for v in values]
    return jnp.concatenate(sums + [jnp.zeros((8 - len(sums), width), F32)], axis=0)


def ffn_bwd_kernel(pa, pb, normed_ref, cot, nb, up0, up1, down0, down1, a_all, b_all,
                   block_out, d2_ref, d2t_ref, dgu, dh_ref, sums_ref, outb, own_sem, ysend, yrecv):
    hidden = down0.shape[0]
    i = pl.program_id(0)
    n, tile, _ = outb.shape
    y_at, c_at = lax.axis_index("y"), lax.axis_index("core")

    @pl.when(i == 0)
    def _():
        barrier = pltpu.get_barrier_semaphore()
        pl.semaphore_signal(barrier, inc=1, device_id={"y": 1 - y_at}, device_id_type=MESH_ID)
        pl.semaphore_wait(barrier, 1)

    def own_copy(t):
        return pltpu.make_async_copy(outb.at[t], block_out.at[pl.ds((y_at * n + t) * tile, tile)], own_sem.at[t])

    def side_copy(t):
        side = tile // 2
        return remote(outb.at[t, pl.ds(c_at * side, side)], block_out.at[pl.ds((y_at * n + t) * tile + c_at * side, side)],
                      ysend.at[t], yrecv.at[t], "y", 1 - y_at)

    h = normed_ref[...] * nb[0:1] + nb[1:2]
    second = pa[...].astype(F32) + pb[...].astype(F32) + nb[5:6] + h
    normed, recip = standardize(second)
    gain = nb[3:4]
    outb[i] = (normed * gain + nb[4:5]).astype(BF16)
    own_copy(i).start()

    @pl.when(i < n - 1)
    def _():
        side_copy(i).start()

    c = cot[...].astype(F32)
    d2 = norm_grad(c, normed, recip, gain)
    d2_ref[...] = d2
    d2b = d2.astype(BF16)
    d2t_ref[...] = d2b.T
    sums = rows_of_sums([c * normed, c, d2])

    @pl.when(pl.program_id(0) == 0)
    def _():
        sums_ref[...] = sums

    @pl.when(pl.program_id(0) > 0)
    def _():
        sums_ref[...] += sums

    total = None
    step = 768
    for g, (up, down) in enumerate(((up0, down0), (up1, down1))):
        for at in range(0, hidden, step):
            cols = slice(at, at + step)
            dact = dot_nt(d2b, down[cols, :])
            dgu[g, :, cols] = (dact * a_all[g, :, cols].astype(F32)).astype(BF16)
            dgu[g, :, slice(hidden + at, hidden + at + step)] = (dact * b_all[g, :, cols].astype(F32)).astype(BF16)
        for k in range(2):
            term = dot_nt(dgu[g, :, k * hidden:(k + 1) * hidden], up[k])
            total = term if total is None else total + term
    dh_ref[...] = total.astype(BF16)

    @pl.when(i == n - 1)
    def _():
        for t in range(n):
            own_copy(t).wait()
        for t in range(n - 1):
            side_copy(t).wait()


def ffn_bwd(tile, pa, pb, normed, cot, nb, up0, up1, down0, down1, a_all, b_all):
    half, d = pa.shape
    hidden = down0.shape[0]
    n = half // tile
    row = lambda w: pl.BlockSpec((tile, w), lambda i, *_: (i, 0))
    return pl.pallas_call(
        ffn_bwd_kernel,
        grid=(n,),
        in_specs=[
            row(d), row(d), row(d),
            pl.BlockSpec((tile, d), lambda i: (lax.axis_index("y") * n + i, 0)),
            whole(nb.shape),
            whole(up0.shape), whole(up1.shape), whole(down0.shape), whole(down1.shape),
            pl.BlockSpec((2, tile, hidden), lambda i: (0, i, 0)),
            pl.BlockSpec((2, tile, hidden), lambda i: (0, i, 0)),
        ],
        out_specs=[
            pl.BlockSpec(memory_space=pl.ANY), row(d),
            pl.BlockSpec((d, tile), lambda i: (0, i)),
            pl.BlockSpec((2, tile, 2 * hidden), lambda i: (0, i, 0)), row(d), whole((8, d)),
        ],
        scratch_shapes=[
            pltpu.VMEM((n, tile, d), BF16), pltpu.SemaphoreType.DMA((n,)), pltpu.SemaphoreType.DMA((n - 1,)),
            pltpu.SemaphoreType.DMA((n - 1,)),
        ],
        out_shape=[
            jax.ShapeDtypeStruct((2 * half, d), BF16),
            jax.ShapeDtypeStruct((half, d), F32),
            jax.ShapeDtypeStruct((d, half), BF16),
            jax.ShapeDtypeStruct((2, half, 2 * hidden), BF16),
            jax.ShapeDtypeStruct((half, d), BF16),
            jax.ShapeDtypeStruct((8, d), F32),
        ],
        compiler_params=pltpu.CompilerParams(
            vmem_limit_bytes=VMEM_LIMIT, dimension_semantics=("arbitrary",), collective_id=2, has_side_effects=True
        ),
        cost_estimate=pl.CostEstimate(
            flops=12 * half * d * hidden, bytes_accessed=half * d * 20 + half * hidden * 16 + 12 * d * hidden,
            transcendentals=half,
        ),
        name="ffn_bwd",
    )(pa, pb, normed, cot, nb, up0, up1, down0, down1, a_all, b_all)


def attn_bwd_kernel(info, slopes, x_ref, d2_ref, ha, hb, normed_ref, recip_ref, nb, wqkv0, wqkv1, wout0, wout1,
                    proj_all, att_all, lse_all,
                    d1_ref, part, grad0, grad1, sums_ref, dist, sum0, sum1):
    step = pl.program_id(0)
    win = d2_ref.shape[0]
    width = wout0.shape[0]
    heads = width // HEAD_DIM

    @pl.when(step == 0)
    def _():
        fill_distance(dist)

    normed = normed_ref[...]
    dh = d2_ref[...] + (ha[...].astype(F32) + hb[...].astype(F32))
    d1 = norm_grad(dh, normed, recip_ref[:, 0:1], nb[0:1])
    d1_ref[...] = d1
    d1b = d1.astype(BF16)
    x = x_ref[...]
    sums = rows_of_sums([dh * normed, dh, d1])

    @pl.when(step == 0)
    def _():
        sums_ref[...] = sums

    @pl.when(step > 0)
    def _():
        sums_ref[...] += sums

    limit = info[1 + info[0] * pl.num_programs(0) + step]
    lanes = head_lanes(width)
    key_on = lax.broadcasted_iota(jnp.int32, (win, 1), 0) < limit
    stat_lane = lax.broadcasted_iota(jnp.int32, (1, 128), 1)
    total = None
    for g, (wqkv, wout, acc) in enumerate(((wqkv0, wout0, sum0), (wqkv1, wout1, sum1))):
        q, k, v = proj_all[g, 0], proj_all[g, 1], proj_all[g, 2]
        datt = dot_nt(d1b, wout[...]).astype(BF16)
        product = datt.astype(F32) * att_all[g].astype(F32)
        stat = jnp.zeros((win, 128), F32)
        for h in range(heads):
            inner = jnp.sum(jnp.where(lanes[h], product, 0.0), axis=1, keepdims=True)
            stat = jnp.where(stat_lane == h, inner, stat)
        inner_rows = stat.T[0:8]
        qs = q * jnp.asarray(SCALE, BF16)
        dq = jnp.zeros((win, width), F32)
        dk = jnp.zeros((win, width), F32)
        dv = jnp.zeros((win, width), F32)
        for h in range(heads):
            qh = jnp.where(lanes[h], qs, jnp.zeros_like(qs))
            oh = jnp.where(lanes[h], datt, jnp.zeros_like(datt))
            s = dot_nt(k, qh) - slopes[g * heads + h] * dist[...]
            s = jnp.where(key_on, s, NEG)
            p = jnp.exp(s - lse_all[g, 0, h:h + 1, :])
            dp = dot_nt(v, oh)
            ds = (p * (dp - inner_rows[h:h + 1, :])).astype(BF16)
            dv = jnp.where(lanes[h], dot(p.astype(BF16), datt), dv)
            dk = jnp.where(lanes[h], dot(ds, q), dk)
            dq = jnp.where(lanes[h], dot_tn(ds, k), dq)
        dqb = (dq * SCALE).astype(BF16)
        dkb = (dk * SCALE).astype(BF16)
        dvb = dv.astype(BF16)
        terms = [dot_tn(x, dqb), dot_tn(x, dkb), dot_tn(x, dvb), dot_tn(d1b, att_all[g])]

        @pl.when(step == 0)
        def _():
            for i in range(4):
                acc[i] = terms[i]

        @pl.when(step > 0)
        def _():
            for i in range(4):
                acc[i] += terms[i]

        term = dot(dqb, wqkv[0]) + dot(dkb, wqkv[1]) + dot(dvb, wqkv[2])
        total = term if total is None else total + term
    part[...] = total.astype(BF16)

    @pl.when(step == pl.num_programs(0) - 1)
    def _():
        for acc, grad in ((sum0, grad0), (sum1, grad1)):
            for i in range(4):
                grad[:, i * width:(i + 1) * width] = acc[i].astype(BF16)


def attn_bwd(info, slopes, tokens, d2, ha, hb, normed, recip, nb, wqkv0, wqkv1, wout0, wout1,
             proj, att, lse):
    half, d = d2.shape
    width = wout0.shape[0]
    _, nwin, _, win = lse.shape
    heads = 2 * width // HEAD_DIM
    row = lambda w: pl.BlockSpec((win, w), lambda i, *_: (i, 0))
    return pl.pallas_call(
        attn_bwd_kernel,
        grid_spec=pltpu.PrefetchScalarGridSpec(
            num_scalar_prefetch=2,
            grid=(nwin,),
            in_specs=[
                pl.BlockSpec((win, d), lambda i, info, sl: (info[0] * nwin + i, 0)),
                row(d), row(d), row(d), row(d), row(128), whole(nb.shape),
                whole(wqkv0.shape), whole(wqkv1.shape), whole(wout0.shape), whole(wout1.shape),
                pl.BlockSpec((2, 3, win, width), lambda i, *_: (0, 0, i, 0)),
                pl.BlockSpec((2, win, width), lambda i, *_: (0, i, 0)),
                pl.BlockSpec((2, 1, 8, win), lambda i, *_: (0, i, 0, 0)),
            ],
            out_specs=[row(d), row(d), whole((d, 4 * width)), whole((d, 4 * width)), whole((8, d))],
            scratch_shapes=[pltpu.VMEM((win, win), F32), pltpu.VMEM((4, d, width), F32), pltpu.VMEM((4, d, width), F32)],
        ),
        out_shape=[
            jax.ShapeDtypeStruct((half, d), F32),
            jax.ShapeDtypeStruct((half, d), BF16),
            jax.ShapeDtypeStruct((d, 4 * width), BF16),
            jax.ShapeDtypeStruct((d, 4 * width), BF16),
            jax.ShapeDtypeStruct((8, d), F32),
        ],
        compiler_params=params(),
        cost_estimate=pl.CostEstimate(
            flops=2 * half * d * width * 16 + 10 * nwin * heads * win * win * 256,
            bytes_accessed=half * d * 20 + half * width * 32 + d * width * 16,
            transcendentals=nwin * heads * win * win,
        ),
        name="attn_bwd",
    )(info, slopes, tokens, d2, ha, hb, normed, recip, nb, wqkv0, wqkv1, wout0, wout1,
      proj, att, lse)


def place_kernel(order, mine, near, far, out):
    step = pl.program_id(0)

    @pl.when(step < 2)
    def _():
        out[...] = mine[...].astype(out.dtype)

    @pl.when(step == 2)
    def _():
        out[...] = near[...].astype(out.dtype)

    @pl.when(step == 3)
    def _():
        out[...] = far[...].astype(out.dtype)


def place(order, mine, near, far, dtype):
    quarter, d = near.shape
    return pl.pallas_call(
        place_kernel,
        grid_spec=pltpu.PrefetchScalarGridSpec(
            num_scalar_prefetch=1,
            grid=(4,),
            in_specs=[
                pl.BlockSpec((quarter, d), lambda i, o: (jnp.minimum(i, 1), 0)),
                whole((quarter, d)),
                whole((quarter, d)),
            ],
            out_specs=pl.BlockSpec((quarter, d), lambda i, o: (o[i], 0)),
        ),
        out_shape=jax.ShapeDtypeStruct((4 * quarter, d), dtype),
        compiler_params=params(),
        cost_estimate=pl.CostEstimate(flops=0, bytes_accessed=24 * quarter * d, transcendentals=0),
        name="place",
    )(order, mine, near, far)


TILE = 256


def forward_kernel(info, slopes, nb, tokens, wqkv, wout, up, down,
                   proj_out, att_out, lse_out, normed_out, recip_out, ht_out, a_out, b_out, act_out, fown_out, frecv_out,
                   wqkv1_out, wout1_out, up1_out, down1_out,
                   xbuf, wqv, wov, upv, downv, projb, attb, lseb, pown, precv, normedb, recipb, hbuf, htb, ab, bb, actb,
                   facc, fown, dist,
                   load_sem, ysend, yrecv, xsend, xrecv, zsend, zrecv, psend, prem, fsend, frem, out_sem, pout_sem, tout_sem, fout_sem):
    wo_at, x_at, y_at, c_at = (lax.axis_index(n) for n in ("wo", "x", "y", "core"))
    nwin, _, win = lse_out.shape[1:]
    half, d = xbuf.shape
    width = wout.shape[0]
    hidden = down.shape[0]
    heads = width // HEAD_DIM
    tiles = half // TILE
    z_at = wo_at % 2
    z_peer = wo_at + 1 - 2 * z_at

    barrier = pltpu.get_barrier_semaphore()
    for axis, to in (("x", 1 - x_at), ("y", 1 - y_at), ("core", 1 - c_at), ("wo", z_peer)):
        pl.semaphore_signal(barrier, inc=1, device_id={axis: to}, device_id_type=MESH_ID)
    pl.semaphore_wait(barrier, 4)

    def quarter(i, q):
        if i == 0:
            return wqkv.at[:, pl.ds(q * (width // 4), width // 4)], wqv.at[1, :, pl.ds(q * (width // 4), width // 4)]
        if i == 1:
            return wout.at[pl.ds(q * (width // 4), width // 4)], wov.at[1, pl.ds(q * (width // 4), width // 4)]
        if i == 2:
            return up.at[:, pl.ds(q * (d // 4), d // 4)], upv.at[1, :, pl.ds(q * (d // 4), d // 4)]
        return down.at[pl.ds(q * (hidden // 4), hidden // 4)], downv.at[1, pl.ds(q * (hidden // 4), hidden // 4)]

    def eighth(i, q, e):
        if i == 0:
            return wqv.at[1, :, pl.ds(q * (width // 4), width // 4), e * (d // 2):(e + 1) * (d // 2)]
        if i == 1:
            return wov.at[1, pl.ds(q * (width // 4), width // 4), e * (d // 2):(e + 1) * (d // 2)]
        if i == 2:
            return upv.at[1, :, pl.ds(q * (d // 4) + e * (d // 8), d // 8)]
        return downv.at[1, pl.ds(q * (hidden // 4) + e * (hidden // 8), hidden // 8)]

    here = 2 * x_at + z_at
    across_x = 2 * (1 - x_at) + z_at
    across_z = 2 * x_at + 1 - z_at

    def over_y(i):
        src, dst = quarter(i, here)
        return remote(src, dst, ysend.at[i], yrecv.at[i], "y", 1 - y_at)

    def level_one(i):
        _, ref = quarter(i, here)
        return (remote(ref, ref, xsend.at[0, i], xrecv.at[0, i], "x", 1 - x_at),
                remote(ref, ref, zsend.at[0, i], zrecv.at[0, i], "wo", z_peer))

    def level_two(i):
        from_z, from_x = eighth(i, across_z, 0), eighth(i, across_x, 1)
        return (remote(from_z, from_z, xsend.at[1, i], xrecv.at[1, i], "x", 1 - x_at),
                remote(from_x, from_x, zsend.at[1, i], zrecv.at[1, i], "wo", z_peer))

    def launch(copies):
        for copy in copies:
            copy.start()

    def arrive(copies):
        for copy in copies:
            copy.wait_recv()

    loads = [
        pltpu.make_async_copy(tokens.at[pl.ds(y_at * half, half)], xbuf, load_sem.at[0]),
        pltpu.make_async_copy(wqkv, wqv.at[0], load_sem.at[1]),
        pltpu.make_async_copy(wout, wov.at[0], load_sem.at[2]),
        pltpu.make_async_copy(up, upv.at[0], load_sem.at[3]),
        pltpu.make_async_copy(down, downv.at[0], load_sem.at[4]),
    ]
    over_y(0).start()
    over_y(1).start()
    for load in loads:
        load.start()
    fill_distance(dist)
    lanes = head_lanes(width)
    stat_lane = lax.broadcasted_iota(jnp.int32, (1, 128), 1)
    key_at = lax.broadcasted_iota(jnp.int32, (1, win), 1)
    for load in loads[:3]:
        load.wait()

    def part_copy(w):
        rows = pl.ds(w * win, win)
        return remote(pown.at[rows], precv.at[rows], psend.at[w], prem.at[w], "core", 1 - c_at)

    def proj_copy(t):
        g, rows = t // nwin, pl.ds((t % nwin) * win, win)
        return (
            pltpu.make_async_copy(projb.at[g, :, rows], proj_out.at[g, :, rows], pout_sem.at[0, t]),
            pltpu.make_async_copy(attb.at[g, rows], att_out.at[g, rows], pout_sem.at[1, t]),
        )

    def attention(t, carry):
        g, w = t // nwin, t % nwin
        start = w * win
        x = xbuf[pl.ds(start, win)]
        q = dot_nt(x, wqv[g, 0]).astype(BF16)
        k = dot_nt(x, wqv[g, 1]).astype(BF16)
        v = dot_nt(x, wqv[g, 2]).astype(BF16)
        projb[g, 0, pl.ds(start, win)] = q
        projb[g, 1, pl.ds(start, win)] = k
        projb[g, 2, pl.ds(start, win)] = v
        key_on = key_at < info[y_at * nwin + w]
        rows = win // 2
        for b in range(2):
            at = slice(b * rows, (b + 1) * rows)
            qb = q[at] * jnp.asarray(SCALE, BF16)
            att = jnp.zeros((rows, width), F32)
            stat = jnp.zeros((rows, 128), F32)
            for h in range(heads):
                qh = jnp.where(lanes[h], qb, jnp.zeros_like(qb))
                s = dot_nt(qh, k) - slopes[g * heads + h] * dist[at]
                s = jnp.where(key_on, s, NEG)
                top = jnp.max(s, axis=1, keepdims=True)
                p = jnp.exp(s - top)
                total = jnp.sum(p, axis=1, keepdims=True)
                o = dot(p.astype(BF16), v) * (1.0 / total)
                att = jnp.where(lanes[h], o, att)
                stat = jnp.where(stat_lane == h, top + jnp.log(total), stat)
            attb[g, pl.ds(start + b * rows, rows)] = att.astype(BF16)
            lseb[g, w, :, at] = stat.T[0:8]
        for copy in proj_copy(t):
            copy.start()

        @pl.when(t >= nwin)
        def _():
            out = dot(attb[0, pl.ds(start, win)], wov[0]) + dot(attb[1, pl.ds(start, win)], wov[1])
            pown[pl.ds(start, win)] = out.astype(BF16)
            part_copy(w).start()

        @pl.when(t == 0)
        def _():
            for i in range(2):
                over_y(i).wait_recv()
                launch(level_one(i))
            over_y(2).start()

        @pl.when(t == nwin - 1)
        def _():
            over_y(3).start()
            for i in range(2):
                arrive(level_one(i))
                launch(level_two(i))
            for i in range(2):
                arrive(level_two(i))

        @pl.when(t == nwin)
        def _():
            over_y(2).wait_recv()
            launch(level_one(2))

        return carry

    lax.fori_loop(0, 2 * nwin, attention, 0)
    lse_copy = pltpu.make_async_copy(lseb, lse_out, out_sem.at[0])
    lse_copy.start()
    loads[3].wait()
    loads[4].wait()
    step = 256

    def hidden_units(g, start, hb):
        for at in range(0, hidden, step):
            cols = slice(at, at + step)
            gate = dot(hb, upv[g, 0, :, cols])
            lift = dot(hb, upv[g, 1, :, cols])
            cdf = 0.5 * (1.0 + lax.erf(gate * (1.0 / math.sqrt(2.0))))
            pdf = jnp.exp(-0.5 * gate * gate) * (1.0 / math.sqrt(2.0 * math.pi))
            gelu = gate * cdf
            rows = pl.ds(start, TILE)
            ab[g, rows, cols] = (lift * (cdf + gate * pdf)).astype(BF16)
            bb[g, rows, cols] = gelu.astype(BF16)
            actb[g, rows, cols] = (gelu * lift).astype(BF16)

    def tile_copies(t):
        g, rows = t // tiles, pl.ds((t % tiles) * TILE, TILE)
        return [
            pltpu.make_async_copy(b.at[g, rows], o.at[g, rows], tout_sem.at[i, t])
            for i, (b, o) in enumerate(((ab, a_out), (bb, b_out), (actb, act_out)))
        ]

    def norm_copies(i):
        rows = pl.ds(pl.multiple_of(i * TILE, TILE), TILE)
        return [
            pltpu.make_async_copy(b.at[rows], o.at[rows], fout_sem.at[n, i])
            for n, (b, o) in enumerate(((normedb, normed_out), (recipb, recip_out)))
        ] + [pltpu.make_async_copy(htb.at[:, rows], ht_out.at[:, rows], fout_sem.at[2, i])]

    def first(i, carry):
        start = i * TILE

        @pl.when(i % (win // TILE) == 0)
        def _():
            part_copy(i // (win // TILE)).wait_recv()

        rows = pl.ds(start, TILE)
        value = (pown[rows].astype(F32) + precv[rows].astype(F32)) + nb[2:3] + xbuf[rows].astype(F32)
        normed, recip = standardize(value)
        normedb[rows] = normed
        recipb[rows] = jnp.broadcast_to(recip, (TILE, 128))
        hb = (normed * nb[0:1] + nb[1:2]).astype(BF16)
        hbuf[rows] = hb
        htb[:, pl.ds(pl.multiple_of(start, TILE), TILE)] = hb.T
        hidden_units(0, start, hb)
        facc[rows] = dot(actb[0, rows], downv[0])
        for copy in tile_copies(i) + norm_copies(i):
            copy.start()

        @pl.when(i == tiles // 2 - 1)
        def _():
            arrive(level_one(2))
            launch(level_two(2))
            over_y(3).wait_recv()

        return carry

    lax.fori_loop(0, tiles, first, 0)
    launch(level_one(3))
    arrive(level_two(2))

    def second(i, carry):
        start = i * TILE
        hidden_units(1, start, hbuf[pl.ds(start, TILE)])
        for copy in tile_copies(tiles + i):
            copy.start()

        @pl.when(i == tiles - 2)
        def _():
            arrive(level_one(3))
            launch(level_two(3))

        return carry

    lax.fori_loop(0, tiles, second, 0)
    arrive(level_two(3))

    def final_copy(i):
        rows = pl.ds(i * TILE, TILE)
        return (
            remote(fown.at[rows], frecv_out.at[rows], fsend.at[i], frem.at[i], "core", 1 - c_at),
            pltpu.make_async_copy(fown.at[rows], fown_out.at[rows], fout_sem.at[3, i]),
        )

    def third(i, carry):
        rows = pl.ds(i * TILE, TILE)
        fown[rows] = (facc[rows] + dot(actb[1, rows], downv[1])).astype(BF16)
        for copy in final_copy(i):
            copy.start()
        return carry

    weights_out = [
        pltpu.make_async_copy(wqv.at[1], wqkv1_out, out_sem.at[1]),
        pltpu.make_async_copy(wov.at[1], wout1_out, out_sem.at[2]),
        pltpu.make_async_copy(upv.at[1], up1_out, out_sem.at[3]),
        pltpu.make_async_copy(downv.at[1], down1_out, out_sem.at[4]),
    ]
    for copy in weights_out:
        copy.start()
    lax.fori_loop(0, tiles, third, 0)

    def finish(i, carry):
        sent, kept = final_copy(i)
        sent.wait_recv()
        sent.wait_send()
        kept.wait()
        for copy in norm_copies(i):
            copy.wait()
        return carry

    lax.fori_loop(0, tiles, finish, 0)

    def drain_tiles(t, carry):
        for copy in tile_copies(t):
            copy.wait()
        return carry

    lax.fori_loop(0, 2 * tiles, drain_tiles, 0)

    def drain_proj(t, carry):
        for copy in proj_copy(t):
            copy.wait()
        return carry

    lax.fori_loop(0, 2 * nwin, drain_proj, 0)

    def drain_part(w, carry):
        part_copy(w).wait_send()
        return carry

    lax.fori_loop(0, nwin, drain_part, 0)
    lse_copy.wait()
    for copy in weights_out:
        copy.wait()
    for i in range(4):
        over_y(i).wait_send()
        for copy in level_one(i) + level_two(i):
            copy.wait_send()


def forward(lengths, slopes, nb, tokens, wqkv, wout, up, down):
    d = tokens.shape[1]
    nwin = lengths.shape[0] // 2
    half = tokens.shape[0] // 2
    win = half // nwin
    width, hidden = wout.shape[0], down.shape[0]
    tiles = half // TILE
    heads = width // HEAD_DIM
    smem = pl.BlockSpec(memory_space=pltpu.SMEM)
    vmem = pl.BlockSpec(memory_space=pltpu.VMEM)
    hbm = pl.BlockSpec(memory_space=pl.ANY)
    acts = [((2, half, hidden), BF16)] * 3
    outs = [
        ((2, 3, half, width), BF16), ((2, half, width), BF16), ((2, nwin, 8, win), F32),
        ((half, d), F32), ((half, 128), F32), ((d, half), BF16), *acts,
        ((half, d), BF16), ((half, d), BF16),
        (wqkv.shape, BF16), (wout.shape, BF16), (up.shape, BF16), (down.shape, BF16),
    ]
    bufs = [
        ((half, d), BF16), ((2,) + wqkv.shape, BF16), ((2,) + wout.shape, BF16), ((2,) + up.shape, BF16),
        ((2,) + down.shape, BF16), ((2, 3, half, width), BF16), ((2, half, width), BF16), ((2, nwin, 8, win), F32),
        ((half, d), BF16), ((half, d), BF16), ((half, d), F32), ((half, 128), F32), ((half, d), BF16), ((d, half), BF16), *acts,
        ((half, d), F32), ((half, d), BF16), ((win, win), F32),
    ]
    sems = [(5,), (4,), (4,), (2, 4), (2, 4), (2, 4), (2, 4), (nwin,), (nwin,), (tiles,), (tiles,), (5,), (2, 2 * nwin), (3, 2 * tiles), (5, tiles)]
    return pl.pallas_call(
        forward_kernel,
        in_specs=[smem, smem, vmem] + [hbm] * 5,
        out_specs=[hbm] * len(outs),
        out_shape=[jax.ShapeDtypeStruct(*o) for o in outs],
        scratch_shapes=[pltpu.VMEM(*b) for b in bufs] + [pltpu.SemaphoreType.DMA(n) for n in sems],
        compiler_params=pltpu.CompilerParams(vmem_limit_bytes=62 * 1024 * 1024, collective_id=0, has_side_effects=True),
        cost_estimate=pl.CostEstimate(
            flops=2 * half * d * width * 16 + 12 * half * d * hidden + 8 * nwin * heads * win * win * 256,
            bytes_accessed=half * d * 30 + half * hidden * 12, transcendentals=half * hidden * 4,
        ),
        name="forward",
    )(lengths, slopes, nb, tokens, wqkv, wout, up, down)


BLOCK = 128
PAIR = 2 * BLOCK
FLIGHT = 6
TAIL_FLIGHT = 3


def backward_kernel(lengths, slopes, nb, sums2, tokens, d2_in, dh_in, normed_in, recip_in, wqkv, wqkv1, wout, wout1,
                    proj_in, att_in, lse_in, dgu_in, act_in, ht_in, d2t_in, half_in,
                    share, total_sums, block_out, input_grad,
                    gbuf, r1, r2, zr, dhr, dhw, normw, d2w, recw, xw, projw, attw, lsev, wqv, wov, ipown, iprecv, totb,
                    sumb, sumr, sumz, sum1,
                    g1s, g1r, g2s, g2r, zs, zrs, pre_sem, win_sem, w_sem, dh_s, dh_r, ip_s, ip_r,
                    tot_sem, iy_s, iy_r, ic_s, ic_r, bo_s, bo_r, sm_s, sm_r, smz_s, smz_r, ring_sem, t_sem):
    at = {n: lax.axis_index(n) for n in ("wo", "x", "y", "core")}
    wo_at, x_at, y_at, c_at = at["wo"], at["x"], at["y"], at["core"]
    n_wo = gbuf.shape[3]
    blocks = gbuf.shape[0]
    own_rows = gbuf.shape[4]
    half, d = normed_in.shape
    _, nwin, _, win = lse_in.shape
    width = wout.shape[0]
    hidden = act_in.shape[2]
    heads = width // HEAD_DIM
    ffn_blocks = 3 * hidden // BLOCK

    barrier = pltpu.get_barrier_semaphore()
    for axis in ("x", "y", "core"):
        pl.semaphore_signal(barrier, inc=1, device_id={axis: 1 - at[axis]}, device_id_type=MESH_ID)
    for k in range(n_wo - 1):
        pl.semaphore_signal(barrier, inc=1, device_id={"wo": (wo_at + k + 1) % n_wo}, device_id_type=MESH_ID)
    pl.semaphore_wait(barrier, n_wo + 2)

    def copy_one(b, is_y):
        send = 1 if is_y else 1 - x_at
        axis = "y" if is_y else "x"
        return remote(gbuf.at[b, send], r1.at[b], g1s.at[b], g1r.at[b], axis, 1 - at[axis])

    def copy_two(b, is_y):
        keep = 0 if is_y else x_at
        send = 1 - x_at if is_y else 1
        axis = "x" if is_y else "y"
        return remote(gbuf.at[b, keep, send], r2.at[b], g2s.at[b], g2r.at[b], axis, 1 - at[axis])

    def copy_z(b, is_y, k):
        keep = 0 if is_y else x_at
        keep2 = x_at if is_y else 0
        to = (wo_at + k + 1) % n_wo
        return remote(gbuf.at[b, keep, keep2, to], zr.at[b, k], zs.at[b, k], zrs.at[b, k], "wo", to)

    def by_kind(b, f):
        @pl.when(b % 3 == 1)
        def _():
            f(True)

        @pl.when(b % 3 != 1)
        def _():
            f(False)

    def stage_one(b):
        copy_one(b, False).wait_recv()

        def go(is_y):
            keep = 0 if is_y else x_at
            gbuf[b, keep] = (gbuf[b, keep].astype(F32) + r1[b].astype(F32)).astype(BF16)
            copy_two(b, is_y).start()

        by_kind(b, go)

        @pl.when(b + FLIGHT < ffn_blocks)
        def _():
            by_kind(b + FLIGHT, lambda is_y: copy_one(b + FLIGHT, is_y).start())

        @pl.when((b >= ffn_blocks) & (b + TAIL_FLIGHT < blocks))
        def _():
            by_kind(b + TAIL_FLIGHT, lambda is_y: copy_one(b + TAIL_FLIGHT, is_y).start())

    def stage_two(b):
        copy_two(b, False).wait_recv()

        def go(is_y):
            keep = 0 if is_y else x_at
            keep2 = x_at if is_y else 0
            gbuf[b, keep, keep2] = (gbuf[b, keep, keep2].astype(F32) + r2[b].astype(F32)).astype(BF16)
            for k in range(n_wo - 1):
                copy_z(b, is_y, k).start()

        by_kind(b, go)

    def stage_three(b):
        for k in range(n_wo - 1):
            copy_z(b, False, k).wait_recv()

        def go(is_y):
            keep = 0 if is_y else x_at
            keep2 = x_at if is_y else 0
            total = gbuf[b, keep, keep2, wo_at].astype(F32)
            for k in range(n_wo - 1):
                total = total + zr[b, k].astype(F32)
            share[b] = total

        by_kind(b, go)

    def advance(k):
        for j in (2 * k, 2 * k + 1):
            stage_one(j)

            @pl.when(k >= 1)
            def _():
                stage_two(j - 2)

            @pl.when(k >= 2)
            def _():
                stage_three(j - 4)

    def put(b, g, value):
        r = b % 3
        is_y = r * (2 - r)
        for j in range(2 * n_wo):
            px, w = j % 2, j // 2
            outer = g * is_y + px * (1 - is_y)
            gbuf[b, outer, g + px - outer, w] = value[j * own_rows:(j + 1) * own_rows].astype(BF16)

    def pre_loads(w):
        rows = pl.ds(w * win, win)
        return [
            pltpu.make_async_copy(src, dst, pre_sem.at[i])
            for i, (src, dst) in enumerate((
                (normed_in.at[rows], normw), (d2_in.at[rows], d2w), (recip_in.at[rows], recw), (dh_in.at[rows], dhw),
                (tokens.at[pl.ds(y_at * half + w * win, win)], xw),
            ))
        ]

    def win_loads(w):
        rows, slot = pl.ds(w * win, win), w % 2
        return [
            pltpu.make_async_copy(proj_in.at[:, :, rows], projw.at[slot], win_sem.at[0, slot]),
            pltpu.make_async_copy(att_in.at[:, rows], attw.at[slot], win_sem.at[1, slot]),
        ]

    dh_copy = remote(dh_in, dhr, dh_s.at[0], dh_r.at[0], "core", 1 - c_at)
    side = win // 2
    last_rows = pl.ds(y_at * half + (nwin - 1) * win + c_at * side, side)
    out_y = remote(block_out.at[last_rows], block_out.at[last_rows], bo_s.at[nwin], bo_r.at[nwin], "y", 1 - y_at)

    def out_c(w):
        rows = pl.ds((1 - y_at) * half + w * win + c_at * side, side)
        return remote(block_out.at[rows], block_out.at[rows], bo_s.at[w], bo_r.at[w], "core", 1 - c_at)

    loads = [
        pltpu.make_async_copy(src, dst, w_sem.at[i])
        for i, (src, dst) in enumerate((
            (wqkv, wqv.at[0]), (wqkv1, wqv.at[1]), (wout, wov.at[0]), (wout1, wov.at[1]), (lse_in, lsev),
        ))
    ]

    def ffn_grads(ring, lhs_d, lhs_h):
        lhs = [pltpu.make_async_copy(d2t_in, lhs_d, t_sem.at[0]), pltpu.make_async_copy(ht_in, lhs_h, t_sem.at[1])]
        down_pairs = hidden // PAIR
        up_pairs = 2 * hidden // PAIR

        def fetch(src, b, g):
            return pltpu.make_async_copy(src.at[g, :, pl.ds(pl.multiple_of(b * PAIR, PAIR), PAIR)],
                                         ring.at[b % 2, :, g * PAIR:(g + 1) * PAIR], ring_sem.at[b % 2, g])

        def run(src, left, count, first):
            for g in range(2):
                fetch(src, 0, g).start()

            def one(b, carry):
                @pl.when(b + 1 < count)
                def _():
                    for g in range(2):
                        fetch(src, b + 1, g).start()

                for g in range(2):
                    fetch(src, b, g).wait()
                value = dot(left[...], ring[b % 2]).astype(BF16)
                k = b + first
                for side in range(2):
                    for g in range(2):
                        at = g * PAIR + side * BLOCK
                        put(2 * k + side, g, value[:, at:at + BLOCK])

                    @pl.when(2 * k + side < FLIGHT)
                    def _():
                        by_kind(2 * k + side, lambda is_y: copy_one(2 * k + side, is_y).start())

                @pl.when((k >= 4) & (k % 2 == 0))
                def _():
                    advance((k - 4) // 2)

                return carry

            lax.fori_loop(0, count, one, 0)

        lhs[0].start()
        dh_copy.start()
        out_y.start()
        for w in range(nwin - 1):
            out_c(w).start()
        lhs[1].start()
        for copy in loads + pre_loads(0) + win_loads(0):
            copy.start()
        lhs[0].wait()
        run(act_in, lhs_d, down_pairs, 0)
        lhs[1].wait()
        run(dgu_in, lhs_h, up_pairs, down_pairs)

    pl.run_scoped(ffn_grads, pltpu.VMEM((2, half, 2 * PAIR), BF16), pltpu.VMEM((d, half), BF16), pltpu.VMEM((d, half), BF16))

    for load in loads:
        load.wait()
    dh_copy.wait_recv()
    lanes = head_lanes(width)
    stat_lane = lax.broadcasted_iota(jnp.int32, (1, 128), 1)

    def part_copy(w):
        return remote(ipown.at[w], iprecv.at[w], ip_s.at[w], ip_r.at[w], "core", 1 - c_at)

    def own_copy(w):
        return pltpu.make_async_copy(totb.at[w], input_grad.at[pl.ds(y_at * half + w * win, win)], tot_sem.at[w])

    def in_y(w):
        return remote(totb.at[w, pl.ds(c_at * side, side)], input_grad.at[pl.ds(y_at * half + w * win + c_at * side, side)],
                      iy_s.at[w], iy_r.at[w], "y", 1 - y_at)

    def in_c(w):
        rows = pl.ds((1 - y_at) * half + w * win + c_at * side, side)
        return remote(input_grad.at[rows], input_grad.at[rows], ic_s.at[w], ic_r.at[w], "core", 1 - c_at)

    def attention(acc, xt, d1t, d1b, d1w, iptot, dist, stage):
        fill_distance(dist)
        acc[...] = jnp.zeros_like(acc)
        sum1[...] = jnp.zeros_like(sum1)

        def send_total(w):
            part_copy(w).wait_recv()
            value = d1w[w % 2] + (ipown[w].astype(F32) + iprecv[w].astype(F32))
            totb[w] = value.astype(BF16)
            own_copy(w).start()
            in_y(w).start()

        def step(t, carry):
            w, g = t // 2, t % 2
            slot = w % 2

            @pl.when(g == 0)
            def _():
                for copy in pre_loads(w) + win_loads(w):
                    copy.wait()
                normed = normw[...]
                dh = d2w[...] + (dhw[...].astype(F32) + dhr[pl.ds(w * win, win)].astype(F32))
                d1 = norm_grad(dh, normed, recw[:, 0:1], nb[0:1])
                d1w[slot] = d1
                low = d1.astype(BF16)
                d1b[...] = low
                d1t[...] = low.T
                xt[...] = xw[...].T
                sum1[...] += rows_of_sums([dh * normed, dh, d1])

                @pl.when(w + 1 < nwin)
                def _():
                    for copy in pre_loads(w + 1) + win_loads(w + 1):
                        copy.start()

            q, k, v = projw[slot, g, 0], projw[slot, g, 1], projw[slot, g, 2]
            att = attw[slot, g]
            datt = dot_nt(d1b[...], wov[g]).astype(BF16)
            product = datt.astype(F32) * att.astype(F32)
            stat = jnp.zeros((win, 128), F32)
            for h in range(heads):
                inner = jnp.sum(jnp.where(lanes[h], product, 0.0), axis=1, keepdims=True)
                stat = jnp.where(stat_lane == h, inner, stat)
            inner_rows = stat.T[0:8]
            qs = q * jnp.asarray(SCALE, BF16)
            dq = jnp.zeros((win, width), F32)
            dks, dvs = [], []
            half_keys = win // 2
            limit = lengths[y_at * nwin + w]
            for kb in range(2):
                keys = slice(kb * half_keys, (kb + 1) * half_keys)
                kk, vk = k[keys], v[keys]
                key_on = lax.broadcasted_iota(jnp.int32, (half_keys, 1), 0) + kb * half_keys < limit
                dk = jnp.zeros((half_keys, width), F32)
                dv = jnp.zeros((half_keys, width), F32)
                for h in range(heads):
                    qh = jnp.where(lanes[h], qs, jnp.zeros_like(qs))
                    oh = jnp.where(lanes[h], datt, jnp.zeros_like(datt))
                    s = dot_nt(kk, qh) - slopes[g * heads + h] * dist[keys]
                    s = jnp.where(key_on, s, NEG)
                    p = jnp.exp(s - lsev[g, w, h:h + 1, :])
                    dp = dot_nt(vk, oh)
                    ds = (p * (dp - inner_rows[h:h + 1, :])).astype(BF16)
                    dv = jnp.where(lanes[h], dot(p.astype(BF16), datt), dv)
                    dk = jnp.where(lanes[h], dot(ds, q), dk)
                    dq = dq + jnp.where(lanes[h], dot_tn(ds, kk), 0.0)
                dks.append((dk * SCALE).astype(BF16))
                dvs.append(dv.astype(BF16))
            dqb = (dq * SCALE).astype(BF16)
            dkb = jnp.concatenate(dks, axis=0)
            dvb = jnp.concatenate(dvs, axis=0)
            acc[g, 0] += dot(xt[...], dqb)
            acc[g, 1] += dot(xt[...], dkb)
            acc[g, 2] += dot(xt[...], dvb)
            acc[g, 3] += dot(d1t[...], att)
            term = dot(dqb, wqv[g, 0]) + dot(dkb, wqv[g, 1]) + dot(dvb, wqv[g, 2])

            @pl.when(g == 0)
            def _():
                iptot[...] = term

            @pl.when(g == 1)
            def _():
                ipown[w] = (iptot[...] + term).astype(BF16)
                part_copy(w).start()

            @pl.when((g == 0) & (w > 0))
            def _():
                send_total(w - 1)

            @pl.when(t == 0)
            def _():
                advance(3)

            @pl.when(t == 1)
            def _():
                advance(4)

            @pl.when((t > 0) & (t < 2 * nwin - 1))
            def _():
                advance(t + 4)

            @pl.when(t == 2 * nwin - 1)
            def _():
                for b in (ffn_blocks - 2, ffn_blocks - 1):
                    stage_two(b)
                    stage_three(b - 2)


            @pl.when(t == 3)
            def _():
                out_y.wait_recv()
                out_c(nwin - 1).start()

            return carry

        lax.fori_loop(0, 2 * nwin, step, 0)

        first = blocks - 4 * width // BLOCK
        for g in range(2):
            for i in range(4):
                stage[:, i * width:(i + 1) * width] = acc[g, i].astype(BF16)
            for i in range(4 * width // BLOCK):
                put(first + i, g, stage[:, i * BLOCK:(i + 1) * BLOCK])
        for i in range(first, first + TAIL_FLIGHT):
            copy_one(i, i % 3 == 1).start()
        for b in (ffn_blocks - 2, ffn_blocks - 1):
            stage_three(b)
        for w in range(nwin - 1):
            in_y(w).wait_recv()
            in_c(w).start()
        stage_one(first)
        stage_one(first + 1)
        send_total(nwin - 1)

    pl.run_scoped(
        attention,
        pltpu.VMEM((2, 4, d, width), F32), pltpu.VMEM((d, win), BF16), pltpu.VMEM((d, win), BF16), pltpu.VMEM((win, d), BF16),
        pltpu.VMEM((2, win, d), F32), pltpu.VMEM((win, d), F32), pltpu.VMEM((win, win), F32), pltpu.VMEM((d, 4 * width), BF16),
    )

    sumb[0] = jnp.concatenate([sum1[0:3], sums2[0:3], jnp.zeros((2, d), F32)], axis=0)

    def sum_copy(i, axis):
        return remote(sumb.at[i], sumr.at[i], sm_s.at[i], sm_r.at[i], axis, 1 - at[axis])

    def sum_z(k):
        to = (wo_at + k + 1) % n_wo
        return remote(sumb.at[2], sumz.at[k], smz_s.at[k], smz_r.at[k], "wo", to)

    sum_copy(0, "y").start()

    def tail(i, carry):
        j = ffn_blocks + 1 + i

        @pl.when((i > 0) & (j < blocks))
        def _():
            stage_one(j)

        @pl.when(j <= blocks)
        def _():
            stage_two(j - 1)

        @pl.when(i > 0)
        def _():
            stage_three(j - 2)

        @pl.when(i == 0)
        def _():
            sum_copy(0, "y").wait_recv()
            sumb[1] = sumb[0] + sumr[0]
            sum_copy(1, "x").start()

        @pl.when(i == 1)
        def _():
            sum_copy(1, "x").wait_recv()
            sumb[2] = sumb[1] + sumr[1]
            for k in range(n_wo - 1):
                sum_z(k).start()

        return carry

    lax.fori_loop(0, blocks + 1 - ffn_blocks, tail, 0)
    in_y(nwin - 1).wait_recv()
    in_c(nwin - 1).start()
    total = sumb[2]
    for k in range(n_wo - 1):
        sum_z(k).wait_recv()
        total = total + sumz[k]
    total_sums[...] = total

    out_y.wait_send()
    for w in range(nwin):
        out_c(w).wait()
    dh_copy.wait_send()
    for i, axis in ((0, "y"), (1, "x")):
        sum_copy(i, axis).wait_send()
    for k in range(n_wo - 1):
        sum_z(k).wait_send()

    def drain_window(w, carry):
        part_copy(w).wait_send()
        own_copy(w).wait()
        in_y(w).wait_send()
        in_c(w).wait_send()
        in_c(w).wait_recv()
        return carry

    lax.fori_loop(0, nwin, drain_window, 0)

    def drain_block(b, carry):
        copy_one(b, False).wait_send()
        copy_two(b, False).wait_send()
        for k in range(n_wo - 1):
            copy_z(b, False, k).wait_send()
        return carry

    lax.fori_loop(0, blocks, drain_block, 0)


def backward(n_wo, lengths, slopes, nb, sums2, tokens, d2, dh, normed, recip, wqkv, wqkv1, wout, wout1,
             proj, att, lse, dgu, act, ht, d2t, half_out):
    half, d = normed.shape
    _, nwin, _, win = lse.shape
    width, hidden = wout.shape[0], act.shape[2]
    rows = d // (2 * n_wo)
    blocks = (3 * hidden + 4 * width) // BLOCK
    heads = width // HEAD_DIM
    smem = pl.BlockSpec(memory_space=pltpu.SMEM)
    vmem = pl.BlockSpec(memory_space=pltpu.VMEM)
    hbm = pl.BlockSpec(memory_space=pl.ANY)
    outs = [((blocks, rows, BLOCK), F32), ((8, d), F32), (tokens.shape, BF16), (tokens.shape, BF16)]
    bufs = [
        ((blocks, 2, 2, n_wo, rows, BLOCK), BF16), ((blocks, 2, n_wo, rows, BLOCK), BF16), ((blocks, n_wo, rows, BLOCK), BF16),
        ((blocks, n_wo - 1, rows, BLOCK), BF16), ((half, d), BF16), ((win, d), BF16), ((win, d), F32), ((win, d), F32),
        ((win, 128), F32), ((win, d), BF16), ((2, 2, 3, win, width), BF16), ((2, 2, win, width), BF16), (lse.shape, F32),
        ((2,) + wqkv.shape, BF16), ((2,) + wout.shape, BF16), ((nwin, win, d), BF16), ((nwin, win, d), BF16),
        ((nwin, win, d), BF16), ((3, 8, d), F32), ((2, 8, d), F32), ((n_wo - 1, 8, d), F32), ((8, d), F32),
    ]
    sems = [(blocks,)] * 4 + [(blocks, n_wo - 1)] * 2 + [(5,), (2, 2), (5,), (1,), (1,)] + [(nwin,)] * 7
    sems += [(nwin + 1,), (nwin + 1,), (2,), (2,), (n_wo - 1,), (n_wo - 1,), (2, 2), (2,)]
    return pl.pallas_call(
        backward_kernel,
        in_specs=[smem, smem, vmem, vmem] + [hbm] * 17,
        out_specs=[vmem, vmem, hbm, hbm],
        input_output_aliases={20: 2},
        out_shape=[jax.ShapeDtypeStruct(*o) for o in outs],
        scratch_shapes=[pltpu.VMEM(*b) for b in bufs] + [pltpu.SemaphoreType.DMA(n) for n in sems],
        compiler_params=pltpu.CompilerParams(vmem_limit_bytes=63 * 1024 * 1024, collective_id=1, has_side_effects=True),
        cost_estimate=pl.CostEstimate(
            flops=2 * half * d * width * 16 + 12 * half * d * hidden + 20 * nwin * heads * win * win * 256,
            bytes_accessed=half * d * 60 + half * hidden * 12, transcendentals=2 * nwin * heads * win * win,
        ),
        name="backward",
    )(lengths, slopes, nb, sums2, tokens, d2, dh, normed, recip, wqkv, wqkv1, wout, wout1,
      proj, att, lse, dgu, act, ht, d2t, half_out)


SWAP = [(0, 1), (1, 0)]
WIDE = ("wo", "x")


def swap(value, axis):
    return lax.ppermute(value, axis, SWAP)


def after(value, *others):
    return lax.optimization_barrier((value, *others))[0]


def weight_shares(columns, hidden, width):
    down_share = columns[:, :hidden].T
    up_share = jnp.stack([columns[:, hidden:2 * hidden], columns[:, 2 * hidden:3 * hidden]])
    start = 3 * hidden
    qkv_share = jnp.stack([columns[:, start + i * width:start + (i + 1) * width] for i in range(3)])
    out_share = columns[:, start + 3 * width:].T
    return qkv_share, out_share, up_share, down_share


def shards(tokens, wqkv, wout, nb, up, down, lengths, cot):
    x_at, y_at, c_at = (lax.axis_index(name) for name in ("x", "y", "core"))
    d = tokens.shape[1]
    group_heads = wout.shape[0] // HEAD_DIM
    wqkv = jnp.swapaxes(wqkv, 1, 2)
    own = 2 * y_at + c_at
    heads = jnp.concatenate([own * group_heads + jnp.arange(group_heads), (own ^ 2) * group_heads + jnp.arange(group_heads)])
    slopes = 2.0 ** (-8.0 * (heads + 1).astype(F32) / HEADS)
    info = jnp.concatenate([y_at[None].astype(jnp.int32), lengths])

    (proj, att, lse, normed, recip, ht, a_all, b_all, act, fpart, fpart_other,
     wqkv1, wout1, up1, down1) = forward(lengths, slopes, nb, tokens, wqkv, wout, up, down)
    out, d2, d2t, dgu, dh, sums2 = ffn_bwd(
        lse.shape[3], fpart, fpart_other, normed, cot, nb, up, up1, down, down1, a_all, b_all
    )
    wo = lax.axis_size("wo")
    width, hidden = wout.shape[0], down.shape[0]
    if (d // (2 * wo)) % 16 == 0:
        share, sums, block_out, input_low = backward(
            wo, lengths, slopes, nb, sums2, tokens, d2, dh, normed, recip, wqkv, wqkv1, wout, wout1,
            proj, att, lse, dgu, act, ht, d2t, out,
        )
        columns = share.transpose(1, 0, 2).reshape(share.shape[1], -1)
        small_share = lax.dynamic_slice_in_dim(sums[:6], (lax.axis_index("wo") * 2 + x_at) * (d // (2 * wo)), d // (2 * wo), 1)
        return (block_out, input_low.astype(F32), *weight_shares(columns, hidden, width), small_share)

    out = lax.dynamic_slice_in_dim(out, y_at * (out.shape[0] // 2), out.shape[0] // 2, 0)
    dh_other = swap(dh, "core")

    def grad(a, b):
        return lax.dot_general(a, b, (((1,), (0,)), ((), ())), preferred_element_type=F32).astype(BF16)

    def part_of(value, at):
        split = value.reshape(wo, 2, -1, value.shape[1])
        return lax.dynamic_index_in_dim(split, at, 1, keepdims=False).reshape(-1, value.shape[1])

    def add(a, b):
        return a.astype(F32) + b.astype(F32)

    down_peer = grad(d2t, act[1])
    down_peer_in = swap(down_peer, "y")
    up_peer = grad(ht, dgu[1])
    up_own = grad(ht, dgu[0])
    up_in = swap(jnp.concatenate([part_of(up_own, 1 - x_at), part_of(up_peer, 1 - x_at)], axis=0), "x")
    down_own = grad(d2t, act[0])

    quarter = out.shape[0] // 2
    order = jnp.stack([2 * y_at, 2 * y_at + 1, 2 * (1 - y_at) + c_at, 2 * (1 - y_at) + 1 - c_at]).astype(jnp.int32)

    def mine(value):
        return lax.dynamic_slice_in_dim(value, c_at * quarter, quarter, 0)

    d2 = after(d2, down_own)
    d1, ipart, agrad0, agrad1, sums1 = attn_bwd(
        info, slopes, tokens, d2, dh, dh_other, normed, recip, nb, wqkv, wqkv1, wout, wout1,
        proj, att, lse,
    )
    ipart_other = swap(ipart, "core")
    near_out = swap(mine(out), "y")

    attn_in = swap(jnp.concatenate([part_of(agrad0, 1 - x_at), part_of(agrad1, 1 - x_at)], axis=0), "x")

    total = (d1 + add(ipart, ipart_other)).astype(BF16)
    near_in = swap(mine(total), "y")

    down_all = add(down_own, down_peer_in).astype(BF16)
    down_in = swap(part_of(down_all, 1 - x_at), "x")
    down_half = add(part_of(down_all, x_at), down_in).astype(BF16)
    n = d // 2
    up_peer_half = add(part_of(up_peer, x_at), up_in[n:]).astype(BF16)
    up_half = add(add(part_of(up_own, x_at), up_in[:n]), swap(up_peer_half, "y")).astype(BF16)
    attn_peer_half = add(part_of(agrad1, x_at), attn_in[n:]).astype(BF16)
    attn_half = add(add(part_of(agrad0, x_at), attn_in[:n]), swap(attn_peer_half, "y")).astype(BF16)

    scatter = functools.partial(lax.psum_scatter, axis_name="wo", scatter_dimension=0, tiled=True)
    columns = jnp.concatenate([scatter(jnp.concatenate([down_half, up_half], axis=1)), scatter(attn_half)], axis=1).astype(F32)
    small = jnp.concatenate([sums1[:3], sums2[:3]], axis=0)
    small_share = lax.psum_scatter(lax.psum(small, "y"), WIDE, scatter_dimension=1, tiled=True)

    block_out = place(order, out, near_out, swap(near_out, "core"), BF16)
    input_grad = place(order, total, near_in, swap(near_in, "core"), F32)
    return (block_out, input_grad, *weight_shares(columns, hidden, width), small_share)


def solution(mesh):
    wide = mesh.shape["wide"]
    grid = Mesh(mesh.devices.reshape(wide // 2, 2, 2, 2), ("wo", "x", "y", "core"))
    narrow = ("y", "core")
    placed = (
        P(WIDE, None),
        P(None, None, narrow),
        P(narrow, None),
        P(),
        P(None, None, narrow),
        P(narrow, None),
        P(WIDE),
        P(WIDE, None),
    )
    return jax.shard_map(
        shards,
        mesh=grid,
        in_specs=placed,
        out_specs=(
            P(WIDE, None),
            P(WIDE, None),
            P(None, WIDE, narrow),
            P(narrow, WIDE),
            P(None, WIDE, narrow),
            P(narrow, WIDE),
            P(None, WIDE),
        ),
        check_vma=False,
    )
```

```python
import functools
import math

import jax
import jax.numpy as jnp
from jax import lax
from jax.experimental import pallas as pl
from jax.experimental.pallas import tpu as pltpu
from jax.sharding import Mesh, PartitionSpec as P

HEADS = 12
HEAD_DIM = 64
EPS = 1e-05
F32 = jnp.float32
BF16 = jnp.bfloat16
SCALE = 1.0 / math.sqrt(HEAD_DIM)
NEG = -1e30
MESH_ID = pl.DeviceIdType.MESH
VMEM_LIMIT = 56 * 1024 * 1024


def dot(a, b):
    return lax.dot_general(a, b, (((1,), (0,)), ((), ())), preferred_element_type=F32)


def dot_nt(a, b):
    return lax.dot_general(a, b, (((1,), (1,)), ((), ())), preferred_element_type=F32)


def dot_tn(a, b):
    return lax.dot_general(a, b, (((0,), (0,)), ((), ())), preferred_element_type=F32)


def whole(shape):
    return pl.BlockSpec(shape, lambda i, *_: (0,) * len(shape))


def head_lanes(width):
    lane = lax.broadcasted_iota(jnp.int32, (1, width), 1)
    return [(lane >= h * HEAD_DIM) & (lane < (h + 1) * HEAD_DIM) for h in range(width // HEAD_DIM)]


def fill_distance(ref):
    n = ref.shape[0]
    row = lax.broadcasted_iota(jnp.int32, (n, n), 0)
    col = lax.broadcasted_iota(jnp.int32, (n, n), 1)
    ref[...] = jnp.abs(row - col).astype(F32)


def params():
    return pltpu.CompilerParams(vmem_limit_bytes=VMEM_LIMIT, dimension_semantics=("arbitrary",))


def remote(src, dst, send, recv, axis, peer):
    return pltpu.make_async_remote_copy(src, dst, send, recv, device_id={axis: peer}, device_id_type=MESH_ID)


def standardize(value):
    center = value - jnp.mean(value, axis=1, keepdims=True)
    recip = lax.rsqrt(jnp.mean(center * center, axis=1, keepdims=True) + EPS)
    return center * recip, recip


def norm_grad(grad, normed, recip, gain):
    e = grad * gain
    inner = jnp.mean(e * normed, axis=1, keepdims=True)
    return recip * (e - jnp.mean(e, axis=1, keepdims=True) - normed * inner)


def rows_of_sums(values):
    width = values[0].shape[1]
    sums = [jnp.sum(v, axis=0, keepdims=True) for v in values]
    return jnp.concatenate(sums + [jnp.zeros((8 - len(sums), width), F32)], axis=0)


def ffn_bwd_kernel(pa, pb, normed_ref, cot, nb, up0, up1, down0, down1, a_all, b_all,
                   block_out, d2_ref, d2t_ref, dgu, dh_ref, sums_ref, outb, own_sem, ysend, yrecv):
    hidden = down0.shape[0]
    i = pl.program_id(0)
    n, tile, _ = outb.shape
    y_at, c_at = lax.axis_index("y"), lax.axis_index("core")

    @pl.when(i == 0)
    def _():
        barrier = pltpu.get_barrier_semaphore()
        pl.semaphore_signal(barrier, inc=1, device_id={"y": 1 - y_at}, device_id_type=MESH_ID)
        pl.semaphore_wait(barrier, 1)

    def own_copy(t):
        return pltpu.make_async_copy(outb.at[t], block_out.at[pl.ds((y_at * n + t) * tile, tile)], own_sem.at[t])

    def side_copy(t):
        side = tile // 2
        return remote(outb.at[t, pl.ds(c_at * side, side)], block_out.at[pl.ds((y_at * n + t) * tile + c_at * side, side)],
                      ysend.at[t], yrecv.at[t], "y", 1 - y_at)

    h = normed_ref[...] * nb[0:1] + nb[1:2]
    second = pa[...].astype(F32) + pb[...].astype(F32) + nb[5:6] + h
    normed, recip = standardize(second)
    gain = nb[3:4]
    outb[i] = (normed * gain + nb[4:5]).astype(BF16)
    own_copy(i).start()

    @pl.when(i < n - 1)
    def _():
        side_copy(i).start()

    c = cot[...].astype(F32)
    d2 = norm_grad(c, normed, recip, gain)
    d2_ref[...] = d2
    d2b = d2.astype(BF16)
    d2t_ref[...] = d2b.T
    sums = rows_of_sums([c * normed, c, d2])

    @pl.when(pl.program_id(0) == 0)
    def _():
        sums_ref[...] = sums

    @pl.when(pl.program_id(0) > 0)
    def _():
        sums_ref[...] += sums

    total = None
    step = 768
    for g, (up, down) in enumerate(((up0, down0), (up1, down1))):
        for at in range(0, hidden, step):
            cols = slice(at, at + step)
            dact = dot_nt(d2b, down[cols, :])
            dgu[g, :, cols] = (dact * a_all[g, :, cols].astype(F32)).astype(BF16)
            dgu[g, :, slice(hidden + at, hidden + at + step)] = (dact * b_all[g, :, cols].astype(F32)).astype(BF16)
        for k in range(2):
            term = dot_nt(dgu[g, :, k * hidden:(k + 1) * hidden], up[k])
            total = term if total is None else total + term
    dh_ref[...] = total.astype(BF16)

    @pl.when(i == n - 1)
    def _():
        for t in range(n):
            own_copy(t).wait()
        for t in range(n - 1):
            side_copy(t).wait()


def ffn_bwd(tile, pa, pb, normed, cot, nb, up0, up1, down0, down1, a_all, b_all):
    half, d = pa.shape
    hidden = down0.shape[0]
    n = half // tile
    row = lambda w: pl.BlockSpec((tile, w), lambda i, *_: (i, 0))
    return pl.pallas_call(
        ffn_bwd_kernel,
        grid=(n,),
        in_specs=[
            row(d), row(d), row(d),
            pl.BlockSpec((tile, d), lambda i: (lax.axis_index("y") * n + i, 0)),
            whole(nb.shape),
            whole(up0.shape), whole(up1.shape), whole(down0.shape), whole(down1.shape),
            pl.BlockSpec((2, tile, hidden), lambda i: (0, i, 0)),
            pl.BlockSpec((2, tile, hidden), lambda i: (0, i, 0)),
        ],
        out_specs=[
            pl.BlockSpec(memory_space=pl.ANY), row(d),
            pl.BlockSpec((d, tile), lambda i: (0, i)),
            pl.BlockSpec((2, tile, 2 * hidden), lambda i: (0, i, 0)), row(d), whole((8, d)),
        ],
        scratch_shapes=[
            pltpu.VMEM((n, tile, d), BF16), pltpu.SemaphoreType.DMA((n,)), pltpu.SemaphoreType.DMA((n - 1,)),
            pltpu.SemaphoreType.DMA((n - 1,)),
        ],
        out_shape=[
            jax.ShapeDtypeStruct((2 * half, d), BF16),
            jax.ShapeDtypeStruct((half, d), F32),
            jax.ShapeDtypeStruct((d, half), BF16),
            jax.ShapeDtypeStruct((2, half, 2 * hidden), BF16),
            jax.ShapeDtypeStruct((half, d), BF16),
            jax.ShapeDtypeStruct((8, d), F32),
        ],
        compiler_params=pltpu.CompilerParams(
            vmem_limit_bytes=VMEM_LIMIT, dimension_semantics=("arbitrary",), collective_id=2, has_side_effects=True
        ),
        cost_estimate=pl.CostEstimate(
            flops=12 * half * d * hidden, bytes_accessed=half * d * 20 + half * hidden * 16 + 12 * d * hidden,
            transcendentals=half,
        ),
        name="ffn_bwd",
    )(pa, pb, normed, cot, nb, up0, up1, down0, down1, a_all, b_all)


def attn_bwd_kernel(info, slopes, x_ref, d2_ref, ha, hb, normed_ref, recip_ref, nb, wqkv0, wqkv1, wout0, wout1,
                    proj_all, att_all, lse_all,
                    d1_ref, part, grad0, grad1, sums_ref, dist, sum0, sum1):
    step = pl.program_id(0)
    win = d2_ref.shape[0]
    width = wout0.shape[0]
    heads = width // HEAD_DIM

    @pl.when(step == 0)
    def _():
        fill_distance(dist)

    normed = normed_ref[...]
    dh = d2_ref[...] + (ha[...].astype(F32) + hb[...].astype(F32))
    d1 = norm_grad(dh, normed, recip_ref[:, 0:1], nb[0:1])
    d1_ref[...] = d1
    d1b = d1.astype(BF16)
    x = x_ref[...]
    sums = rows_of_sums([dh * normed, dh, d1])

    @pl.when(step == 0)
    def _():
        sums_ref[...] = sums

    @pl.when(step > 0)
    def _():
        sums_ref[...] += sums

    limit = info[1 + info[0] * pl.num_programs(0) + step]
    lanes = head_lanes(width)
    key_on = lax.broadcasted_iota(jnp.int32, (win, 1), 0) < limit
    stat_lane = lax.broadcasted_iota(jnp.int32, (1, 128), 1)
    total = None
    for g, (wqkv, wout, acc) in enumerate(((wqkv0, wout0, sum0), (wqkv1, wout1, sum1))):
        q, k, v = proj_all[g, 0], proj_all[g, 1], proj_all[g, 2]
        datt = dot_nt(d1b, wout[...]).astype(BF16)
        product = datt.astype(F32) * att_all[g].astype(F32)
        stat = jnp.zeros((win, 128), F32)
        for h in range(heads):
            inner = jnp.sum(jnp.where(lanes[h], product, 0.0), axis=1, keepdims=True)
            stat = jnp.where(stat_lane == h, inner, stat)
        inner_rows = stat.T[0:8]
        qs = q * jnp.asarray(SCALE, BF16)
        dq = jnp.zeros((win, width), F32)
        dk = jnp.zeros((win, width), F32)
        dv = jnp.zeros((win, width), F32)
        for h in range(heads):
            qh = jnp.where(lanes[h], qs, jnp.zeros_like(qs))
            oh = jnp.where(lanes[h], datt, jnp.zeros_like(datt))
            s = dot_nt(k, qh) - slopes[g * heads + h] * dist[...]
            s = jnp.where(key_on, s, NEG)
            p = jnp.exp(s - lse_all[g, 0, h:h + 1, :])
            dp = dot_nt(v, oh)
            ds = (p * (dp - inner_rows[h:h + 1, :])).astype(BF16)
            dv = jnp.where(lanes[h], dot(p.astype(BF16), datt), dv)
            dk = jnp.where(lanes[h], dot(ds, q), dk)
            dq = jnp.where(lanes[h], dot_tn(ds, k), dq)
        dqb = (dq * SCALE).astype(BF16)
        dkb = (dk * SCALE).astype(BF16)
        dvb = dv.astype(BF16)
        terms = [dot_tn(x, dqb), dot_tn(x, dkb), dot_tn(x, dvb), dot_tn(d1b, att_all[g])]

        @pl.when(step == 0)
        def _():
            for i in range(4):
                acc[i] = terms[i]

        @pl.when(step > 0)
        def _():
            for i in range(4):
                acc[i] += terms[i]

        term = dot(dqb, wqkv[0]) + dot(dkb, wqkv[1]) + dot(dvb, wqkv[2])
        total = term if total is None else total + term
    part[...] = total.astype(BF16)

    @pl.when(step == pl.num_programs(0) - 1)
    def _():
        for acc, grad in ((sum0, grad0), (sum1, grad1)):
            for i in range(4):
                grad[:, i * width:(i + 1) * width] = acc[i].astype(BF16)


def attn_bwd(info, slopes, tokens, d2, ha, hb, normed, recip, nb, wqkv0, wqkv1, wout0, wout1,
             proj, att, lse):
    half, d = d2.shape
    width = wout0.shape[0]
    _, nwin, _, win = lse.shape
    heads = 2 * width // HEAD_DIM
    row = lambda w: pl.BlockSpec((win, w), lambda i, *_: (i, 0))
    return pl.pallas_call(
        attn_bwd_kernel,
        grid_spec=pltpu.PrefetchScalarGridSpec(
            num_scalar_prefetch=2,
            grid=(nwin,),
            in_specs=[
                pl.BlockSpec((win, d), lambda i, info, sl: (info[0] * nwin + i, 0)),
                row(d), row(d), row(d), row(d), row(128), whole(nb.shape),
                whole(wqkv0.shape), whole(wqkv1.shape), whole(wout0.shape), whole(wout1.shape),
                pl.BlockSpec((2, 3, win, width), lambda i, *_: (0, 0, i, 0)),
                pl.BlockSpec((2, win, width), lambda i, *_: (0, i, 0)),
                pl.BlockSpec((2, 1, 8, win), lambda i, *_: (0, i, 0, 0)),
            ],
            out_specs=[row(d), row(d), whole((d, 4 * width)), whole((d, 4 * width)), whole((8, d))],
            scratch_shapes=[pltpu.VMEM((win, win), F32), pltpu.VMEM((4, d, width), F32), pltpu.VMEM((4, d, width), F32)],
        ),
        out_shape=[
            jax.ShapeDtypeStruct((half, d), F32),
            jax.ShapeDtypeStruct((half, d), BF16),
            jax.ShapeDtypeStruct((d, 4 * width), BF16),
            jax.ShapeDtypeStruct((d, 4 * width), BF16),
            jax.ShapeDtypeStruct((8, d), F32),
        ],
        compiler_params=params(),
        cost_estimate=pl.CostEstimate(
            flops=2 * half * d * width * 16 + 10 * nwin * heads * win * win * 256,
            bytes_accessed=half * d * 20 + half * width * 32 + d * width * 16,
            transcendentals=nwin * heads * win * win,
        ),
        name="attn_bwd",
    )(info, slopes, tokens, d2, ha, hb, normed, recip, nb, wqkv0, wqkv1, wout0, wout1,
      proj, att, lse)


def place_kernel(order, mine, near, far, out):
    step = pl.program_id(0)

    @pl.when(step < 2)
    def _():
        out[...] = mine[...].astype(out.dtype)

    @pl.when(step == 2)
    def _():
        out[...] = near[...].astype(out.dtype)

    @pl.when(step == 3)
    def _():
        out[...] = far[...].astype(out.dtype)


def place(order, mine, near, far, dtype):
    quarter, d = near.shape
    return pl.pallas_call(
        place_kernel,
        grid_spec=pltpu.PrefetchScalarGridSpec(
            num_scalar_prefetch=1,
            grid=(4,),
            in_specs=[
                pl.BlockSpec((quarter, d), lambda i, o: (jnp.minimum(i, 1), 0)),
                whole((quarter, d)),
                whole((quarter, d)),
            ],
            out_specs=pl.BlockSpec((quarter, d), lambda i, o: (o[i], 0)),
        ),
        out_shape=jax.ShapeDtypeStruct((4 * quarter, d), dtype),
        compiler_params=params(),
        cost_estimate=pl.CostEstimate(flops=0, bytes_accessed=24 * quarter * d, transcendentals=0),
        name="place",
    )(order, mine, near, far)


TILE = 256


def forward_kernel(info, slopes, nb, tokens, wqkv, wout, up, down,
                   proj_out, att_out, lse_out, normed_out, recip_out, ht_out, a_out, b_out, act_out, fown_out, frecv_out,
                   wqkv1_out, wout1_out, up1_out, down1_out,
                   xbuf, wqv, wov, upv, downv, projb, attb, lseb, pown, precv, normedb, recipb, hbuf, htb, ab, bb, actb,
                   facc, fown, dist,
                   load_sem, ysend, yrecv, xsend, xrecv, zsend, zrecv, psend, prem, fsend, frem, out_sem, pout_sem, tout_sem, fout_sem):
    wo_at, x_at, y_at, c_at = (lax.axis_index(n) for n in ("wo", "x", "y", "core"))
    nwin, _, win = lse_out.shape[1:]
    half, d = xbuf.shape
    width = wout.shape[0]
    hidden = down.shape[0]
    heads = width // HEAD_DIM
    tiles = half // TILE
    z_at = wo_at % 2
    z_peer = wo_at + 1 - 2 * z_at

    barrier = pltpu.get_barrier_semaphore()
    for axis, to in (("x", 1 - x_at), ("y", 1 - y_at), ("core", 1 - c_at), ("wo", z_peer)):
        pl.semaphore_signal(barrier, inc=1, device_id={axis: to}, device_id_type=MESH_ID)
    pl.semaphore_wait(barrier, 4)

    def quarter(i, q):
        if i == 0:
            return wqkv.at[:, pl.ds(q * (width // 4), width // 4)], wqv.at[1, :, pl.ds(q * (width // 4), width // 4)]
        if i == 1:
            return wout.at[pl.ds(q * (width // 4), width // 4)], wov.at[1, pl.ds(q * (width // 4), width // 4)]
        if i == 2:
            return up.at[:, pl.ds(q * (d // 4), d // 4)], upv.at[1, :, pl.ds(q * (d // 4), d // 4)]
        return down.at[pl.ds(q * (hidden // 4), hidden // 4)], downv.at[1, pl.ds(q * (hidden // 4), hidden // 4)]

    def eighth(i, q, e):
        if i == 0:
            return wqv.at[1, :, pl.ds(q * (width // 4), width // 4), e * (d // 2):(e + 1) * (d // 2)]
        if i == 1:
            return wov.at[1, pl.ds(q * (width // 4), width // 4), e * (d // 2):(e + 1) * (d // 2)]
        if i == 2:
            return upv.at[1, :, pl.ds(q * (d // 4) + e * (d // 8), d // 8)]
        return downv.at[1, pl.ds(q * (hidden // 4) + e * (hidden // 8), hidden // 8)]

    here = 2 * x_at + z_at
    across_x = 2 * (1 - x_at) + z_at
    across_z = 2 * x_at + 1 - z_at

    def over_y(i):
        src, dst = quarter(i, here)
        return remote(src, dst, ysend.at[i], yrecv.at[i], "y", 1 - y_at)

    def level_one(i):
        _, ref = quarter(i, here)
        return (remote(ref, ref, xsend.at[0, i], xrecv.at[0, i], "x", 1 - x_at),
                remote(ref, ref, zsend.at[0, i], zrecv.at[0, i], "wo", z_peer))

    def level_two(i):
        from_z, from_x = eighth(i, across_z, 0), eighth(i, across_x, 1)
        return (remote(from_z, from_z, xsend.at[1, i], xrecv.at[1, i], "x", 1 - x_at),
                remote(from_x, from_x, zsend.at[1, i], zrecv.at[1, i], "wo", z_peer))

    def launch(copies):
        for copy in copies:
            copy.start()

    def arrive(copies):
        for copy in copies:
            copy.wait_recv()

    loads = [
        pltpu.make_async_copy(tokens.at[pl.ds(y_at * half, half)], xbuf, load_sem.at[0]),
        pltpu.make_async_copy(wqkv, wqv.at[0], load_sem.at[1]),
        pltpu.make_async_copy(wout, wov.at[0], load_sem.at[2]),
        pltpu.make_async_copy(up, upv.at[0], load_sem.at[3]),
        pltpu.make_async_copy(down, downv.at[0], load_sem.at[4]),
    ]
    over_y(0).start()
    over_y(1).start()
    for load in loads:
        load.start()
    fill_distance(dist)
    lanes = head_lanes(width)
    stat_lane = lax.broadcasted_iota(jnp.int32, (1, 128), 1)
    key_at = lax.broadcasted_iota(jnp.int32, (1, win), 1)
    for load in loads[:3]:
        load.wait()

    def part_copy(w):
        rows = pl.ds(w * win, win)
        return remote(pown.at[rows], precv.at[rows], psend.at[w], prem.at[w], "core", 1 - c_at)

    def proj_copy(t):
        g, rows = t // nwin, pl.ds((t % nwin) * win, win)
        return (
            pltpu.make_async_copy(projb.at[g, :, rows], proj_out.at[g, :, rows], pout_sem.at[0, t]),
            pltpu.make_async_copy(attb.at[g, rows], att_out.at[g, rows], pout_sem.at[1, t]),
        )

    def attention(t, carry):
        g, w = t // nwin, t % nwin
        start = w * win
        x = xbuf[pl.ds(start, win)]
        q = dot_nt(x, wqv[g, 0]).astype(BF16)
        k = dot_nt(x, wqv[g, 1]).astype(BF16)
        v = dot_nt(x, wqv[g, 2]).astype(BF16)
        projb[g, 0, pl.ds(start, win)] = q
        projb[g, 1, pl.ds(start, win)] = k
        projb[g, 2, pl.ds(start, win)] = v
        key_on = key_at < info[y_at * nwin + w]
        rows = win // 2
        for b in range(2):
            at = slice(b * rows, (b + 1) * rows)
            qb = q[at] * jnp.asarray(SCALE, BF16)
            att = jnp.zeros((rows, width), F32)
            stat = jnp.zeros((rows, 128), F32)
            for h in range(heads):
                qh = jnp.where(lanes[h], qb, jnp.zeros_like(qb))
                s = dot_nt(qh, k) - slopes[g * heads + h] * dist[at]
                s = jnp.where(key_on, s, NEG)
                top = jnp.max(s, axis=1, keepdims=True)
                p = jnp.exp(s - top)
                total = jnp.sum(p, axis=1, keepdims=True)
                o = dot(p.astype(BF16), v) * (1.0 / total)
                att = jnp.where(lanes[h], o, att)
                stat = jnp.where(stat_lane == h, top + jnp.log(total), stat)
            attb[g, pl.ds(start + b * rows, rows)] = att.astype(BF16)
            lseb[g, w, :, at] = stat.T[0:8]
        for copy in proj_copy(t):
            copy.start()

        @pl.when(t >= nwin)
        def _():
            out = dot(attb[0, pl.ds(start, win)], wov[0]) + dot(attb[1, pl.ds(start, win)], wov[1])
            pown[pl.ds(start, win)] = out.astype(BF16)
            part_copy(w).start()

        @pl.when(t == 0)
        def _():
            for i in range(2):
                over_y(i).wait_recv()
                launch(level_one(i))
            over_y(2).start()

        @pl.when(t == nwin - 1)
        def _():
            over_y(3).start()
            for i in range(2):
                arrive(level_one(i))
                launch(level_two(i))
            for i in range(2):
                arrive(level_two(i))

        @pl.when(t == nwin)
        def _():
            over_y(2).wait_recv()
            launch(level_one(2))

        return carry

    lax.fori_loop(0, 2 * nwin, attention, 0)
    lse_copy = pltpu.make_async_copy(lseb, lse_out, out_sem.at[0])
    lse_copy.start()
    loads[3].wait()
    loads[4].wait()
    step = 256

    def hidden_units(g, start, hb):
        for at in range(0, hidden, step):
            cols = slice(at, at + step)
            gate = dot(hb, upv[g, 0, :, cols])
            lift = dot(hb, upv[g, 1, :, cols])
            cdf = 0.5 * (1.0 + lax.erf(gate * (1.0 / math.sqrt(2.0))))
            pdf = jnp.exp(-0.5 * gate * gate) * (1.0 / math.sqrt(2.0 * math.pi))
            gelu = gate * cdf
            rows = pl.ds(start, TILE)
            ab[g, rows, cols] = (lift * (cdf + gate * pdf)).astype(BF16)
            bb[g, rows, cols] = gelu.astype(BF16)
            actb[g, rows, cols] = (gelu * lift).astype(BF16)

    def tile_copies(t):
        g, rows = t // tiles, pl.ds((t % tiles) * TILE, TILE)
        return [
            pltpu.make_async_copy(b.at[g, rows], o.at[g, rows], tout_sem.at[i, t])
            for i, (b, o) in enumerate(((ab, a_out), (bb, b_out), (actb, act_out)))
        ]

    def norm_copies(i):
        rows = pl.ds(pl.multiple_of(i * TILE, TILE), TILE)
        return [
            pltpu.make_async_copy(b.at[rows], o.at[rows], fout_sem.at[n, i])
            for n, (b, o) in enumerate(((normedb, normed_out), (recipb, recip_out)))
        ] + [pltpu.make_async_copy(htb.at[:, rows], ht_out.at[:, rows], fout_sem.at[2, i])]

    def first(i, carry):
        start = i * TILE

        @pl.when(i % (win // TILE) == 0)
        def _():
            part_copy(i // (win // TILE)).wait_recv()

        rows = pl.ds(start, TILE)
        value = (pown[rows].astype(F32) + precv[rows].astype(F32)) + nb[2:3] + xbuf[rows].astype(F32)
        normed, recip = standardize(value)
        normedb[rows] = normed
        recipb[rows] = jnp.broadcast_to(recip, (TILE, 128))
        hb = (normed * nb[0:1] + nb[1:2]).astype(BF16)
        hbuf[rows] = hb
        htb[:, pl.ds(pl.multiple_of(start, TILE), TILE)] = hb.T
        hidden_units(0, start, hb)
        facc[rows] = dot(actb[0, rows], downv[0])
        for copy in tile_copies(i) + norm_copies(i):
            copy.start()

        @pl.when(i == tiles // 2 - 1)
        def _():
            arrive(level_one(2))
            launch(level_two(2))
            over_y(3).wait_recv()
            launch(level_one(3))

        return carry

    lax.fori_loop(0, tiles, first, 0)
    arrive(level_two(2))

    def second(i, carry):
        start = i * TILE
        hidden_units(1, start, hbuf[pl.ds(start, TILE)])
        for copy in tile_copies(tiles + i):
            copy.start()

        @pl.when(i == tiles - 2)
        def _():
            arrive(level_one(3))
            launch(level_two(3))

        return carry

    lax.fori_loop(0, tiles, second, 0)
    arrive(level_two(3))

    def final_copy(i):
        rows = pl.ds(i * TILE, TILE)
        return (
            remote(fown.at[rows], frecv_out.at[rows], fsend.at[i], frem.at[i], "core", 1 - c_at),
            pltpu.make_async_copy(fown.at[rows], fown_out.at[rows], fout_sem.at[3, i]),
        )

    def third(i, carry):
        rows = pl.ds(i * TILE, TILE)
        fown[rows] = (facc[rows] + dot(actb[1, rows], downv[1])).astype(BF16)
        for copy in final_copy(i):
            copy.start()
        return carry

    weights_out = [
        pltpu.make_async_copy(wqv.at[1], wqkv1_out, out_sem.at[1]),
        pltpu.make_async_copy(wov.at[1], wout1_out, out_sem.at[2]),
        pltpu.make_async_copy(upv.at[1], up1_out, out_sem.at[3]),
        pltpu.make_async_copy(downv.at[1], down1_out, out_sem.at[4]),
    ]
    for copy in weights_out:
        copy.start()
    lax.fori_loop(0, tiles, third, 0)

    def finish(i, carry):
        sent, kept = final_copy(i)
        sent.wait_recv()
        sent.wait_send()
        kept.wait()
        for copy in norm_copies(i):
            copy.wait()
        return carry

    lax.fori_loop(0, tiles, finish, 0)

    def drain_tiles(t, carry):
        for copy in tile_copies(t):
            copy.wait()
        return carry

    lax.fori_loop(0, 2 * tiles, drain_tiles, 0)

    def drain_proj(t, carry):
        for copy in proj_copy(t):
            copy.wait()
        return carry

    lax.fori_loop(0, 2 * nwin, drain_proj, 0)

    def drain_part(w, carry):
        part_copy(w).wait_send()
        return carry

    lax.fori_loop(0, nwin, drain_part, 0)
    lse_copy.wait()
    for copy in weights_out:
        copy.wait()
    for i in range(4):
        over_y(i).wait_send()
        for copy in level_one(i) + level_two(i):
            copy.wait_send()


def forward(lengths, slopes, nb, tokens, wqkv, wout, up, down):
    d = tokens.shape[1]
    nwin = lengths.shape[0] // 2
    half = tokens.shape[0] // 2
    win = half // nwin
    width, hidden = wout.shape[0], down.shape[0]
    tiles = half // TILE
    heads = width // HEAD_DIM
    smem = pl.BlockSpec(memory_space=pltpu.SMEM)
    vmem = pl.BlockSpec(memory_space=pltpu.VMEM)
    hbm = pl.BlockSpec(memory_space=pl.ANY)
    acts = [((2, half, hidden), BF16)] * 3
    outs = [
        ((2, 3, half, width), BF16), ((2, half, width), BF16), ((2, nwin, 8, win), F32),
        ((half, d), F32), ((half, 128), F32), ((d, half), BF16), *acts,
        ((half, d), BF16), ((half, d), BF16),
        (wqkv.shape, BF16), (wout.shape, BF16), (up.shape, BF16), (down.shape, BF16),
    ]
    bufs = [
        ((half, d), BF16), ((2,) + wqkv.shape, BF16), ((2,) + wout.shape, BF16), ((2,) + up.shape, BF16),
        ((2,) + down.shape, BF16), ((2, 3, half, width), BF16), ((2, half, width), BF16), ((2, nwin, 8, win), F32),
        ((half, d), BF16), ((half, d), BF16), ((half, d), F32), ((half, 128), F32), ((half, d), BF16), ((d, half), BF16), *acts,
        ((half, d), F32), ((half, d), BF16), ((win, win), F32),
    ]
    sems = [(5,), (4,), (4,), (2, 4), (2, 4), (2, 4), (2, 4), (nwin,), (nwin,), (tiles,), (tiles,), (5,), (2, 2 * nwin), (3, 2 * tiles), (5, tiles)]
    return pl.pallas_call(
        forward_kernel,
        in_specs=[smem, smem, vmem] + [hbm] * 5,
        out_specs=[hbm] * len(outs),
        out_shape=[jax.ShapeDtypeStruct(*o) for o in outs],
        scratch_shapes=[pltpu.VMEM(*b) for b in bufs] + [pltpu.SemaphoreType.DMA(n) for n in sems],
        compiler_params=pltpu.CompilerParams(vmem_limit_bytes=62 * 1024 * 1024, collective_id=0, has_side_effects=True),
        cost_estimate=pl.CostEstimate(
            flops=2 * half * d * width * 16 + 12 * half * d * hidden + 8 * nwin * heads * win * win * 256,
            bytes_accessed=half * d * 30 + half * hidden * 12, transcendentals=half * hidden * 4,
        ),
        name="forward",
    )(lengths, slopes, nb, tokens, wqkv, wout, up, down)


BLOCK = 128
PAIR = 2 * BLOCK
FLIGHT = 4
TAIL_FLIGHT = 3


def backward_kernel(lengths, slopes, nb, sums2, tokens, d2_in, dh_in, normed_in, recip_in, wqkv, wqkv1, wout, wout1,
                    proj_in, att_in, lse_in, dgu_in, act_in, ht_in, d2t_in, half_in,
                    share, total_sums, block_out, input_grad,
                    gbuf, r1, r2, zr, dhr, dhw, normw, d2w, recw, xw, projw, attw, lsev, wqv, wov, ipown, iprecv, totb,
                    sumb, sumr, sumz, sum1,
                    g1s, g1r, g2s, g2r, zs, zrs, pre_sem, win_sem, w_sem, dh_s, dh_r, ip_s, ip_r,
                    tot_sem, iy_s, iy_r, ic_s, ic_r, bo_s, bo_r, sm_s, sm_r, smz_s, smz_r, ring_sem, t_sem):
    at = {n: lax.axis_index(n) for n in ("wo", "x", "y", "core")}
    wo_at, x_at, y_at, c_at = at["wo"], at["x"], at["y"], at["core"]
    n_wo = gbuf.shape[3]
    blocks = gbuf.shape[0]
    own_rows = gbuf.shape[4]
    half, d = normed_in.shape
    _, nwin, _, win = lse_in.shape
    width = wout.shape[0]
    hidden = act_in.shape[2]
    heads = width // HEAD_DIM
    ffn_blocks = 3 * hidden // BLOCK

    barrier = pltpu.get_barrier_semaphore()
    for axis in ("x", "y", "core"):
        pl.semaphore_signal(barrier, inc=1, device_id={axis: 1 - at[axis]}, device_id_type=MESH_ID)
    for k in range(n_wo - 1):
        pl.semaphore_signal(barrier, inc=1, device_id={"wo": (wo_at + k + 1) % n_wo}, device_id_type=MESH_ID)
    pl.semaphore_wait(barrier, n_wo + 2)

    def copy_one(b, is_y):
        send = 1 if is_y else 1 - x_at
        axis = "y" if is_y else "x"
        return remote(gbuf.at[b, send], r1.at[b], g1s.at[b], g1r.at[b], axis, 1 - at[axis])

    def copy_two(b, is_y):
        keep = 0 if is_y else x_at
        send = 1 - x_at if is_y else 1
        axis = "x" if is_y else "y"
        return remote(gbuf.at[b, keep, send], r2.at[b], g2s.at[b], g2r.at[b], axis, 1 - at[axis])

    def copy_z(b, is_y, k):
        keep = 0 if is_y else x_at
        keep2 = x_at if is_y else 0
        to = (wo_at + k + 1) % n_wo
        return remote(gbuf.at[b, keep, keep2, to], zr.at[b, k], zs.at[b, k], zrs.at[b, k], "wo", to)

    def by_kind(b, f):
        @pl.when(b % 3 == 1)
        def _():
            f(True)

        @pl.when(b % 3 != 1)
        def _():
            f(False)

    def stage_one(b):
        copy_one(b, False).wait_recv()

        def go(is_y):
            keep = 0 if is_y else x_at
            gbuf[b, keep] = (gbuf[b, keep].astype(F32) + r1[b].astype(F32)).astype(BF16)
            copy_two(b, is_y).start()

        by_kind(b, go)

        @pl.when(b + FLIGHT < ffn_blocks)
        def _():
            by_kind(b + FLIGHT, lambda is_y: copy_one(b + FLIGHT, is_y).start())

        @pl.when((b >= ffn_blocks) & (b + TAIL_FLIGHT < blocks))
        def _():
            by_kind(b + TAIL_FLIGHT, lambda is_y: copy_one(b + TAIL_FLIGHT, is_y).start())

    def stage_two(b):
        copy_two(b, False).wait_recv()

        def go(is_y):
            keep = 0 if is_y else x_at
            keep2 = x_at if is_y else 0
            gbuf[b, keep, keep2] = (gbuf[b, keep, keep2].astype(F32) + r2[b].astype(F32)).astype(BF16)
            for k in range(n_wo - 1):
                copy_z(b, is_y, k).start()

        by_kind(b, go)

    def stage_three(b):
        for k in range(n_wo - 1):
            copy_z(b, False, k).wait_recv()

        def go(is_y):
            keep = 0 if is_y else x_at
            keep2 = x_at if is_y else 0
            total = gbuf[b, keep, keep2, wo_at].astype(F32)
            for k in range(n_wo - 1):
                total = total + zr[b, k].astype(F32)
            share[b] = total

        by_kind(b, go)

    def advance(k):
        for j in (2 * k, 2 * k + 1):
            stage_one(j)

            @pl.when(k >= 2)
            def _():
                stage_two(j - 4)

            @pl.when(k >= 4)
            def _():
                stage_three(j - 8)

    def put(b, g, value):
        r = b % 3
        is_y = r * (2 - r)
        for j in range(2 * n_wo):
            px, w = j % 2, j // 2
            outer = g * is_y + px * (1 - is_y)
            gbuf[b, outer, g + px - outer, w] = value[j * own_rows:(j + 1) * own_rows].astype(BF16)

    def pre_loads(w):
        rows = pl.ds(w * win, win)
        return [
            pltpu.make_async_copy(src, dst, pre_sem.at[i])
            for i, (src, dst) in enumerate((
                (normed_in.at[rows], normw), (d2_in.at[rows], d2w), (recip_in.at[rows], recw), (dh_in.at[rows], dhw),
                (tokens.at[pl.ds(y_at * half + w * win, win)], xw),
            ))
        ]

    def win_loads(w):
        rows, slot = pl.ds(w * win, win), w % 2
        return [
            pltpu.make_async_copy(proj_in.at[:, :, rows], projw.at[slot], win_sem.at[0, slot]),
            pltpu.make_async_copy(att_in.at[:, rows], attw.at[slot], win_sem.at[1, slot]),
        ]

    dh_copy = remote(dh_in, dhr, dh_s.at[0], dh_r.at[0], "core", 1 - c_at)
    side = win // 2
    last_rows = pl.ds(y_at * half + (nwin - 1) * win + c_at * side, side)
    out_y = remote(block_out.at[last_rows], block_out.at[last_rows], bo_s.at[nwin], bo_r.at[nwin], "y", 1 - y_at)

    def out_c(w):
        rows = pl.ds((1 - y_at) * half + w * win + c_at * side, side)
        return remote(block_out.at[rows], block_out.at[rows], bo_s.at[w], bo_r.at[w], "core", 1 - c_at)

    loads = [
        pltpu.make_async_copy(src, dst, w_sem.at[i])
        for i, (src, dst) in enumerate((
            (wqkv, wqv.at[0]), (wqkv1, wqv.at[1]), (wout, wov.at[0]), (wout1, wov.at[1]), (lse_in, lsev),
        ))
    ]

    def ffn_grads(ring, lhs_d, lhs_h):
        lhs = [pltpu.make_async_copy(d2t_in, lhs_d, t_sem.at[0]), pltpu.make_async_copy(ht_in, lhs_h, t_sem.at[1])]
        down_pairs = hidden // PAIR
        up_pairs = 2 * hidden // PAIR

        def fetch(src, b, g):
            return pltpu.make_async_copy(src.at[g, :, pl.ds(pl.multiple_of(b * PAIR, PAIR), PAIR)],
                                         ring.at[b % 2, :, g * PAIR:(g + 1) * PAIR], ring_sem.at[b % 2, g])

        def run(src, left, count, first):
            for g in range(2):
                fetch(src, 0, g).start()

            def one(b, carry):
                @pl.when(b + 1 < count)
                def _():
                    for g in range(2):
                        fetch(src, b + 1, g).start()

                for g in range(2):
                    fetch(src, b, g).wait()
                value = dot(left[...], ring[b % 2]).astype(BF16)
                k = b + first
                for side in range(2):
                    for g in range(2):
                        at = g * PAIR + side * BLOCK
                        put(2 * k + side, g, value[:, at:at + BLOCK])

                    @pl.when(2 * k + side < FLIGHT)
                    def _():
                        by_kind(2 * k + side, lambda is_y: copy_one(2 * k + side, is_y).start())

                @pl.when((k >= 4) & (k % 2 == 0))
                def _():
                    advance((k - 4) // 2)

                return carry

            lax.fori_loop(0, count, one, 0)

        lhs[0].start()
        dh_copy.start()
        out_y.start()
        for w in range(nwin - 1):
            out_c(w).start()
        lhs[1].start()
        for copy in loads + pre_loads(0) + win_loads(0):
            copy.start()
        lhs[0].wait()
        run(act_in, lhs_d, down_pairs, 0)
        lhs[1].wait()
        run(dgu_in, lhs_h, up_pairs, down_pairs)

    pl.run_scoped(ffn_grads, pltpu.VMEM((2, half, 2 * PAIR), BF16), pltpu.VMEM((d, half), BF16), pltpu.VMEM((d, half), BF16))

    for load in loads:
        load.wait()
    dh_copy.wait_recv()
    lanes = head_lanes(width)
    stat_lane = lax.broadcasted_iota(jnp.int32, (1, 128), 1)

    def part_copy(w):
        return remote(ipown.at[w], iprecv.at[w], ip_s.at[w], ip_r.at[w], "core", 1 - c_at)

    def own_copy(w):
        return pltpu.make_async_copy(totb.at[w], input_grad.at[pl.ds(y_at * half + w * win, win)], tot_sem.at[w])

    def in_y(w):
        return remote(totb.at[w, pl.ds(c_at * side, side)], input_grad.at[pl.ds(y_at * half + w * win + c_at * side, side)],
                      iy_s.at[w], iy_r.at[w], "y", 1 - y_at)

    def in_c(w):
        rows = pl.ds((1 - y_at) * half + w * win + c_at * side, side)
        return remote(input_grad.at[rows], input_grad.at[rows], ic_s.at[w], ic_r.at[w], "core", 1 - c_at)

    def attention(acc, xt, d1t, d1b, d1w, iptot, dist, stage):
        fill_distance(dist)
        acc[...] = jnp.zeros_like(acc)
        sum1[...] = jnp.zeros_like(sum1)

        def send_total(w):
            part_copy(w).wait_recv()
            value = d1w[w % 2] + (ipown[w].astype(F32) + iprecv[w].astype(F32))
            totb[w] = value.astype(BF16)
            own_copy(w).start()
            in_y(w).start()

        def step(t, carry):
            w, g = t // 2, t % 2
            slot = w % 2

            @pl.when(g == 0)
            def _():
                for copy in pre_loads(w) + win_loads(w):
                    copy.wait()
                normed = normw[...]
                dh = d2w[...] + (dhw[...].astype(F32) + dhr[pl.ds(w * win, win)].astype(F32))
                d1 = norm_grad(dh, normed, recw[:, 0:1], nb[0:1])
                d1w[slot] = d1
                low = d1.astype(BF16)
                d1b[...] = low
                d1t[...] = low.T
                xt[...] = xw[...].T
                sum1[...] += rows_of_sums([dh * normed, dh, d1])

                @pl.when(w + 1 < nwin)
                def _():
                    for copy in pre_loads(w + 1) + win_loads(w + 1):
                        copy.start()

            q, k, v = projw[slot, g, 0], projw[slot, g, 1], projw[slot, g, 2]
            att = attw[slot, g]
            datt = dot_nt(d1b[...], wov[g]).astype(BF16)
            product = datt.astype(F32) * att.astype(F32)
            stat = jnp.zeros((win, 128), F32)
            for h in range(heads):
                inner = jnp.sum(jnp.where(lanes[h], product, 0.0), axis=1, keepdims=True)
                stat = jnp.where(stat_lane == h, inner, stat)
            inner_rows = stat.T[0:8]
            qs = q * jnp.asarray(SCALE, BF16)
            dq = jnp.zeros((win, width), F32)
            dks, dvs = [], []
            half_keys = win // 2
            limit = lengths[y_at * nwin + w]
            for kb in range(2):
                keys = slice(kb * half_keys, (kb + 1) * half_keys)
                kk, vk = k[keys], v[keys]
                key_on = lax.broadcasted_iota(jnp.int32, (half_keys, 1), 0) + kb * half_keys < limit
                dk = jnp.zeros((half_keys, width), F32)
                dv = jnp.zeros((half_keys, width), F32)
                for h in range(heads):
                    qh = jnp.where(lanes[h], qs, jnp.zeros_like(qs))
                    oh = jnp.where(lanes[h], datt, jnp.zeros_like(datt))
                    s = dot_nt(kk, qh) - slopes[g * heads + h] * dist[keys]
                    s = jnp.where(key_on, s, NEG)
                    p = jnp.exp(s - lsev[g, w, h:h + 1, :])
                    dp = dot_nt(vk, oh)
                    ds = (p * (dp - inner_rows[h:h + 1, :])).astype(BF16)
                    dv = jnp.where(lanes[h], dot(p.astype(BF16), datt), dv)
                    dk = jnp.where(lanes[h], dot(ds, q), dk)
                    dq = dq + jnp.where(lanes[h], dot_tn(ds, kk), 0.0)
                dks.append((dk * SCALE).astype(BF16))
                dvs.append(dv.astype(BF16))
            dqb = (dq * SCALE).astype(BF16)
            dkb = jnp.concatenate(dks, axis=0)
            dvb = jnp.concatenate(dvs, axis=0)
            acc[g, 0] += dot(xt[...], dqb)
            acc[g, 1] += dot(xt[...], dkb)
            acc[g, 2] += dot(xt[...], dvb)
            acc[g, 3] += dot(d1t[...], att)
            term = dot(dqb, wqv[g, 0]) + dot(dkb, wqv[g, 1]) + dot(dvb, wqv[g, 2])

            @pl.when(g == 0)
            def _():
                iptot[...] = term

            @pl.when(g == 1)
            def _():
                ipown[w] = (iptot[...] + term).astype(BF16)
                part_copy(w).start()

            @pl.when((g == 0) & (w > 0))
            def _():
                send_total(w - 1)

            @pl.when(t == 0)
            def _():
                advance(3)

            @pl.when(t == 1)
            def _():
                advance(4)

            @pl.when((t > 0) & (t < 2 * nwin - 1))
            def _():
                advance(t + 4)

            @pl.when(t == 2 * nwin - 1)
            def _():
                for b in (ffn_blocks - 4, ffn_blocks - 3):
                    stage_two(b)
                    stage_three(b - 4)


            @pl.when(t == 3)
            def _():
                out_y.wait_recv()
                out_c(nwin - 1).start()

            return carry

        lax.fori_loop(0, 2 * nwin, step, 0)

        first = blocks - 4 * width // BLOCK
        for g in range(2):
            for i in range(4):
                stage[:, i * width:(i + 1) * width] = acc[g, i].astype(BF16)
            for i in range(4 * width // BLOCK):
                put(first + i, g, stage[:, i * BLOCK:(i + 1) * BLOCK])
        for i in range(first, first + TAIL_FLIGHT):
            copy_one(i, i % 3 == 1).start()
        for b in (ffn_blocks - 2, ffn_blocks - 1):
            stage_two(b)

        def rest(b, carry):
            stage_three(b)
            return carry

        lax.fori_loop(ffn_blocks - 6, ffn_blocks, rest, 0)
        for w in range(nwin - 1):
            in_y(w).wait_recv()
            in_c(w).start()
        stage_one(first)
        stage_one(first + 1)
        send_total(nwin - 1)

    pl.run_scoped(
        attention,
        pltpu.VMEM((2, 4, d, width), F32), pltpu.VMEM((d, win), BF16), pltpu.VMEM((d, win), BF16), pltpu.VMEM((win, d), BF16),
        pltpu.VMEM((2, win, d), F32), pltpu.VMEM((win, d), F32), pltpu.VMEM((win, win), F32), pltpu.VMEM((d, 4 * width), BF16),
    )

    sumb[0] = jnp.concatenate([sum1[0:3], sums2[0:3], jnp.zeros((2, d), F32)], axis=0)

    def sum_copy(i, axis):
        return remote(sumb.at[i], sumr.at[i], sm_s.at[i], sm_r.at[i], axis, 1 - at[axis])

    def sum_z(k):
        to = (wo_at + k + 1) % n_wo
        return remote(sumb.at[2], sumz.at[k], smz_s.at[k], smz_r.at[k], "wo", to)

    sum_copy(0, "y").start()

    def tail(i, carry):
        j = ffn_blocks + 1 + i

        @pl.when((i > 0) & (j < blocks))
        def _():
            stage_one(j)

        @pl.when(j <= blocks)
        def _():
            stage_two(j - 1)

        @pl.when(i > 0)
        def _():
            stage_three(j - 2)

        @pl.when(i == 0)
        def _():
            sum_copy(0, "y").wait_recv()
            sumb[1] = sumb[0] + sumr[0]
            sum_copy(1, "x").start()

        @pl.when(i == 1)
        def _():
            sum_copy(1, "x").wait_recv()
            sumb[2] = sumb[1] + sumr[1]
            for k in range(n_wo - 1):
                sum_z(k).start()

        return carry

    lax.fori_loop(0, blocks + 1 - ffn_blocks, tail, 0)
    in_y(nwin - 1).wait_recv()
    in_c(nwin - 1).start()
    total = sumb[2]
    for k in range(n_wo - 1):
        sum_z(k).wait_recv()
        total = total + sumz[k]
    total_sums[...] = total

    out_y.wait_send()
    for w in range(nwin):
        out_c(w).wait()
    dh_copy.wait_send()
    for i, axis in ((0, "y"), (1, "x")):
        sum_copy(i, axis).wait_send()
    for k in range(n_wo - 1):
        sum_z(k).wait_send()

    def drain_window(w, carry):
        part_copy(w).wait_send()
        own_copy(w).wait()
        in_y(w).wait_send()
        in_c(w).wait_send()
        in_c(w).wait_recv()
        return carry

    lax.fori_loop(0, nwin, drain_window, 0)

    def drain_block(b, carry):
        copy_one(b, False).wait_send()
        copy_two(b, False).wait_send()
        for k in range(n_wo - 1):
            copy_z(b, False, k).wait_send()
        return carry

    lax.fori_loop(0, blocks, drain_block, 0)


def backward(n_wo, lengths, slopes, nb, sums2, tokens, d2, dh, normed, recip, wqkv, wqkv1, wout, wout1,
             proj, att, lse, dgu, act, ht, d2t, half_out):
    half, d = normed.shape
    _, nwin, _, win = lse.shape
    width, hidden = wout.shape[0], act.shape[2]
    rows = d // (2 * n_wo)
    blocks = (3 * hidden + 4 * width) // BLOCK
    heads = width // HEAD_DIM
    smem = pl.BlockSpec(memory_space=pltpu.SMEM)
    vmem = pl.BlockSpec(memory_space=pltpu.VMEM)
    hbm = pl.BlockSpec(memory_space=pl.ANY)
    outs = [((blocks, rows, BLOCK), F32), ((8, d), F32), (tokens.shape, BF16), (tokens.shape, BF16)]
    bufs = [
        ((blocks, 2, 2, n_wo, rows, BLOCK), BF16), ((blocks, 2, n_wo, rows, BLOCK), BF16), ((blocks, n_wo, rows, BLOCK), BF16),
        ((blocks, n_wo - 1, rows, BLOCK), BF16), ((half, d), BF16), ((win, d), BF16), ((win, d), F32), ((win, d), F32),
        ((win, 128), F32), ((win, d), BF16), ((2, 2, 3, win, width), BF16), ((2, 2, win, width), BF16), (lse.shape, F32),
        ((2,) + wqkv.shape, BF16), ((2,) + wout.shape, BF16), ((nwin, win, d), BF16), ((nwin, win, d), BF16),
        ((nwin, win, d), BF16), ((3, 8, d), F32), ((2, 8, d), F32), ((n_wo - 1, 8, d), F32), ((8, d), F32),
    ]
    sems = [(blocks,)] * 4 + [(blocks, n_wo - 1)] * 2 + [(5,), (2, 2), (5,), (1,), (1,)] + [(nwin,)] * 7
    sems += [(nwin + 1,), (nwin + 1,), (2,), (2,), (n_wo - 1,), (n_wo - 1,), (2, 2), (2,)]
    return pl.pallas_call(
        backward_kernel,
        in_specs=[smem, smem, vmem, vmem] + [hbm] * 17,
        out_specs=[vmem, vmem, hbm, hbm],
        input_output_aliases={20: 2},
        out_shape=[jax.ShapeDtypeStruct(*o) for o in outs],
        scratch_shapes=[pltpu.VMEM(*b) for b in bufs] + [pltpu.SemaphoreType.DMA(n) for n in sems],
        compiler_params=pltpu.CompilerParams(vmem_limit_bytes=63 * 1024 * 1024, collective_id=1, has_side_effects=True),
        cost_estimate=pl.CostEstimate(
            flops=2 * half * d * width * 16 + 12 * half * d * hidden + 20 * nwin * heads * win * win * 256,
            bytes_accessed=half * d * 60 + half * hidden * 12, transcendentals=2 * nwin * heads * win * win,
        ),
        name="backward",
    )(lengths, slopes, nb, sums2, tokens, d2, dh, normed, recip, wqkv, wqkv1, wout, wout1,
      proj, att, lse, dgu, act, ht, d2t, half_out)


SWAP = [(0, 1), (1, 0)]
WIDE = ("wo", "x")


def swap(value, axis):
    return lax.ppermute(value, axis, SWAP)


def after(value, *others):
    return lax.optimization_barrier((value, *others))[0]


def weight_shares(columns, hidden, width):
    down_share = columns[:, :hidden].T
    up_share = jnp.stack([columns[:, hidden:2 * hidden], columns[:, 2 * hidden:3 * hidden]])
    start = 3 * hidden
    qkv_share = jnp.stack([columns[:, start + i * width:start + (i + 1) * width] for i in range(3)])
    out_share = columns[:, start + 3 * width:].T
    return qkv_share, out_share, up_share, down_share


def shards(tokens, wqkv, wout, nb, up, down, lengths, cot):
    x_at, y_at, c_at = (lax.axis_index(name) for name in ("x", "y", "core"))
    d = tokens.shape[1]
    group_heads = wout.shape[0] // HEAD_DIM
    wqkv = jnp.swapaxes(wqkv, 1, 2)
    own = 2 * y_at + c_at
    heads = jnp.concatenate([own * group_heads + jnp.arange(group_heads), (own ^ 2) * group_heads + jnp.arange(group_heads)])
    slopes = 2.0 ** (-8.0 * (heads + 1).astype(F32) / HEADS)
    info = jnp.concatenate([y_at[None].astype(jnp.int32), lengths])

    (proj, att, lse, normed, recip, ht, a_all, b_all, act, fpart, fpart_other,
     wqkv1, wout1, up1, down1) = forward(lengths, slopes, nb, tokens, wqkv, wout, up, down)
    out, d2, d2t, dgu, dh, sums2 = ffn_bwd(
        lse.shape[3], fpart, fpart_other, normed, cot, nb, up, up1, down, down1, a_all, b_all
    )
    wo = lax.axis_size("wo")
    width, hidden = wout.shape[0], down.shape[0]
    if (d // (2 * wo)) % 16 == 0:
        share, sums, block_out, input_low = backward(
            wo, lengths, slopes, nb, sums2, tokens, d2, dh, normed, recip, wqkv, wqkv1, wout, wout1,
            proj, att, lse, dgu, act, ht, d2t, out,
        )
        columns = share.transpose(1, 0, 2).reshape(share.shape[1], -1)
        small_share = lax.dynamic_slice_in_dim(sums[:6], (lax.axis_index("wo") * 2 + x_at) * (d // (2 * wo)), d // (2 * wo), 1)
        return (block_out, input_low.astype(F32), *weight_shares(columns, hidden, width), small_share)

    out = lax.dynamic_slice_in_dim(out, y_at * (out.shape[0] // 2), out.shape[0] // 2, 0)
    dh_other = swap(dh, "core")

    def grad(a, b):
        return lax.dot_general(a, b, (((1,), (0,)), ((), ())), preferred_element_type=F32).astype(BF16)

    def part_of(value, at):
        split = value.reshape(wo, 2, -1, value.shape[1])
        return lax.dynamic_index_in_dim(split, at, 1, keepdims=False).reshape(-1, value.shape[1])

    def add(a, b):
        return a.astype(F32) + b.astype(F32)

    down_peer = grad(d2t, act[1])
    down_peer_in = swap(down_peer, "y")
    up_peer = grad(ht, dgu[1])
    up_own = grad(ht, dgu[0])
    up_in = swap(jnp.concatenate([part_of(up_own, 1 - x_at), part_of(up_peer, 1 - x_at)], axis=0), "x")
    down_own = grad(d2t, act[0])

    quarter = out.shape[0] // 2
    order = jnp.stack([2 * y_at, 2 * y_at + 1, 2 * (1 - y_at) + c_at, 2 * (1 - y_at) + 1 - c_at]).astype(jnp.int32)

    def mine(value):
        return lax.dynamic_slice_in_dim(value, c_at * quarter, quarter, 0)

    d2 = after(d2, down_own)
    d1, ipart, agrad0, agrad1, sums1 = attn_bwd(
        info, slopes, tokens, d2, dh, dh_other, normed, recip, nb, wqkv, wqkv1, wout, wout1,
        proj, att, lse,
    )
    ipart_other = swap(ipart, "core")
    near_out = swap(mine(out), "y")

    attn_in = swap(jnp.concatenate([part_of(agrad0, 1 - x_at), part_of(agrad1, 1 - x_at)], axis=0), "x")

    total = (d1 + add(ipart, ipart_other)).astype(BF16)
    near_in = swap(mine(total), "y")

    down_all = add(down_own, down_peer_in).astype(BF16)
    down_in = swap(part_of(down_all, 1 - x_at), "x")
    down_half = add(part_of(down_all, x_at), down_in).astype(BF16)
    n = d // 2
    up_peer_half = add(part_of(up_peer, x_at), up_in[n:]).astype(BF16)
    up_half = add(add(part_of(up_own, x_at), up_in[:n]), swap(up_peer_half, "y")).astype(BF16)
    attn_peer_half = add(part_of(agrad1, x_at), attn_in[n:]).astype(BF16)
    attn_half = add(add(part_of(agrad0, x_at), attn_in[:n]), swap(attn_peer_half, "y")).astype(BF16)

    scatter = functools.partial(lax.psum_scatter, axis_name="wo", scatter_dimension=0, tiled=True)
    columns = jnp.concatenate([scatter(jnp.concatenate([down_half, up_half], axis=1)), scatter(attn_half)], axis=1).astype(F32)
    small = jnp.concatenate([sums1[:3], sums2[:3]], axis=0)
    small_share = lax.psum_scatter(lax.psum(small, "y"), WIDE, scatter_dimension=1, tiled=True)

    block_out = place(order, out, near_out, swap(near_out, "core"), BF16)
    input_grad = place(order, total, near_in, swap(near_in, "core"), F32)
    return (block_out, input_grad, *weight_shares(columns, hidden, width), small_share)


def solution(mesh):
    wide = mesh.shape["wide"]
    grid = Mesh(mesh.devices.reshape(wide // 2, 2, 2, 2), ("wo", "x", "y", "core"))
    narrow = ("y", "core")
    placed = (
        P(WIDE, None),
        P(None, None, narrow),
        P(narrow, None),
        P(),
        P(None, None, narrow),
        P(narrow, None),
        P(WIDE),
        P(WIDE, None),
    )
    return jax.shard_map(
        shards,
        mesh=grid,
        in_specs=placed,
        out_specs=(
            P(WIDE, None),
            P(WIDE, None),
            P(None, WIDE, narrow),
            P(narrow, WIDE),
            P(None, WIDE, narrow),
            P(narrow, WIDE),
            P(None, WIDE),
        ),
        check_vma=False,
    )
```

```python
import functools
import math

import jax
import jax.numpy as jnp
from jax import lax
from jax.experimental import pallas as pl
from jax.experimental.pallas import tpu as pltpu
from jax.sharding import Mesh, PartitionSpec as P

HEADS = 12
HEAD_DIM = 64
EPS = 1e-05
F32 = jnp.float32
BF16 = jnp.bfloat16
SCALE = 1.0 / math.sqrt(HEAD_DIM)
NEG = -1e30
MESH_ID = pl.DeviceIdType.MESH
VMEM_LIMIT = 56 * 1024 * 1024


def dot(a, b):
    return lax.dot_general(a, b, (((1,), (0,)), ((), ())), preferred_element_type=F32)


def dot_nt(a, b):
    return lax.dot_general(a, b, (((1,), (1,)), ((), ())), preferred_element_type=F32)


def dot_tn(a, b):
    return lax.dot_general(a, b, (((0,), (0,)), ((), ())), preferred_element_type=F32)


def whole(shape):
    return pl.BlockSpec(shape, lambda i, *_: (0,) * len(shape))


def head_lanes(width):
    lane = lax.broadcasted_iota(jnp.int32, (1, width), 1)
    return [(lane >= h * HEAD_DIM) & (lane < (h + 1) * HEAD_DIM) for h in range(width // HEAD_DIM)]


def fill_distance(ref):
    n = ref.shape[0]
    row = lax.broadcasted_iota(jnp.int32, (n, n), 0)
    col = lax.broadcasted_iota(jnp.int32, (n, n), 1)
    ref[...] = jnp.abs(row - col).astype(F32)


def params():
    return pltpu.CompilerParams(vmem_limit_bytes=VMEM_LIMIT, dimension_semantics=("arbitrary",))


def remote(src, dst, send, recv, axis, peer):
    return pltpu.make_async_remote_copy(src, dst, send, recv, device_id={axis: peer}, device_id_type=MESH_ID)


def standardize(value):
    center = value - jnp.mean(value, axis=1, keepdims=True)
    recip = lax.rsqrt(jnp.mean(center * center, axis=1, keepdims=True) + EPS)
    return center * recip, recip


def norm_grad(grad, normed, recip, gain):
    e = grad * gain
    inner = jnp.mean(e * normed, axis=1, keepdims=True)
    return recip * (e - jnp.mean(e, axis=1, keepdims=True) - normed * inner)


def rows_of_sums(values):
    width = values[0].shape[1]
    sums = [jnp.sum(v, axis=0, keepdims=True) for v in values]
    return jnp.concatenate(sums + [jnp.zeros((8 - len(sums), width), F32)], axis=0)


def ffn_bwd_kernel(pa, pb, normed_ref, cot, nb, up0, up1, down0, down1, a_all, b_all,
                   block_out, d2_ref, d2t_ref, dgu, dh_ref, sums_ref, outb, upv, downv, own_sem, ysend, yrecv, w_sem):
    hidden = down0.shape[0]
    i = pl.program_id(0)
    n, tile, _ = outb.shape
    y_at, c_at = lax.axis_index("y"), lax.axis_index("core")
    loads = [
        pltpu.make_async_copy(src, dst, w_sem.at[j])
        for j, (src, dst) in enumerate(((down0, downv.at[0]), (up0, upv.at[0]), (down1, downv.at[1]), (up1, upv.at[1])))
    ]

    @pl.when(i == 0)
    def _():
        barrier = pltpu.get_barrier_semaphore()
        pl.semaphore_signal(barrier, inc=1, device_id={"y": 1 - y_at}, device_id_type=MESH_ID)
        for copy in loads:
            copy.start()
        pl.semaphore_wait(barrier, 1)

    def own_copy(t):
        return pltpu.make_async_copy(outb.at[t], block_out.at[pl.ds((y_at * n + t) * tile, tile)], own_sem.at[t])

    def side_copy(t):
        side = tile // 2
        return remote(outb.at[t, pl.ds(c_at * side, side)], block_out.at[pl.ds((y_at * n + t) * tile + c_at * side, side)],
                      ysend.at[t], yrecv.at[t], "y", 1 - y_at)

    h = normed_ref[...].astype(F32) * nb[0:1] + nb[1:2]
    second = pa[...].astype(F32) + pb[...].astype(F32) + nb[5:6] + h
    normed, recip = standardize(second)
    gain = nb[3:4]
    outb[i] = (normed * gain + nb[4:5]).astype(BF16)
    own_copy(i).start()

    @pl.when(i < n - 1)
    def _():
        side_copy(i).start()

    c = cot[...].astype(F32)
    d2 = norm_grad(c, normed, recip, gain)
    d2b = d2.astype(BF16)
    d2_ref[...] = d2b
    d2t_ref[...] = d2b.T
    sums = rows_of_sums([c * normed, c, d2])

    @pl.when(pl.program_id(0) == 0)
    def _():
        sums_ref[...] = sums

    @pl.when(pl.program_id(0) > 0)
    def _():
        sums_ref[...] += sums

    total = None
    step = 768
    for g in range(2):
        @pl.when(i == 0)
        def _():
            loads[2 * g].wait()
            loads[2 * g + 1].wait()

        for at in range(0, hidden, step):
            cols = slice(at, at + step)
            dact = dot_nt(d2b, downv[g, cols, :])
            dgu[g, :, cols] = (dact * a_all[g, :, cols].astype(F32)).astype(BF16)
            dgu[g, :, slice(hidden + at, hidden + at + step)] = (dact * b_all[g, :, cols].astype(F32)).astype(BF16)
        for k in range(2):
            term = dot_nt(dgu[g, :, k * hidden:(k + 1) * hidden], upv[g, k])
            total = term if total is None else total + term
    dh_ref[...] = total.astype(BF16)

    @pl.when(i == n - 1)
    def _():
        for t in range(n):
            own_copy(t).wait()
        for t in range(n - 1):
            side_copy(t).wait()


def ffn_bwd(tile, pa, pb, normed, cot, nb, up0, up1, down0, down1, a_all, b_all):
    half, d = pa.shape
    hidden = down0.shape[0]
    n = half // tile
    row = lambda w: pl.BlockSpec((tile, w), lambda i, *_: (i, 0))
    return pl.pallas_call(
        ffn_bwd_kernel,
        grid=(n,),
        in_specs=[
            row(d), row(d), row(d),
            pl.BlockSpec((tile, d), lambda i: (lax.axis_index("y") * n + i, 0)),
            whole(nb.shape),
            *[pl.BlockSpec(memory_space=pl.ANY)] * 4,
            pl.BlockSpec((2, tile, hidden), lambda i: (0, i, 0)),
            pl.BlockSpec((2, tile, hidden), lambda i: (0, i, 0)),
        ],
        out_specs=[
            pl.BlockSpec(memory_space=pl.ANY), row(d),
            pl.BlockSpec((d, tile), lambda i: (0, i)),
            pl.BlockSpec((2, tile, 2 * hidden), lambda i: (0, i, 0)), row(d), whole((8, d)),
        ],
        scratch_shapes=[
            pltpu.VMEM((n, tile, d), BF16), pltpu.VMEM((2,) + up0.shape, BF16), pltpu.VMEM((2,) + down0.shape, BF16),
            *[pltpu.SemaphoreType.DMA((m,)) for m in (n, n - 1, n - 1, 4)],
        ],
        out_shape=[
            jax.ShapeDtypeStruct((2 * half, d), BF16),
            jax.ShapeDtypeStruct((half, d), BF16),
            jax.ShapeDtypeStruct((d, half), BF16),
            jax.ShapeDtypeStruct((2, half, 2 * hidden), BF16),
            jax.ShapeDtypeStruct((half, d), BF16),
            jax.ShapeDtypeStruct((8, d), F32),
        ],
        compiler_params=pltpu.CompilerParams(
            vmem_limit_bytes=VMEM_LIMIT, dimension_semantics=("arbitrary",), collective_id=2, has_side_effects=True
        ),
        cost_estimate=pl.CostEstimate(
            flops=12 * half * d * hidden, bytes_accessed=half * d * 20 + half * hidden * 16 + 12 * d * hidden,
            transcendentals=half,
        ),
        name="ffn_bwd",
    )(pa, pb, normed, cot, nb, up0, up1, down0, down1, a_all, b_all)


def attn_bwd_kernel(info, slopes, x_ref, d2_ref, ha, hb, normed_ref, recip_ref, nb, wqkv0, wqkv1, wout0, wout1,
                    proj_all, att_all, lse_all,
                    d1_ref, part, grad0, grad1, sums_ref, dist, sum0, sum1):
    step = pl.program_id(0)
    win = d2_ref.shape[0]
    width = wout0.shape[0]
    heads = width // HEAD_DIM

    @pl.when(step == 0)
    def _():
        fill_distance(dist)

    normed = normed_ref[...].astype(F32)
    dh = d2_ref[...].astype(F32) + (ha[...].astype(F32) + hb[...].astype(F32))
    d1 = norm_grad(dh, normed, recip_ref[:, 0:1], nb[0:1])
    d1_ref[...] = d1
    d1b = d1.astype(BF16)
    x = x_ref[...]
    sums = rows_of_sums([dh * normed, dh, d1])

    @pl.when(step == 0)
    def _():
        sums_ref[...] = sums

    @pl.when(step > 0)
    def _():
        sums_ref[...] += sums

    limit = info[1 + info[0] * pl.num_programs(0) + step]
    lanes = head_lanes(width)
    key_on = lax.broadcasted_iota(jnp.int32, (win, 1), 0) < limit
    stat_lane = lax.broadcasted_iota(jnp.int32, (1, 128), 1)
    total = None
    for g, (wqkv, wout, acc) in enumerate(((wqkv0, wout0, sum0), (wqkv1, wout1, sum1))):
        q, k, v = proj_all[g, 0], proj_all[g, 1], proj_all[g, 2]
        datt = dot_nt(d1b, wout[...]).astype(BF16)
        product = datt.astype(F32) * att_all[g].astype(F32)
        stat = jnp.zeros((win, 128), F32)
        for h in range(heads):
            inner = jnp.sum(jnp.where(lanes[h], product, 0.0), axis=1, keepdims=True)
            stat = jnp.where(stat_lane == h, inner, stat)
        inner_rows = stat.T[0:8]
        qs = q * jnp.asarray(SCALE, BF16)
        dq = jnp.zeros((win, width), F32)
        dk = jnp.zeros((win, width), F32)
        dv = jnp.zeros((win, width), F32)
        for h in range(heads):
            qh = jnp.where(lanes[h], qs, jnp.zeros_like(qs))
            oh = jnp.where(lanes[h], datt, jnp.zeros_like(datt))
            s = dot_nt(k, qh) - slopes[g * heads + h] * dist[...]
            s = jnp.where(key_on, s, NEG)
            p = jnp.exp(s - lse_all[g, 0, h:h + 1, :])
            dp = dot_nt(v, oh)
            ds = (p * (dp - inner_rows[h:h + 1, :])).astype(BF16)
            dv = jnp.where(lanes[h], dot(p.astype(BF16), datt), dv)
            dk = jnp.where(lanes[h], dot(ds, q), dk)
            dq = jnp.where(lanes[h], dot_tn(ds, k), dq)
        dqb = (dq * SCALE).astype(BF16)
        dkb = (dk * SCALE).astype(BF16)
        dvb = dv.astype(BF16)
        terms = [dot_tn(x, dqb), dot_tn(x, dkb), dot_tn(x, dvb), dot_tn(d1b, att_all[g])]

        @pl.when(step == 0)
        def _():
            for i in range(4):
                acc[i] = terms[i]

        @pl.when(step > 0)
        def _():
            for i in range(4):
                acc[i] += terms[i]

        term = dot(dqb, wqkv[0]) + dot(dkb, wqkv[1]) + dot(dvb, wqkv[2])
        total = term if total is None else total + term
    part[...] = total.astype(BF16)

    @pl.when(step == pl.num_programs(0) - 1)
    def _():
        for acc, grad in ((sum0, grad0), (sum1, grad1)):
            for i in range(4):
                grad[:, i * width:(i + 1) * width] = acc[i].astype(BF16)


def attn_bwd(info, slopes, tokens, d2, ha, hb, normed, recip, nb, wqkv0, wqkv1, wout0, wout1,
             proj, att, lse):
    half, d = d2.shape
    width = wout0.shape[0]
    _, nwin, _, win = lse.shape
    heads = 2 * width // HEAD_DIM
    row = lambda w: pl.BlockSpec((win, w), lambda i, *_: (i, 0))
    return pl.pallas_call(
        attn_bwd_kernel,
        grid_spec=pltpu.PrefetchScalarGridSpec(
            num_scalar_prefetch=2,
            grid=(nwin,),
            in_specs=[
                pl.BlockSpec((win, d), lambda i, info, sl: (info[0] * nwin + i, 0)),
                row(d), row(d), row(d), row(d), row(128), whole(nb.shape),
                whole(wqkv0.shape), whole(wqkv1.shape), whole(wout0.shape), whole(wout1.shape),
                pl.BlockSpec((2, 3, win, width), lambda i, *_: (0, 0, i, 0)),
                pl.BlockSpec((2, win, width), lambda i, *_: (0, i, 0)),
                pl.BlockSpec((2, 1, 8, win), lambda i, *_: (0, i, 0, 0)),
            ],
            out_specs=[row(d), row(d), whole((d, 4 * width)), whole((d, 4 * width)), whole((8, d))],
            scratch_shapes=[pltpu.VMEM((win, win), F32), pltpu.VMEM((4, d, width), F32), pltpu.VMEM((4, d, width), F32)],
        ),
        out_shape=[
            jax.ShapeDtypeStruct((half, d), F32),
            jax.ShapeDtypeStruct((half, d), BF16),
            jax.ShapeDtypeStruct((d, 4 * width), BF16),
            jax.ShapeDtypeStruct((d, 4 * width), BF16),
            jax.ShapeDtypeStruct((8, d), F32),
        ],
        compiler_params=params(),
        cost_estimate=pl.CostEstimate(
            flops=2 * half * d * width * 16 + 10 * nwin * heads * win * win * 256,
            bytes_accessed=half * d * 20 + half * width * 32 + d * width * 16,
            transcendentals=nwin * heads * win * win,
        ),
        name="attn_bwd",
    )(info, slopes, tokens, d2, ha, hb, normed, recip, nb, wqkv0, wqkv1, wout0, wout1,
      proj, att, lse)


def place_kernel(order, mine, near, far, out):
    step = pl.program_id(0)

    @pl.when(step < 2)
    def _():
        out[...] = mine[...].astype(out.dtype)

    @pl.when(step == 2)
    def _():
        out[...] = near[...].astype(out.dtype)

    @pl.when(step == 3)
    def _():
        out[...] = far[...].astype(out.dtype)


def place(order, mine, near, far, dtype):
    quarter, d = near.shape
    return pl.pallas_call(
        place_kernel,
        grid_spec=pltpu.PrefetchScalarGridSpec(
            num_scalar_prefetch=1,
            grid=(4,),
            in_specs=[
                pl.BlockSpec((quarter, d), lambda i, o: (jnp.minimum(i, 1), 0)),
                whole((quarter, d)),
                whole((quarter, d)),
            ],
            out_specs=pl.BlockSpec((quarter, d), lambda i, o: (o[i], 0)),
        ),
        out_shape=jax.ShapeDtypeStruct((4 * quarter, d), dtype),
        compiler_params=params(),
        cost_estimate=pl.CostEstimate(flops=0, bytes_accessed=24 * quarter * d, transcendentals=0),
        name="place",
    )(order, mine, near, far)


TILE = 256


def forward_kernel(info, slopes, nb, tokens, wqkv, wout, up, down,
                   proj_out, att_out, lse_out, normed_out, recip_out, ht_out, a_out, b_out, act_out, fown_out, frecv_out,
                   wqkv1_out, wout1_out, up1_out, down1_out,
                   xbuf, wqv, wov, upv, downv, projb, attb, lseb, pown, precv, normedb, recipb, hbuf, htb, ab, bb, actb,
                   facc, fown, dist,
                   load_sem, ysend, yrecv, xsend, xrecv, zsend, zrecv, psend, prem, fsend, frem, out_sem, pout_sem, tout_sem, fout_sem):
    wo_at, x_at, y_at, c_at = (lax.axis_index(n) for n in ("wo", "x", "y", "core"))
    nwin, _, win = lse_out.shape[1:]
    half, d = xbuf.shape
    width = wout.shape[0]
    hidden = down.shape[0]
    heads = width // HEAD_DIM
    tiles = half // TILE
    z_at = wo_at % 2
    z_peer = wo_at + 1 - 2 * z_at

    barrier = pltpu.get_barrier_semaphore()
    for axis, to in (("x", 1 - x_at), ("y", 1 - y_at), ("core", 1 - c_at), ("wo", z_peer)):
        pl.semaphore_signal(barrier, inc=1, device_id={axis: to}, device_id_type=MESH_ID)
    pl.semaphore_wait(barrier, 4)

    def quarter(i, q):
        if i == 0:
            return wqkv.at[:, pl.ds(q * (width // 4), width // 4)], wqv.at[1, :, pl.ds(q * (width // 4), width // 4)]
        if i == 1:
            return wout.at[pl.ds(q * (width // 4), width // 4)], wov.at[1, pl.ds(q * (width // 4), width // 4)]
        if i == 2:
            return up.at[:, pl.ds(q * (d // 4), d // 4)], upv.at[1, :, pl.ds(q * (d // 4), d // 4)]
        return down.at[pl.ds(q * (hidden // 4), hidden // 4)], downv.at[1, pl.ds(q * (hidden // 4), hidden // 4)]

    def eighth(i, q, e):
        if i == 0:
            return wqv.at[1, :, pl.ds(q * (width // 4), width // 4), e * (d // 2):(e + 1) * (d // 2)]
        if i == 1:
            return wov.at[1, pl.ds(q * (width // 4), width // 4), e * (d // 2):(e + 1) * (d // 2)]
        if i == 2:
            return upv.at[1, :, pl.ds(q * (d // 4) + e * (d // 8), d // 8)]
        return downv.at[1, pl.ds(q * (hidden // 4) + e * (hidden // 8), hidden // 8)]

    here = 2 * x_at + z_at
    across_x = 2 * (1 - x_at) + z_at
    across_z = 2 * x_at + 1 - z_at

    def over_y(i):
        src, dst = quarter(i, here)
        return remote(src, dst, ysend.at[i], yrecv.at[i], "y", 1 - y_at)

    def level_one(i):
        _, ref = quarter(i, here)
        return (remote(ref, ref, xsend.at[0, i], xrecv.at[0, i], "x", 1 - x_at),
                remote(ref, ref, zsend.at[0, i], zrecv.at[0, i], "wo", z_peer))

    def level_two(i):
        from_z, from_x = eighth(i, across_z, 0), eighth(i, across_x, 1)
        return (remote(from_z, from_z, xsend.at[1, i], xrecv.at[1, i], "x", 1 - x_at),
                remote(from_x, from_x, zsend.at[1, i], zrecv.at[1, i], "wo", z_peer))

    def launch(copies):
        for copy in copies:
            copy.start()

    def arrive(copies):
        for copy in copies:
            copy.wait_recv()

    loads = [
        pltpu.make_async_copy(tokens.at[pl.ds(y_at * half, half)], xbuf, load_sem.at[0]),
        pltpu.make_async_copy(wqkv, wqv.at[0], load_sem.at[1]),
        pltpu.make_async_copy(wout, wov.at[0], load_sem.at[2]),
        pltpu.make_async_copy(up, upv.at[0], load_sem.at[3]),
        pltpu.make_async_copy(down, downv.at[0], load_sem.at[4]),
    ]
    over_y(0).start()
    over_y(1).start()
    for load in loads:
        load.start()
    fill_distance(dist)
    lanes = head_lanes(width)
    stat_lane = lax.broadcasted_iota(jnp.int32, (1, 128), 1)
    key_at = lax.broadcasted_iota(jnp.int32, (1, win), 1)
    for load in loads[:3]:
        load.wait()

    def part_copy(w):
        rows = pl.ds(w * win, win)
        return remote(pown.at[rows], precv.at[rows], psend.at[w], prem.at[w], "core", 1 - c_at)

    def proj_copy(t):
        g, rows = t // nwin, pl.ds((t % nwin) * win, win)
        return (
            pltpu.make_async_copy(projb.at[g, :, rows], proj_out.at[g, :, rows], pout_sem.at[0, t]),
            pltpu.make_async_copy(attb.at[g, rows], att_out.at[g, rows], pout_sem.at[1, t]),
        )

    def attention(t, carry):
        g, w = t // nwin, t % nwin
        start = w * win
        x = xbuf[pl.ds(start, win)]
        q = dot_nt(x, wqv[g, 0]).astype(BF16)
        k = dot_nt(x, wqv[g, 1]).astype(BF16)
        v = dot_nt(x, wqv[g, 2]).astype(BF16)
        projb[g, 0, pl.ds(start, win)] = q
        projb[g, 1, pl.ds(start, win)] = k
        projb[g, 2, pl.ds(start, win)] = v
        key_on = key_at < info[y_at * nwin + w]
        rows = win // 2
        for b in range(2):
            at = slice(b * rows, (b + 1) * rows)
            qb = q[at] * jnp.asarray(SCALE, BF16)
            att = jnp.zeros((rows, width), F32)
            stat = jnp.zeros((rows, 128), F32)
            for h in range(heads):
                qh = jnp.where(lanes[h], qb, jnp.zeros_like(qb))
                s = dot_nt(qh, k) - slopes[g * heads + h] * dist[at]
                s = jnp.where(key_on, s, NEG)
                top = jnp.max(s, axis=1, keepdims=True)
                p = jnp.exp(s - top)
                total = jnp.sum(p, axis=1, keepdims=True)
                o = dot(p.astype(BF16), v) * (1.0 / total)
                att = jnp.where(lanes[h], o, att)
                stat = jnp.where(stat_lane == h, top + jnp.log(total), stat)
            attb[g, pl.ds(start + b * rows, rows)] = att.astype(BF16)
            lseb[g, w, :, at] = stat.T[0:8]
        for copy in proj_copy(t):
            copy.start()

        @pl.when(t >= nwin)
        def _():
            out = dot(attb[0, pl.ds(start, win)], wov[0]) + dot(attb[1, pl.ds(start, win)], wov[1])
            pown[pl.ds(start, win)] = out.astype(BF16)
            part_copy(w).start()

        @pl.when(t == 0)
        def _():
            for i in range(2):
                over_y(i).wait_recv()
                launch(level_one(i))
            over_y(2).start()

        @pl.when(t == nwin - 1)
        def _():
            over_y(3).start()
            for i in range(2):
                arrive(level_one(i))
                launch(level_two(i))
            for i in range(2):
                arrive(level_two(i))

        @pl.when(t == nwin)
        def _():
            over_y(2).wait_recv()
            launch(level_one(2))

        return carry

    lax.fori_loop(0, 2 * nwin, attention, 0)
    lse_copy = pltpu.make_async_copy(lseb, lse_out, out_sem.at[0])
    lse_copy.start()
    loads[3].wait()
    loads[4].wait()
    step = 256

    def hidden_units(g, start, hb):
        for at in range(0, hidden, step):
            cols = slice(at, at + step)
            gate = dot(hb, upv[g, 0, :, cols])
            lift = dot(hb, upv[g, 1, :, cols])
            cdf = 0.5 * (1.0 + lax.erf(gate * (1.0 / math.sqrt(2.0))))
            pdf = jnp.exp(-0.5 * gate * gate) * (1.0 / math.sqrt(2.0 * math.pi))
            gelu = gate * cdf
            rows = pl.ds(start, TILE)
            ab[g, rows, cols] = (lift * (cdf + gate * pdf)).astype(BF16)
            bb[g, rows, cols] = gelu.astype(BF16)
            actb[g, rows, cols] = (gelu * lift).astype(BF16)

    def tile_copies(t):
        g, rows = t // tiles, pl.ds((t % tiles) * TILE, TILE)
        return [
            pltpu.make_async_copy(b.at[g, rows], o.at[g, rows], tout_sem.at[i, t])
            for i, (b, o) in enumerate(((ab, a_out), (bb, b_out), (actb, act_out)))
        ]

    def norm_copies(i):
        rows = pl.ds(pl.multiple_of(i * TILE, TILE), TILE)
        return [
            pltpu.make_async_copy(b.at[rows], o.at[rows], fout_sem.at[n, i])
            for n, (b, o) in enumerate(((normedb, normed_out), (recipb, recip_out)))
        ] + [pltpu.make_async_copy(htb.at[:, rows], ht_out.at[:, rows], fout_sem.at[2, i])]

    def first(i, carry):
        start = i * TILE

        @pl.when(i % (win // TILE) == 0)
        def _():
            part_copy(i // (win // TILE)).wait_recv()

        rows = pl.ds(start, TILE)
        value = (pown[rows].astype(F32) + precv[rows].astype(F32)) + nb[2:3] + xbuf[rows].astype(F32)
        normed, recip = standardize(value)
        normedb[rows] = normed.astype(BF16)
        recipb[rows] = jnp.broadcast_to(recip, (TILE, 128))
        hb = (normed * nb[0:1] + nb[1:2]).astype(BF16)
        hbuf[rows] = hb
        htb[:, pl.ds(pl.multiple_of(start, TILE), TILE)] = hb.T
        hidden_units(0, start, hb)
        facc[rows] = dot(actb[0, rows], downv[0])
        for copy in tile_copies(i) + norm_copies(i):
            copy.start()

        @pl.when(i == tiles // 2 - 1)
        def _():
            arrive(level_one(2))
            launch(level_two(2))
            over_y(3).wait_recv()
            launch(level_one(3))

        return carry

    lax.fori_loop(0, tiles, first, 0)
    arrive(level_two(2))

    def second(i, carry):
        start = i * TILE
        hidden_units(1, start, hbuf[pl.ds(start, TILE)])
        for copy in tile_copies(tiles + i):
            copy.start()

        @pl.when(i == tiles - 2)
        def _():
            arrive(level_one(3))
            launch(level_two(3))

        return carry

    lax.fori_loop(0, tiles, second, 0)
    arrive(level_two(3))

    def final_copy(i):
        rows = pl.ds(i * TILE, TILE)
        return (
            remote(fown.at[rows], frecv_out.at[rows], fsend.at[i], frem.at[i], "core", 1 - c_at),
            pltpu.make_async_copy(fown.at[rows], fown_out.at[rows], fout_sem.at[3, i]),
        )

    def third(i, carry):
        rows = pl.ds(i * TILE, TILE)
        fown[rows] = (facc[rows] + dot(actb[1, rows], downv[1])).astype(BF16)
        for copy in final_copy(i):
            copy.start()
        return carry

    weights_out = [
        pltpu.make_async_copy(wqv.at[1], wqkv1_out, out_sem.at[1]),
        pltpu.make_async_copy(wov.at[1], wout1_out, out_sem.at[2]),
        pltpu.make_async_copy(upv.at[1], up1_out, out_sem.at[3]),
        pltpu.make_async_copy(downv.at[1], down1_out, out_sem.at[4]),
    ]
    for copy in weights_out:
        copy.start()
    lax.fori_loop(0, tiles, third, 0)

    def finish(i, carry):
        sent, kept = final_copy(i)
        sent.wait_recv()
        sent.wait_send()
        kept.wait()
        for copy in norm_copies(i):
            copy.wait()
        return carry

    lax.fori_loop(0, tiles, finish, 0)

    def drain_tiles(t, carry):
        for copy in tile_copies(t):
            copy.wait()
        return carry

    lax.fori_loop(0, 2 * tiles, drain_tiles, 0)

    def drain_proj(t, carry):
        for copy in proj_copy(t):
            copy.wait()
        return carry

    lax.fori_loop(0, 2 * nwin, drain_proj, 0)

    def drain_part(w, carry):
        part_copy(w).wait_send()
        return carry

    lax.fori_loop(0, nwin, drain_part, 0)
    lse_copy.wait()
    for copy in weights_out:
        copy.wait()
    for i in range(4):
        over_y(i).wait_send()
        for copy in level_one(i) + level_two(i):
            copy.wait_send()


def forward(lengths, slopes, nb, tokens, wqkv, wout, up, down):
    d = tokens.shape[1]
    nwin = lengths.shape[0] // 2
    half = tokens.shape[0] // 2
    win = half // nwin
    width, hidden = wout.shape[0], down.shape[0]
    tiles = half // TILE
    heads = width // HEAD_DIM
    smem = pl.BlockSpec(memory_space=pltpu.SMEM)
    vmem = pl.BlockSpec(memory_space=pltpu.VMEM)
    hbm = pl.BlockSpec(memory_space=pl.ANY)
    acts = [((2, half, hidden), BF16)] * 3
    outs = [
        ((2, 3, half, width), BF16), ((2, half, width), BF16), ((2, nwin, 8, win), F32),
        ((half, d), BF16), ((half, 128), F32), ((d, half), BF16), *acts,
        ((half, d), BF16), ((half, d), BF16),
        (wqkv.shape, BF16), (wout.shape, BF16), (up.shape, BF16), (down.shape, BF16),
    ]
    bufs = [
        ((half, d), BF16), ((2,) + wqkv.shape, BF16), ((2,) + wout.shape, BF16), ((2,) + up.shape, BF16),
        ((2,) + down.shape, BF16), ((2, 3, half, width), BF16), ((2, half, width), BF16), ((2, nwin, 8, win), F32),
        ((half, d), BF16), ((half, d), BF16), ((half, d), BF16), ((half, 128), F32), ((half, d), BF16), ((d, half), BF16), *acts,
        ((half, d), F32), ((half, d), BF16), ((win, win), F32),
    ]
    sems = [(5,), (4,), (4,), (2, 4), (2, 4), (2, 4), (2, 4), (nwin,), (nwin,), (tiles,), (tiles,), (5,), (2, 2 * nwin), (3, 2 * tiles), (5, tiles)]
    return pl.pallas_call(
        forward_kernel,
        in_specs=[smem, smem, vmem] + [hbm] * 5,
        out_specs=[hbm] * len(outs),
        out_shape=[jax.ShapeDtypeStruct(*o) for o in outs],
        scratch_shapes=[pltpu.VMEM(*b) for b in bufs] + [pltpu.SemaphoreType.DMA(n) for n in sems],
        compiler_params=pltpu.CompilerParams(vmem_limit_bytes=62 * 1024 * 1024, collective_id=0, has_side_effects=True),
        cost_estimate=pl.CostEstimate(
            flops=2 * half * d * width * 16 + 12 * half * d * hidden + 8 * nwin * heads * win * win * 256,
            bytes_accessed=half * d * 30 + half * hidden * 12, transcendentals=half * hidden * 4,
        ),
        name="forward",
    )(lengths, slopes, nb, tokens, wqkv, wout, up, down)


BLOCK = 128
PAIR = 2 * BLOCK
FLIGHT = 4
TAIL_FLIGHT = 3


def backward_kernel(lengths, slopes, nb, sums2, tokens, d2_in, dh_in, normed_in, recip_in, wqkv, wqkv1, wout, wout1,
                    proj_in, att_in, lse_in, dgu_in, act_in, ht_in, d2t_in, half_in,
                    share, total_sums, block_out, input_grad,
                    gbuf, r1, r2, zr, dhr, dhw, normw, d2w, recw, xw, projw, attw, lsev, wqv, wov, ipown, iprecv, totb,
                    sumb, sumr, sumz, sum1,
                    g1s, g1r, g2s, g2r, zs, zrs, pre_sem, win_sem, w_sem, dh_s, dh_r, ip_s, ip_r,
                    tot_sem, iy_s, iy_r, ic_s, ic_r, bo_s, bo_r, sm_s, sm_r, smz_s, smz_r, ring_sem, t_sem):
    at = {n: lax.axis_index(n) for n in ("wo", "x", "y", "core")}
    wo_at, x_at, y_at, c_at = at["wo"], at["x"], at["y"], at["core"]
    n_wo = gbuf.shape[3]
    blocks = gbuf.shape[0]
    own_rows = gbuf.shape[4]
    half, d = normed_in.shape
    _, nwin, _, win = lse_in.shape
    width = wout.shape[0]
    hidden = act_in.shape[2]
    heads = width // HEAD_DIM
    ffn_blocks = 3 * hidden // BLOCK

    barrier = pltpu.get_barrier_semaphore()
    for axis in ("x", "y", "core"):
        pl.semaphore_signal(barrier, inc=1, device_id={axis: 1 - at[axis]}, device_id_type=MESH_ID)
    for k in range(n_wo - 1):
        pl.semaphore_signal(barrier, inc=1, device_id={"wo": (wo_at + k + 1) % n_wo}, device_id_type=MESH_ID)
    pl.semaphore_wait(barrier, n_wo + 2)

    def copy_one(b, is_y):
        send = 1 if is_y else 1 - x_at
        axis = "y" if is_y else "x"
        return remote(gbuf.at[b, send], r1.at[b], g1s.at[b], g1r.at[b], axis, 1 - at[axis])

    def copy_two(b, is_y):
        keep = 0 if is_y else x_at
        send = 1 - x_at if is_y else 1
        axis = "x" if is_y else "y"
        return remote(gbuf.at[b, keep, send], r2.at[b], g2s.at[b], g2r.at[b], axis, 1 - at[axis])

    def copy_z(b, is_y, k):
        keep = 0 if is_y else x_at
        keep2 = x_at if is_y else 0
        to = (wo_at + k + 1) % n_wo
        return remote(gbuf.at[b, keep, keep2, to], zr.at[b, k], zs.at[b, k], zrs.at[b, k], "wo", to)

    def by_kind(b, f):
        @pl.when(b % 3 == 1)
        def _():
            f(True)

        @pl.when(b % 3 != 1)
        def _():
            f(False)

    def stage_one(b):
        copy_one(b, False).wait_recv()

        def go(is_y):
            keep = 0 if is_y else x_at
            gbuf[b, keep] = (gbuf[b, keep].astype(F32) + r1[b].astype(F32)).astype(BF16)
            copy_two(b, is_y).start()

        by_kind(b, go)

        @pl.when(b + FLIGHT < ffn_blocks)
        def _():
            by_kind(b + FLIGHT, lambda is_y: copy_one(b + FLIGHT, is_y).start())

        @pl.when((b >= ffn_blocks) & (b + TAIL_FLIGHT < blocks))
        def _():
            by_kind(b + TAIL_FLIGHT, lambda is_y: copy_one(b + TAIL_FLIGHT, is_y).start())

    def stage_two(b):
        copy_two(b, False).wait_recv()

        def go(is_y):
            keep = 0 if is_y else x_at
            keep2 = x_at if is_y else 0
            gbuf[b, keep, keep2] = (gbuf[b, keep, keep2].astype(F32) + r2[b].astype(F32)).astype(BF16)
            for k in range(n_wo - 1):
                copy_z(b, is_y, k).start()

        by_kind(b, go)

    def stage_three(b):
        for k in range(n_wo - 1):
            copy_z(b, False, k).wait_recv()

        def go(is_y):
            keep = 0 if is_y else x_at
            keep2 = x_at if is_y else 0
            total = gbuf[b, keep, keep2, wo_at].astype(F32)
            for k in range(n_wo - 1):
                total = total + zr[b, k].astype(F32)
            share[b] = total

        by_kind(b, go)

    def advance(k):
        for j in (2 * k, 2 * k + 1):
            stage_one(j)

            @pl.when(k >= 2)
            def _():
                stage_two(j - 4)

            @pl.when(k >= 4)
            def _():
                stage_three(j - 8)

    def put(b, g, value):
        r = b % 3
        is_y = r * (2 - r)
        for j in range(2 * n_wo):
            px, w = j % 2, j // 2
            outer = g * is_y + px * (1 - is_y)
            gbuf[b, outer, g + px - outer, w] = value[j * own_rows:(j + 1) * own_rows].astype(BF16)

    def pre_loads(w):
        rows = pl.ds(w * win, win)
        return [
            pltpu.make_async_copy(src, dst, pre_sem.at[i])
            for i, (src, dst) in enumerate((
                (normed_in.at[rows], normw), (d2_in.at[rows], d2w), (recip_in.at[rows], recw), (dh_in.at[rows], dhw),
                (tokens.at[pl.ds(y_at * half + w * win, win)], xw),
            ))
        ]

    def win_loads(w):
        rows, slot = pl.ds(w * win, win), w % 2
        return [
            pltpu.make_async_copy(proj_in.at[:, :, rows], projw.at[slot], win_sem.at[0, slot]),
            pltpu.make_async_copy(att_in.at[:, rows], attw.at[slot], win_sem.at[1, slot]),
        ]

    dh_copy = remote(dh_in, dhr, dh_s.at[0], dh_r.at[0], "core", 1 - c_at)
    side = win // 2
    last_rows = pl.ds(y_at * half + (nwin - 1) * win + c_at * side, side)
    out_y = remote(block_out.at[last_rows], block_out.at[last_rows], bo_s.at[nwin], bo_r.at[nwin], "y", 1 - y_at)

    def out_c(w):
        rows = pl.ds((1 - y_at) * half + w * win + c_at * side, side)
        return remote(block_out.at[rows], block_out.at[rows], bo_s.at[w], bo_r.at[w], "core", 1 - c_at)

    loads = [
        pltpu.make_async_copy(src, dst, w_sem.at[i])
        for i, (src, dst) in enumerate((
            (wqkv, wqv.at[0]), (wqkv1, wqv.at[1]), (wout, wov.at[0]), (wout1, wov.at[1]), (lse_in, lsev),
        ))
    ]

    def ffn_grads(ring, lhs_d, lhs_h):
        lhs = [pltpu.make_async_copy(d2t_in, lhs_d, t_sem.at[0]), pltpu.make_async_copy(ht_in, lhs_h, t_sem.at[1])]
        down_pairs = hidden // PAIR
        up_pairs = 2 * hidden // PAIR

        def fetch(src, b, g):
            return pltpu.make_async_copy(src.at[g, :, pl.ds(pl.multiple_of(b * PAIR, PAIR), PAIR)],
                                         ring.at[b % 2, :, g * PAIR:(g + 1) * PAIR], ring_sem.at[b % 2, g])

        def run(src, left, count, first):
            for g in range(2):
                fetch(src, 0, g).start()

            def one(b, carry):
                @pl.when(b + 1 < count)
                def _():
                    for g in range(2):
                        fetch(src, b + 1, g).start()

                for g in range(2):
                    fetch(src, b, g).wait()
                value = dot(left[...], ring[b % 2]).astype(BF16)
                k = b + first
                for side in range(2):
                    for g in range(2):
                        at = g * PAIR + side * BLOCK
                        put(2 * k + side, g, value[:, at:at + BLOCK])

                    @pl.when(2 * k + side < FLIGHT)
                    def _():
                        by_kind(2 * k + side, lambda is_y: copy_one(2 * k + side, is_y).start())

                @pl.when((k >= 4) & (k % 2 == 0))
                def _():
                    advance((k - 4) // 2)

                return carry

            lax.fori_loop(0, count, one, 0)

        lhs[0].start()
        dh_copy.start()
        out_y.start()
        for w in range(nwin - 1):
            out_c(w).start()
        lhs[1].start()
        for copy in loads + pre_loads(0) + win_loads(0):
            copy.start()
        lhs[0].wait()
        run(act_in, lhs_d, down_pairs, 0)
        lhs[1].wait()
        run(dgu_in, lhs_h, up_pairs, down_pairs)

    pl.run_scoped(ffn_grads, pltpu.VMEM((2, half, 2 * PAIR), BF16), pltpu.VMEM((d, half), BF16), pltpu.VMEM((d, half), BF16))

    for load in loads:
        load.wait()
    dh_copy.wait_recv()
    lanes = head_lanes(width)
    stat_lane = lax.broadcasted_iota(jnp.int32, (1, 128), 1)

    def part_copy(w):
        return remote(ipown.at[w], iprecv.at[w], ip_s.at[w], ip_r.at[w], "core", 1 - c_at)

    def own_copy(w):
        return pltpu.make_async_copy(totb.at[w], input_grad.at[pl.ds(y_at * half + w * win, win)], tot_sem.at[w])

    def in_y(w):
        return remote(totb.at[w, pl.ds(c_at * side, side)], input_grad.at[pl.ds(y_at * half + w * win + c_at * side, side)],
                      iy_s.at[w], iy_r.at[w], "y", 1 - y_at)

    def in_c(w):
        rows = pl.ds((1 - y_at) * half + w * win + c_at * side, side)
        return remote(input_grad.at[rows], input_grad.at[rows], ic_s.at[w], ic_r.at[w], "core", 1 - c_at)

    def attention(acc, xt, d1t, d1b, d1w, iptot, dist, stage):
        fill_distance(dist)
        acc[...] = jnp.zeros_like(acc)
        sum1[...] = jnp.zeros_like(sum1)

        def send_total(w):
            part_copy(w).wait_recv()
            value = d1w[w % 2] + (ipown[w].astype(F32) + iprecv[w].astype(F32))
            totb[w] = value.astype(BF16)
            own_copy(w).start()
            in_y(w).start()

        def step(t, carry):
            w, g = t // 2, t % 2
            slot = w % 2

            @pl.when(g == 0)
            def _():
                for copy in pre_loads(w) + win_loads(w):
                    copy.wait()
                normed = normw[...].astype(F32)
                dh = d2w[...].astype(F32) + (dhw[...].astype(F32) + dhr[pl.ds(w * win, win)].astype(F32))
                d1 = norm_grad(dh, normed, recw[:, 0:1], nb[0:1])
                d1w[slot] = d1
                low = d1.astype(BF16)
                d1b[...] = low
                d1t[...] = low.T
                xt[...] = xw[...].T
                sum1[...] += rows_of_sums([dh * normed, dh, d1])

                @pl.when(w + 1 < nwin)
                def _():
                    for copy in pre_loads(w + 1) + win_loads(w + 1):
                        copy.start()

            q, k, v = projw[slot, g, 0], projw[slot, g, 1], projw[slot, g, 2]
            att = attw[slot, g]
            datt = dot_nt(d1b[...], wov[g]).astype(BF16)
            product = datt.astype(F32) * att.astype(F32)
            stat = jnp.zeros((win, 128), F32)
            for h in range(heads):
                inner = jnp.sum(jnp.where(lanes[h], product, 0.0), axis=1, keepdims=True)
                stat = jnp.where(stat_lane == h, inner, stat)
            inner_rows = stat.T[0:8]
            qs = q * jnp.asarray(SCALE, BF16)
            dq = jnp.zeros((win, width), F32)
            dks, dvs = [], []
            half_keys = win // 2
            limit = lengths[y_at * nwin + w]
            for kb in range(2):
                keys = slice(kb * half_keys, (kb + 1) * half_keys)
                kk, vk = k[keys], v[keys]
                key_on = lax.broadcasted_iota(jnp.int32, (half_keys, 1), 0) + kb * half_keys < limit
                dk = jnp.zeros((half_keys, width), F32)
                dv = jnp.zeros((half_keys, width), F32)
                for h in range(heads):
                    qh = jnp.where(lanes[h], qs, jnp.zeros_like(qs))
                    oh = jnp.where(lanes[h], datt, jnp.zeros_like(datt))
                    s = dot_nt(kk, qh) - slopes[g * heads + h] * dist[keys]
                    s = jnp.where(key_on, s, NEG)
                    p = jnp.exp(s - lsev[g, w, h:h + 1, :])
                    dp = dot_nt(vk, oh)
                    ds = (p * (dp - inner_rows[h:h + 1, :])).astype(BF16)
                    dv = jnp.where(lanes[h], dot(p.astype(BF16), datt), dv)
                    dk = jnp.where(lanes[h], dot(ds, q), dk)
                    dq = dq + jnp.where(lanes[h], dot_tn(ds, kk), 0.0)
                dks.append((dk * SCALE).astype(BF16))
                dvs.append(dv.astype(BF16))
            dqb = (dq * SCALE).astype(BF16)
            dkb = jnp.concatenate(dks, axis=0)
            dvb = jnp.concatenate(dvs, axis=0)
            acc[g, 0] += dot(xt[...], dqb)
            acc[g, 1] += dot(xt[...], dkb)
            acc[g, 2] += dot(xt[...], dvb)
            acc[g, 3] += dot(d1t[...], att)
            term = dot(dqb, wqv[g, 0]) + dot(dkb, wqv[g, 1]) + dot(dvb, wqv[g, 2])

            @pl.when(g == 0)
            def _():
                iptot[...] = term

            @pl.when(g == 1)
            def _():
                ipown[w] = (iptot[...] + term).astype(BF16)
                part_copy(w).start()

            @pl.when((g == 0) & (w > 0))
            def _():
                send_total(w - 1)

            @pl.when(t == 0)
            def _():
                advance(3)

            @pl.when(t == 1)
            def _():
                advance(4)

            @pl.when((t > 0) & (t < 2 * nwin - 1))
            def _():
                advance(t + 4)

            @pl.when(t == 2 * nwin - 1)
            def _():
                for b in (ffn_blocks - 4, ffn_blocks - 3):
                    stage_two(b)
                    stage_three(b - 4)


            @pl.when(t == 3)
            def _():
                out_y.wait_recv()
                out_c(nwin - 1).start()

            return carry

        lax.fori_loop(0, 2 * nwin, step, 0)

        first = blocks - 4 * width // BLOCK
        for g in range(2):
            for i in range(4):
                stage[:, i * width:(i + 1) * width] = acc[g, i].astype(BF16)
            for i in range(4 * width // BLOCK):
                put(first + i, g, stage[:, i * BLOCK:(i + 1) * BLOCK])
        for i in range(first, first + TAIL_FLIGHT):
            copy_one(i, i % 3 == 1).start()
        for b in (ffn_blocks - 2, ffn_blocks - 1):
            stage_two(b)

        def rest(b, carry):
            stage_three(b)
            return carry

        lax.fori_loop(ffn_blocks - 6, ffn_blocks, rest, 0)
        for w in range(nwin - 1):
            in_y(w).wait_recv()
            in_c(w).start()
        stage_one(first)
        stage_one(first + 1)
        send_total(nwin - 1)

    pl.run_scoped(
        attention,
        pltpu.VMEM((2, 4, d, width), F32), pltpu.VMEM((d, win), BF16), pltpu.VMEM((d, win), BF16), pltpu.VMEM((win, d), BF16),
        pltpu.VMEM((2, win, d), F32), pltpu.VMEM((win, d), F32), pltpu.VMEM((win, win), F32), pltpu.VMEM((d, 4 * width), BF16),
    )

    sumb[0] = jnp.concatenate([sum1[0:3], sums2[0:3], jnp.zeros((2, d), F32)], axis=0)

    def sum_copy(i, axis):
        return remote(sumb.at[i], sumr.at[i], sm_s.at[i], sm_r.at[i], axis, 1 - at[axis])

    def sum_z(k):
        to = (wo_at + k + 1) % n_wo
        return remote(sumb.at[2], sumz.at[k], smz_s.at[k], smz_r.at[k], "wo", to)

    sum_copy(0, "y").start()

    def tail(i, carry):
        j = ffn_blocks + 1 + i

        @pl.when((i > 0) & (j < blocks))
        def _():
            stage_one(j)

        @pl.when(j <= blocks)
        def _():
            stage_two(j - 1)

        @pl.when(i > 0)
        def _():
            stage_three(j - 2)

        @pl.when(i == 0)
        def _():
            sum_copy(0, "y").wait_recv()
            sumb[1] = sumb[0] + sumr[0]
            sum_copy(1, "x").start()

        @pl.when(i == 1)
        def _():
            sum_copy(1, "x").wait_recv()
            sumb[2] = sumb[1] + sumr[1]
            for k in range(n_wo - 1):
                sum_z(k).start()

        return carry

    lax.fori_loop(0, blocks + 1 - ffn_blocks, tail, 0)
    in_y(nwin - 1).wait_recv()
    in_c(nwin - 1).start()
    total = sumb[2]
    for k in range(n_wo - 1):
        sum_z(k).wait_recv()
        total = total + sumz[k]
    for j in range(2 * n_wo):
        @pl.when(2 * wo_at + x_at == j)
        def _():
            total_sums[...] = total[0:6, j * own_rows:(j + 1) * own_rows]


    out_y.wait_send()
    for w in range(nwin):
        out_c(w).wait()
    dh_copy.wait_send()
    for i, axis in ((0, "y"), (1, "x")):
        sum_copy(i, axis).wait_send()
    for k in range(n_wo - 1):
        sum_z(k).wait_send()

    def drain_window(w, carry):
        part_copy(w).wait_send()
        own_copy(w).wait()
        in_y(w).wait_send()
        in_c(w).wait_send()
        in_c(w).wait_recv()
        return carry

    lax.fori_loop(0, nwin, drain_window, 0)

    def drain_block(b, carry):
        copy_one(b, False).wait_send()
        copy_two(b, False).wait_send()
        for k in range(n_wo - 1):
            copy_z(b, False, k).wait_send()
        return carry

    lax.fori_loop(0, blocks, drain_block, 0)


def backward(n_wo, lengths, slopes, nb, sums2, tokens, d2, dh, normed, recip, wqkv, wqkv1, wout, wout1,
             proj, att, lse, dgu, act, ht, d2t, half_out):
    half, d = normed.shape
    _, nwin, _, win = lse.shape
    width, hidden = wout.shape[0], act.shape[2]
    rows = d // (2 * n_wo)
    blocks = (3 * hidden + 4 * width) // BLOCK
    heads = width // HEAD_DIM
    smem = pl.BlockSpec(memory_space=pltpu.SMEM)
    vmem = pl.BlockSpec(memory_space=pltpu.VMEM)
    hbm = pl.BlockSpec(memory_space=pl.ANY)
    outs = [((blocks, rows, BLOCK), F32), ((6, rows), F32), (tokens.shape, BF16), (tokens.shape, BF16)]
    bufs = [
        ((blocks, 2, 2, n_wo, rows, BLOCK), BF16), ((blocks, 2, n_wo, rows, BLOCK), BF16), ((blocks, n_wo, rows, BLOCK), BF16),
        ((blocks, n_wo - 1, rows, BLOCK), BF16), ((half, d), BF16), ((win, d), BF16), ((win, d), BF16), ((win, d), BF16),
        ((win, 128), F32), ((win, d), BF16), ((2, 2, 3, win, width), BF16), ((2, 2, win, width), BF16), (lse.shape, F32),
        ((2,) + wqkv.shape, BF16), ((2,) + wout.shape, BF16), ((nwin, win, d), BF16), ((nwin, win, d), BF16),
        ((nwin, win, d), BF16), ((3, 8, d), F32), ((2, 8, d), F32), ((n_wo - 1, 8, d), F32), ((8, d), F32),
    ]
    sems = [(blocks,)] * 4 + [(blocks, n_wo - 1)] * 2 + [(5,), (2, 2), (5,), (1,), (1,)] + [(nwin,)] * 7
    sems += [(nwin + 1,), (nwin + 1,), (2,), (2,), (n_wo - 1,), (n_wo - 1,), (2, 2), (2,)]
    return pl.pallas_call(
        backward_kernel,
        in_specs=[smem, smem, vmem, vmem] + [hbm] * 17,
        out_specs=[vmem, vmem, hbm, hbm],
        input_output_aliases={20: 2},
        out_shape=[jax.ShapeDtypeStruct(*o) for o in outs],
        scratch_shapes=[pltpu.VMEM(*b) for b in bufs] + [pltpu.SemaphoreType.DMA(n) for n in sems],
        compiler_params=pltpu.CompilerParams(vmem_limit_bytes=63 * 1024 * 1024, collective_id=1, has_side_effects=True),
        cost_estimate=pl.CostEstimate(
            flops=2 * half * d * width * 16 + 12 * half * d * hidden + 20 * nwin * heads * win * win * 256,
            bytes_accessed=half * d * 60 + half * hidden * 12, transcendentals=2 * nwin * heads * win * win,
        ),
        name="backward",
    )(lengths, slopes, nb, sums2, tokens, d2, dh, normed, recip, wqkv, wqkv1, wout, wout1,
      proj, att, lse, dgu, act, ht, d2t, half_out)


SWAP = [(0, 1), (1, 0)]
WIDE = ("wo", "x")


def swap(value, axis):
    return lax.ppermute(value, axis, SWAP)


def after(value, *others):
    return lax.optimization_barrier((value, *others))[0]


def weight_shares(columns, hidden, width):
    down_share = columns[:, :hidden].T
    up_share = jnp.stack([columns[:, hidden:2 * hidden], columns[:, 2 * hidden:3 * hidden]])
    start = 3 * hidden
    qkv_share = jnp.stack([columns[:, start + i * width:start + (i + 1) * width] for i in range(3)])
    out_share = columns[:, start + 3 * width:].T
    return qkv_share, out_share, up_share, down_share


def shards(tokens, wqkv, wout, nb, up, down, lengths, cot):
    x_at, y_at, c_at = (lax.axis_index(name) for name in ("x", "y", "core"))
    d = tokens.shape[1]
    group_heads = wout.shape[0] // HEAD_DIM
    wqkv = jnp.swapaxes(wqkv, 1, 2)
    own = 2 * y_at + c_at
    heads = jnp.concatenate([own * group_heads + jnp.arange(group_heads), (own ^ 2) * group_heads + jnp.arange(group_heads)])
    slopes = 2.0 ** (-8.0 * (heads + 1).astype(F32) / HEADS)
    info = jnp.concatenate([y_at[None].astype(jnp.int32), lengths])

    (proj, att, lse, normed, recip, ht, a_all, b_all, act, fpart, fpart_other,
     wqkv1, wout1, up1, down1) = forward(lengths, slopes, nb, tokens, wqkv, wout, up, down)
    out, d2, d2t, dgu, dh, sums2 = ffn_bwd(
        lse.shape[3], fpart, fpart_other, normed, cot, nb, up, up1, down, down1, a_all, b_all
    )
    wo = lax.axis_size("wo")
    width, hidden = wout.shape[0], down.shape[0]
    if (d // (2 * wo)) % 16 == 0:
        share, sums, block_out, input_low = backward(
            wo, lengths, slopes, nb, sums2, tokens, d2, dh, normed, recip, wqkv, wqkv1, wout, wout1,
            proj, att, lse, dgu, act, ht, d2t, out,
        )
        columns = share.transpose(1, 0, 2).reshape(share.shape[1], -1)
        return (block_out, input_low.astype(F32), *weight_shares(columns, hidden, width), sums)

    out = lax.dynamic_slice_in_dim(out, y_at * (out.shape[0] // 2), out.shape[0] // 2, 0)
    dh_other = swap(dh, "core")

    def grad(a, b):
        return lax.dot_general(a, b, (((1,), (0,)), ((), ())), preferred_element_type=F32).astype(BF16)

    def part_of(value, at):
        split = value.reshape(wo, 2, -1, value.shape[1])
        return lax.dynamic_index_in_dim(split, at, 1, keepdims=False).reshape(-1, value.shape[1])

    def add(a, b):
        return a.astype(F32) + b.astype(F32)

    down_peer = grad(d2t, act[1])
    down_peer_in = swap(down_peer, "y")
    up_peer = grad(ht, dgu[1])
    up_own = grad(ht, dgu[0])
    up_in = swap(jnp.concatenate([part_of(up_own, 1 - x_at), part_of(up_peer, 1 - x_at)], axis=0), "x")
    down_own = grad(d2t, act[0])

    quarter = out.shape[0] // 2
    order = jnp.stack([2 * y_at, 2 * y_at + 1, 2 * (1 - y_at) + c_at, 2 * (1 - y_at) + 1 - c_at]).astype(jnp.int32)

    def mine(value):
        return lax.dynamic_slice_in_dim(value, c_at * quarter, quarter, 0)

    d2 = after(d2, down_own)
    d1, ipart, agrad0, agrad1, sums1 = attn_bwd(
        info, slopes, tokens, d2, dh, dh_other, normed, recip, nb, wqkv, wqkv1, wout, wout1,
        proj, att, lse,
    )
    ipart_other = swap(ipart, "core")
    near_out = swap(mine(out), "y")

    attn_in = swap(jnp.concatenate([part_of(agrad0, 1 - x_at), part_of(agrad1, 1 - x_at)], axis=0), "x")

    total = (d1 + add(ipart, ipart_other)).astype(BF16)
    near_in = swap(mine(total), "y")

    down_all = add(down_own, down_peer_in).astype(BF16)
    down_in = swap(part_of(down_all, 1 - x_at), "x")
    down_half = add(part_of(down_all, x_at), down_in).astype(BF16)
    n = d // 2
    up_peer_half = add(part_of(up_peer, x_at), up_in[n:]).astype(BF16)
    up_half = add(add(part_of(up_own, x_at), up_in[:n]), swap(up_peer_half, "y")).astype(BF16)
    attn_peer_half = add(part_of(agrad1, x_at), attn_in[n:]).astype(BF16)
    attn_half = add(add(part_of(agrad0, x_at), attn_in[:n]), swap(attn_peer_half, "y")).astype(BF16)

    scatter = functools.partial(lax.psum_scatter, axis_name="wo", scatter_dimension=0, tiled=True)
    columns = jnp.concatenate([scatter(jnp.concatenate([down_half, up_half], axis=1)), scatter(attn_half)], axis=1).astype(F32)
    small = jnp.concatenate([sums1[:3], sums2[:3]], axis=0)
    small_share = lax.psum_scatter(lax.psum(small, "y"), WIDE, scatter_dimension=1, tiled=True)

    block_out = place(order, out, near_out, swap(near_out, "core"), BF16)
    input_grad = place(order, total, near_in, swap(near_in, "core"), F32)
    return (block_out, input_grad, *weight_shares(columns, hidden, width), small_share)


def solution(mesh):
    wide = mesh.shape["wide"]
    grid = Mesh(mesh.devices.reshape(wide // 2, 2, 2, 2), ("wo", "x", "y", "core"))
    narrow = ("y", "core")
    placed = (
        P(WIDE, None),
        P(None, None, narrow),
        P(narrow, None),
        P(),
        P(None, None, narrow),
        P(narrow, None),
        P(WIDE),
        P(WIDE, None),
    )
    return jax.shard_map(
        shards,
        mesh=grid,
        in_specs=placed,
        out_specs=(
            P(WIDE, None),
            P(WIDE, None),
            P(None, WIDE, narrow),
            P(narrow, WIDE),
            P(None, WIDE, narrow),
            P(narrow, WIDE),
            P(None, WIDE),
        ),
        check_vma=False,
    )
```
